256 devices in a mesh: clip: 16 (over y, z_hi, core), space: 16 (over z_lo, x).
Axes of the slice: x: 4, y: 4, z: 8 (z_hi: 2, z_lo: 4; z = z_hi * 4 + z_lo), core: 2. Of those that a mesh axis runs over, the one named last changes fastest.
Arguments:
- teacher_input: bfloat16 [16, 2, 128, 32, 512], P('clip', None, 'space'), may hold values from -6 to 6
- conv_first: bfloat16 [3, 3, 3, 512, 256], replicated, may hold values from -0.0546875 to 0.0546875
- conv_second: bfloat16 [3, 3, 3, 256, 256], replicated, may hold values from -0.078125 to 0.078125
- student_low: bfloat16 [16, 2, 128, 32, 256], P('clip', None, 'space'), may hold values from -6 to 6
- student_high: bfloat16 [16, 2, 256, 64, 128], P('clip', None, 'space'), may hold values from -6 to 6
- kernel_low: float32 [3, 3, 3, 256], replicated, may hold values from -1 to 1
- kernel_high: float32 [3, 3, 3, 128], replicated, may hold values from -1 to 1
- adapter_low: bfloat16 [256, 256], replicated, may hold values from -0.0078125 to 0.0078125
- adapter_high: bfloat16 [128, 256], replicated, may hold values from -0.009765625 to 0.009765625
Outputs:
- adapter_low_gradient: float32 [256, 256], P('clip')
- kernel_low_gradient: float32 [3, 3, 3, 256], P(None, None, None, 'clip')
- adapter_high_gradient: float32 [128, 256], P('clip')
- kernel_high_gradient: float32 [3, 3, 3, 128], P(None, None, None, 'clip')
- fine_mismatch: bfloat16 [16, 2, 256, 64, 256], P('clip', None, 'space')
The draws below stay inside these ranges and needn't reach their ends.
All inputs are finite; a program needn't handle non-finite values.
Results may differ from the reference program's by a relative error of at most 0.0067.
Values may be sent and summed in bfloat16 or wider, within the bound.
A program may use at most 192 MiB of HBM per device.

```python
import jax
import jax.numpy as jnp
from jax import lax

TEACH_IN = 512
TEACH_OUT = 256
STU_LOW = 256
STU_HIGH = 128
FRAMES = 2
COLS = 32
CLIPS = 16
ROWS = 128


def with_spikes(entries, own_key, source, target, shards_of, factor):
    def block_of(axis_at):
        return (jnp.arange(entries.shape[axis_at]) // (entries.shape[axis_at] // shards_of)).reshape((-1,) + (1,) * (entries.ndim - 1 - axis_at))

    first = jax.random.permutation(own_key, shards_of)[block_of(target)]
    far = (block_of(target) + shards_of // 2) % shards_of
    return jnp.where((block_of(source) == first) | (block_of(source) == far), factor * entries, entries)


def block_scale(own_key, shape, pieces, least, top_value):
    gain = 1.0
    for dim, shards_of in pieces:
        steps = jax.random.uniform(jax.random.fold_in(jax.random.fold_in(own_key, 6), dim), (shards_of,), jnp.float32, least / len(pieces), top_value / len(pieces))
        gain = gain * jnp.repeat(jnp.exp(steps), shape[dim] // shards_of).reshape((-1,) + (1,) * (len(shape) - 1 - dim))
    return gain


def noise(rng, dims, deviation, reach, split=(), dtype=jnp.bfloat16):
    result = deviation * jax.random.normal(rng, dims, jnp.float32)
    if split:
        result = result * block_scale(rng, dims, split, -0.22, 0.18)
    return jnp.clip(result, -reach, reach).astype(dtype)


def noise_with(stream_key, shape, spread, limit, shards, heavy, held_as=jnp.bfloat16):
    result = spread * jax.random.normal(stream_key, shape, jnp.float32)
    if shards:
        result = result * block_scale(stream_key, shape, shards, -0.22, 0.18)
    return jnp.clip(with_spikes(result, jax.random.fold_in(stream_key, 3), *heavy), -limit, limit).astype(held_as)


def setup_inputs(seed: int = 0) -> dict:
    arg_keys = jax.random.split(jax.random.key(seed), 10)
    teacher_input = noise(arg_keys[0], (CLIPS, FRAMES, ROWS, COLS, TEACH_IN), 1.0, 6.0, ((0, 16), (2, 16)))
    conv_first = noise(arg_keys[1], (3, 3, 3, TEACH_IN, TEACH_OUT), (27 * TEACH_IN) ** -0.5, 0.0546875)
    conv_second = noise(arg_keys[2], (3, 3, 3, TEACH_OUT, TEACH_OUT), (27 * TEACH_OUT) ** -0.5, 0.078125)
    student_low = noise_with(arg_keys[3], (CLIPS, FRAMES, ROWS, COLS, STU_LOW), 1.0, 6.0, ((0, 16), (2, 16)), (0, 4, 16, 2.0))
    student_high = noise_with(arg_keys[4], (CLIPS, FRAMES, 2 * ROWS, 2 * COLS, STU_HIGH), 1.0, 6.0, ((0, 16), (2, 16)), (0, 4, 16, 2.0))
    kernel_low = noise(arg_keys[5], (3, 3, 3, STU_LOW), 0.2, 1.0, (), jnp.float32)
    kernel_high = noise(arg_keys[6], (3, 3, 3, STU_HIGH), 0.2, 1.0, (), jnp.float32)
    adapter_low = noise(arg_keys[7], (STU_LOW, TEACH_OUT), (2500 * STU_LOW) ** -0.5, 0.0078125)
    adapter_high = noise(arg_keys[8], (STU_HIGH, TEACH_OUT), (2500 * STU_HIGH) ** -0.5, 0.009765625)
    return dict(teacher_input=teacher_input, conv_first=conv_first, conv_second=conv_second, student_low=student_low, student_high=student_high, kernel_low=kernel_low, kernel_high=kernel_high, adapter_low=adapter_low, adapter_high=adapter_high)


def conv_full(field, weight):
    padded = jnp.pad(field, ((1, 1), (1, 1), (1, 1), (0, 0)))
    frames, row_count, col_count = field.shape[0], field.shape[1], field.shape[2]
    summed = jnp.zeros((frames, row_count, col_count, weight.shape[-1]), jnp.float32)
    for tap_t in range(3):
        for tap_h in range(3):
            for tap_w in range(3):
                window_part = padded[tap_t:tap_t + frames, tap_h:tap_h + row_count, tap_w:tap_w + col_count, :]
                summed = summed + jnp.dot(window_part, weight[tap_t, tap_h, tap_w], preferred_element_type=jnp.float32)
    return summed


def level_grads(field, kernel, adapter, target, scale):
    padded = jnp.pad(field, ((1, 1), (1, 1), (1, 1), (0, 0)))
    frames, row_count, col_count = field.shape[0], field.shape[1], field.shape[2]
    mixed = field.astype(jnp.float32)
    for tap_t in range(3):
        for tap_h in range(3):
            for tap_w in range(3):
                shifted = padded[tap_t:tap_t + frames, tap_h:tap_h + row_count, tap_w:tap_w + col_count, :].astype(jnp.float32)
                mixed = mixed + shifted * kernel[tap_t, tap_h, tap_w]
    student = mixed.astype(jnp.bfloat16)
    output = jnp.dot(student, adapter, preferred_element_type=jnp.float32)
    mismatch = output - target.astype(jnp.float32)
    resid = (mismatch * scale).astype(jnp.bfloat16)
    adapter_part = jnp.einsum("fhwc,fhwd->cd", student.astype(jnp.float32), resid.astype(jnp.float32))
    back = jnp.einsum("fhwd,cd->fhwc", resid.astype(jnp.float32), adapter.astype(jnp.float32))
    kernel_rows = []
    for tap_t in range(3):
        for tap_h in range(3):
            for tap_w in range(3):
                shifted = padded[tap_t:tap_t + frames, tap_h:tap_h + row_count, tap_w:tap_w + col_count, :].astype(jnp.float32)
                kernel_rows.append(jnp.sum(back * shifted, axis=(0, 1, 2)))
    kernel_part = jnp.stack(kernel_rows).reshape(kernel.shape)
    return adapter_part, kernel_part, mismatch.astype(jnp.bfloat16)


def reference(teacher_input, conv_first, conv_second, student_low, student_high, kernel_low, kernel_high, adapter_low, adapter_high):
    low_count = teacher_input.shape[0] * teacher_input.shape[1] * teacher_input.shape[2] * teacher_input.shape[3]
    scale_low = 1.0 / low_count
    scale_high = 1.0 / (4 * low_count)

    def one_clip(items):
        clip_input, clip_low, clip_high = items
        first_feature = conv_full(clip_input, conv_first).astype(jnp.bfloat16)
        gated = jax.nn.silu(first_feature.astype(jnp.float32)).astype(jnp.bfloat16)
        upsampled = jnp.repeat(jnp.repeat(gated, 2, axis=1), 2, axis=2)
        second_feature = conv_full(upsampled, conv_second).astype(jnp.bfloat16)
        adapter_one, kernel_one, unused_low = level_grads(clip_low, kernel_low, adapter_low, first_feature, scale_low)
        adapter_two, kernel_two, mismatch_two = level_grads(clip_high, kernel_high, adapter_high, second_feature, scale_high)
        return adapter_one, kernel_one, adapter_two, kernel_two, mismatch_two

    results = lax.map(one_clip, (teacher_input, student_low, student_high))
    return (jnp.sum(results[0], axis=0), jnp.sum(results[1], axis=0),
            jnp.sum(results[2], axis=0), jnp.sum(results[3], axis=0), results[4])
```

```python
import functools

import jax
import jax.numpy as jnp
from jax import lax
from jax.experimental import pallas as pl
from jax.experimental.pallas import tpu as pltpu
from jax.sharding import PartitionSpec as P

F32 = jnp.float32
BF16 = jnp.bfloat16
MESH = pl.DeviceIdType.MESH
ANY = pl.BlockSpec(memory_space=pl.ANY)
VM = pl.BlockSpec(memory_space=pltpu.VMEM)
VMEM_LIMIT = 60 * 1024 * 1024


def dot(a, b):
    return jnp.dot(a, b, preferred_element_type=F32)


def row_ids(v, width):
    ids = lax.broadcasted_iota(jnp.int32, v.shape, 0)
    return ids if v.shape[0] == width else lax.rem(ids, width)


def from_left(v, width):
    return jnp.where(row_ids(v, width) == 0, 0.0, pltpu.roll(v, 1, 0))


def from_right(v, width):
    return jnp.where(row_ids(v, width) == width - 1, 0.0, pltpu.roll(v, v.shape[0] - 1, 0))


def halo_kernel(x, sl, sh, hx, hl, hh, send_sem, recv_sem):
    me = lax.axis_index("space")
    last = lax.axis_size("space") - 1
    barrier = pltpu.get_barrier_semaphore()

    @pl.when(me > 0)
    def _():
        pl.semaphore_signal(barrier, inc=1, device_id={"space": me - 1}, device_id_type=MESH)

    @pl.when(me < last)
    def _():
        pl.semaphore_signal(barrier, inc=1, device_id={"space": me + 1}, device_id_type=MESH)

    inner = jnp.logical_and(me > 0, me < last)

    @pl.when(inner)
    def _():
        pl.semaphore_wait(barrier, 2)

    @pl.when(jnp.logical_not(inner))
    def _():
        pl.semaphore_wait(barrier, 1)

    def copies(side):
        peer = me + 1 if side == 0 else me - 1
        out = []
        for n, (src, dst, width) in enumerate(((x, hx, 2), (sl, hl, 1), (sh, hh, 1))):
            rows = src.shape[2]
            lo = rows - width if side == 0 else 0
            out.append(
                pltpu.make_async_remote_copy(
                    src_ref=src.at[0, :, lo : lo + width],
                    dst_ref=dst.at[side],
                    send_sem=send_sem.at[side, n],
                    recv_sem=recv_sem.at[side, n],
                    device_id={"space": peer},
                    device_id_type=MESH,
                )
            )
        return out

    down, up = copies(0), copies(1)

    @pl.when(me < last)
    def _():
        for c in down:
            c.start()

    @pl.when(me > 0)
    def _():
        for c in up:
            c.start()

    @pl.when(me < last)
    def _():
        for c in down:
            c.wait_send()
        for c in up:
            c.wait_recv()

    @pl.when(me > 0)
    def _():
        for c in up:
            c.wait_send()
        for c in down:
            c.wait_recv()


def halo_call(x, sl, sh):
    def half(v, width):
        return jax.ShapeDtypeStruct((2, v.shape[1], width) + v.shape[3:], v.dtype)

    return pl.pallas_call(
        halo_kernel,
        out_shape=(half(x, 2), half(sl, 1), half(sh, 1)),
        in_specs=[ANY] * 3,
        out_specs=(ANY,) * 3,
        scratch_shapes=[pltpu.SemaphoreType.DMA((2, 3)), pltpu.SemaphoreType.DMA((2, 3))],
        compiler_params=pltpu.CompilerParams(
            collective_id=0, has_side_effects=True, vmem_limit_bytes=1 << 20
        ),
        name="halo",
    )(x, sl, sh)


def build_taps(w2, v):
    def body(step, _):
        dt, chunk = step // 16, step % 16
        rows = pl.ds(pl.multiple_of(chunk * 16, 16), 16)
        out_rows = pl.ds(pl.multiple_of(dt * 256 + chunk * 16, 16), 16)
        tap = [[w2[dt * 9 + dh * 3 + dw, rows, :].astype(F32) for dw in range(3)] for dh in range(3)]
        for m in range(4):
            r = []
            for dw in range(3):
                a, b, c = tap[0][dw], tap[1][dw], tap[2][dw]
                r.append((a, b + c, a + b, c)[m])
            for j, col in enumerate((r[0], r[1] + r[2], r[0] + r[1], r[2])):
                v[m, out_rows, j * 256 : (j + 1) * 256] = col.astype(BF16)
        return 0

    lax.fori_loop(0, 48, body, 0)


def widen(src, dst):
    for f in range(2):

        def body(r, _):
            dst[f, r] = src[f, r].astype(F32)
            return 0

        lax.fori_loop(0, src.shape[1], body, 0)


def depthwise(u, k, s):
    rows, width = u.shape[1] - 2, u.shape[2]
    for f in range(2):

        def body(r, _):
            parts = [None, None, None]
            for g in range(2):
                for dh in range(3):
                    val = u[g, r + dh]
                    for dw in range(3):
                        tap = (g - f + 1) * 9 + dh * 3 + dw
                        term = val * k[tap : tap + 1, :]
                        parts[dw] = term if parts[dw] is None else parts[dw] + term
            total = u[f, r + 1] + (
                from_left(parts[0], width) + parts[1] + from_right(parts[2], width)
            )
            at = pl.multiple_of((f * rows + r) * width, width)
            s[pl.ds(at, width), :] = total.astype(BF16)
            return 0

        lax.fori_loop(0, rows, body, 0)


def kernel_terms(u, back, kg):
    rows, width, ch = u.shape[1] - 2, u.shape[2], u.shape[3]
    kg[...] = jnp.zeros_like(kg)
    for f in range(2):

        def body(r, _):
            at = pl.multiple_of((f * rows + r) * width, width)
            b = back[pl.ds(at, width), :]
            shifted = (from_right(b, width), b, from_left(b, width))
            for g in range(2):
                for dh in range(3):
                    val = u[g, r + dh]
                    for dw in range(3):
                        tap = (g - f + 1) * 9 + dh * 3 + dw
                        prod = (shifted[dw] * val).reshape(width // 8, 8, ch)
                        kg[tap] += jnp.sum(prod, axis=0)
            return 0

        lax.fori_loop(0, rows, body, 0)


def kernel_rows(kg):
    ch = kg.shape[2]
    summed = jnp.sum(kg[...], axis=1)
    padded = jnp.concatenate([summed, jnp.zeros((128 - 27, ch), F32)], axis=0)
    return padded.T


def local_kernel(
    x, w1, w2, sl, sh, kl, kh, pl_low, pl_high, hx, hl, hh,
    mism, grads,
    xs, w1s, w2s, vs, ys, tgt, gate, ulb, uhb, ul, uh, s_low, s_high, r_low, r_high,
    b_low, b_high, kg_low, kg_high, fine, mism_s, sem, out_sem,
):
    me = lax.axis_index("space")
    last = lax.axis_size("space") - 1
    scale_low = 1.0 / (16 * 2 * 128 * 32)
    scale_high = scale_low / 4

    loads = []

    def load(src, dst):
        c = pltpu.make_async_copy(src, dst, sem.at[len(loads)])
        loads.append(c)
        c.start()
        return c

    c_w2 = load(w2, w2s)
    c_x = [load(x.at[0, f], xs.at[2:10, :, f * 512 : (f + 1) * 512]) for f in range(2)]
    c_sl = load(sl.at[0], ulb.at[:, 1:9])
    c_sh = load(sh.at[0], uhb.at[:, 1:17])
    c_w1 = [
        load(w1.at[dt, :, dw], w1s.at[:, dt * 512 : (dt + 1) * 512, dw * 256 : (dw + 1) * 256])
        for dt in range(3)
        for dw in range(3)
    ]

    def border(side, inside):
        n = 14 + 4 * side
        out = []
        for f in range(2):
            out.append((hx.at[side, f], xs.at[10 * side : 10 * side + 2, :, f * 512 : (f + 1) * 512]))
        out.append((hl.at[side], ulb.at[:, 9 * side : 9 * side + 1]))
        out.append((hh.at[side], uhb.at[:, 17 * side : 17 * side + 1]))

        @pl.when(inside)
        def _():
            cs = [pltpu.make_async_copy(a, b, sem.at[n + q]) for q, (a, b) in enumerate(out)]
            for c in cs:
                c.start()
            for c in cs:
                c.wait()

        @pl.when(jnp.logical_not(inside))
        def _():
            for _, b in out:
                b[...] = jnp.zeros(b.shape, BF16)

    border(0, me > 0)
    border(1, me < last)

    c_w2.wait()
    build_taps(w2s, vs)
    c_sl.wait()
    c_sh.wait()
    widen(ulb, ul)
    widen(uhb, uh)
    depthwise(ul, kl, s_low)
    depthwise(uh, kh, s_high)

    for c in c_x + c_w1:
        c.wait()

    for f in range(2):
        acc = None
        for dh in range(3):
            part = dot(
                xs[dh : dh + 10].reshape(320, 1024), w1s[dh, (1 - f) * 512 : (1 - f) * 512 + 1024, :]
            )
            acc = part if acc is None else acc + part
        ys[:320, :768] = acc
        feat = (
            from_left(ys[:320, 0:256], 32)
            + ys[:320, 256:512]
            + from_right(ys[:320, 512:768], 32)
        ).astype(BF16)
        tgt[f * 256 : (f + 1) * 256, :] = feat[32:288]
        wide = feat.astype(F32)
        gated = wide / (1.0 + jnp.exp(-wide))
        gate[:, :, f * 256 : (f + 1) * 256] = gated.astype(BF16).reshape(10, 32, 256)

    @pl.when(me == 0)
    def _():
        gate[0] = jnp.zeros((32, 512), BF16)

    @pl.when(me == last)
    def _():
        gate[9] = jnp.zeros((32, 512), BF16)

    for q in range(2):
        rows = slice(q * 256, (q + 1) * 256)
        res = dot(s_low[rows, :], pl_low[...]) - tgt[rows, :].astype(F32)
        resid = (res * scale_low).astype(BF16)
        r_low[rows, :] = resid
        b_low[rows, :] = lax.dot_general(
            resid, pl_low[...], (((1,), (1,)), ((), ())), preferred_element_type=F32
        )
    a_low = lax.dot_general(
        s_low[...], r_low[...], (((0,), (0,)), ((), ())), preferred_element_type=F32
    )
    kernel_terms(ul, b_low, kg_low)
    k_low = kernel_rows(kg_low)
    for b in range(16):
        i = (b % 8) * 2 + b // 8
        grads[b * 16 : (b + 1) * 16, 0:256] = a_low[i * 16 : (i + 1) * 16]
        grads[b * 16 : (b + 1) * 16, 256:384] = k_low[i * 16 : (i + 1) * 16]

    for f in range(2):
        for pr in range(2):
            acc = None
            for a in range(2):
                part = dot(
                    gate[pr + a : pr + a + 8].reshape(256, 512),
                    vs[pr * 2 + a, (1 - f) * 256 : (1 - f) * 256 + 512, :],
                )
                acc = part if acc is None else acc + part
            ys[:256, :] = acc
            even = from_left(ys[:256, 0:256], 32) + ys[:256, 256:512]
            odd = ys[:256, 512:768] + from_right(ys[:256, 768:1024], 32)
            for pc, val in enumerate((even, odd)):
                for r in range(8):
                    at = (f * 16 + 2 * r + pr) * 64 + pc
                    for half in range(2):
                        fine[half, pl.ds(at, 32, stride=2), :] = val[
                            r * 32 : (r + 1) * 32, half * 128 : (half + 1) * 128
                        ]

    def fine_body(q, _):
        rows = pl.ds(pl.multiple_of(q * 256, 256), 256)
        target = jnp.concatenate([fine[0, rows, :], fine[1, rows, :]], axis=1)
        target = target.astype(BF16).astype(F32)
        res = dot(s_high[rows, :], pl_high[...]) - target
        mism_s[rows, :] = res.astype(BF16)
        resid = (res * scale_high).astype(BF16)
        r_high[rows, :] = resid
        b_high[rows, :] = lax.dot_general(
            resid, pl_high[...], (((1,), (1,)), ((), ())), preferred_element_type=F32
        )
        return 0

    lax.fori_loop(0, 8, fine_body, 0)
    outs = []
    for f in range(2):
        c = pltpu.make_async_copy(
            mism_s.reshape(2, 16, 64, 256).at[f], mism.at[0, f], out_sem.at[f]
        )
        c.start()
        outs.append(c)
    a_high = lax.dot_general(
        s_high[...], r_high[...], (((0,), (0,)), ((), ())), preferred_element_type=F32
    )
    kernel_terms(uh, b_high, kg_high)
    k_high = kernel_rows(kg_high)
    for b in range(16):
        i = (b % 8) * 2 + b // 8
        grads[b * 16 : b * 16 + 8, 384:512] = a_high[i * 8 : (i + 1) * 8, 0:128]
        grads[b * 16 + 8 : b * 16 + 16, 384:512] = a_high[i * 8 : (i + 1) * 8, 128:256]
        grads[b * 16 : b * 16 + 8, 512:640] = k_high[i * 8 : (i + 1) * 8]
        grads[b * 16 + 8 : b * 16 + 16, 512:640] = jnp.zeros((8, 128), F32)
    for c in outs:
        c.wait()


def local_call(x, w1, w2, sl, sh, kl, kh, p_low, p_high, hx, hl, hh):
    w2 = w2.reshape(27, 256, 256)
    kl = kl.reshape(27, 256)
    kh = kh.reshape(27, 128)
    v = pltpu.VMEM
    return pl.pallas_call(
        local_kernel,
        out_shape=(
            jax.ShapeDtypeStruct((1, 2, 16, 64, 256), BF16),
            jax.ShapeDtypeStruct((256, 640), F32),
        ),
        in_specs=[ANY, ANY, ANY, ANY, ANY, VM, VM, VM, VM, ANY, ANY, ANY],
        out_specs=(ANY, VM),
        scratch_shapes=[
            v((12, 32, 1024), BF16),
            v((3, 1536, 768), BF16),
            v((27, 256, 256), BF16),
            v((4, 768, 1024), BF16),
            v((320, 1024), F32),
            v((512, 256), BF16),
            v((10, 32, 512), BF16),
            v((2, 10, 32, 256), BF16),
            v((2, 18, 64, 128), BF16),
            v((2, 10, 32, 256), F32),
            v((2, 18, 64, 128), F32),
            v((512, 256), BF16),
            v((2048, 128), BF16),
            v((512, 256), BF16),
            v((2048, 256), BF16),
            v((512, 256), F32),
            v((2048, 128), F32),
            v((27, 8, 256), F32),
            v((27, 8, 128), F32),
            v((2, 2048, 128), F32),
            v((2048, 256), BF16),
            pltpu.SemaphoreType.DMA((22,)),
            pltpu.SemaphoreType.DMA((2,)),
        ],
        compiler_params=pltpu.CompilerParams(vmem_limit_bytes=VMEM_LIMIT),
        name="local",
    )(x, w1, w2, sl, sh, kl, kh, p_low, p_high, hx, hl, hh)


def reduce_kernel(
    g, o_al, o_kl, o_ah, o_kh, s1, r1, h1, s2, r2, h2, s3, r3, r4, r5, h3,
    snd, rcv, loc,
):
    clip = lax.axis_index("clip")
    space = lax.axis_index("space")
    core = lax.rem(clip, 2)
    zh = lax.rem(clip // 2, 2)
    y = clip // 4
    zl = space // 4
    xx = lax.rem(space, 4)

    def dev(core=core, y=y, zh=zh, zl=zl, xx=xx):
        return ((y * 2 + zh) * 2 + core, zl * 4 + xx)

    peers = [dev(core=1 - core), dev(zh=1 - zh)]
    for d in range(1, 4):
        peers.append(dev(y=lax.rem(y + d, 4)))
        peers.append(dev(zl=lax.rem(zl + d, 4)))
        peers.append(dev(xx=lax.rem(xx + d, 4)))
    barrier = pltpu.get_barrier_semaphore()
    for p in peers:
        pl.semaphore_signal(barrier, inc=1, device_id=p, device_id_type=MESH)

    s1[...] = g[pl.ds(pl.multiple_of((1 - core) * 128, 128), 128), :].astype(BF16)
    pl.semaphore_wait(barrier, len(peers))

    def send(src, dst, n, peer):
        return pltpu.make_async_remote_copy(
            src_ref=src, dst_ref=dst, send_sem=snd.at[n], recv_sem=rcv.at[n],
            device_id=peer, device_id_type=MESH,
        )

    c = send(s1, r1, 0, dev(core=1 - core))
    c.start()
    c.wait()
    h1[...] = g[pl.ds(pl.multiple_of(core * 128, 128), 128), :] + r1[...].astype(F32)

    s2[...] = h1[...].astype(BF16)
    cs = []
    for d in range(1, 4):
        to = lax.rem(y + d, 4)
        cs.append(
            send(s2.at[pl.ds(pl.multiple_of(to * 32, 32), 32), :], r2.at[d - 1], d, dev(y=to))
        )
    for c in cs:
        c.start()
    for c in cs:
        c.wait()
    h2[...] = h1[pl.ds(pl.multiple_of(y * 32, 32), 32), :] + (
        r2[0].astype(F32) + r2[1].astype(F32) + r2[2].astype(F32)
    )

    s3[...] = h2[...].astype(BF16)
    c = send(s3.at[pl.ds(pl.multiple_of((1 - zh) * 16, 16), 16), :], r3, 4, dev(zh=1 - zh))
    c.start()
    c.wait()
    h3[...] = (h2[pl.ds(pl.multiple_of(zh * 16, 16), 16), :] + r3[...].astype(F32)).astype(BF16)

    def gather(src, slots, mine, base, peer):
        cs = []
        for d in range(1, 4):
            to = lax.rem(mine + d, 4)
            cs.append(send(src, slots.at[mine], base + d, peer(to)))
        for c in cs:
            c.start()
        slots[mine] = src[...]
        for d, c in enumerate(cs):
            c.wait_send()
        for d in range(1, 4):
            came = lax.rem(mine + 4 - d, 4)
            pltpu.make_async_remote_copy(
                src_ref=src, dst_ref=slots.at[came], send_sem=snd.at[base + d],
                recv_sem=rcv.at[base + d], device_id=peer(came), device_id_type=MESH,
            ).wait_recv()
        return (slots[0].astype(F32) + slots[1].astype(F32)) + (
            slots[2].astype(F32) + slots[3].astype(F32)
        )

    total = gather(h3, r4, zl, 4, lambda to: dev(zl=to))
    s3[0:16] = total.astype(BF16)
    total = gather(s3.at[0:16], r5, xx, 7, lambda to: dev(xx=to))
    o_al[...] = total[:, 0:256]
    o_kl[...] = total[:, 256:384]
    o_ah[...] = jnp.concatenate([total[0:8, 384:512], total[8:16, 384:512]], axis=1)
    o_kh[...] = total[0:8, 512:640]


def reduce_call(g):
    v = pltpu.VMEM
    return pl.pallas_call(
        reduce_kernel,
        out_shape=(
            jax.ShapeDtypeStruct((16, 256), F32),
            jax.ShapeDtypeStruct((16, 128), F32),
            jax.ShapeDtypeStruct((8, 256), F32),
            jax.ShapeDtypeStruct((8, 128), F32),
        ),
        in_specs=[VM],
        out_specs=(VM,) * 4,
        scratch_shapes=[
            v((128, 640), BF16),
            v((128, 640), BF16),
            v((128, 640), F32),
            v((128, 640), BF16),
            v((3, 32, 640), BF16),
            v((32, 640), F32),
            v((32, 640), BF16),
            v((16, 640), BF16),
            v((4, 16, 640), BF16),
            v((4, 16, 640), BF16),
            v((16, 640), BF16),
            pltpu.SemaphoreType.DMA((11,)),
            pltpu.SemaphoreType.DMA((11,)),
            pltpu.SemaphoreType.DMA((1,)),
        ],
        compiler_params=pltpu.CompilerParams(
            collective_id=1, has_side_effects=True, vmem_limit_bytes=8 << 20
        ),
        name="reduce",
    )(g)


def on_device(x, w1, w2, sl, sh, kl, kh, p_low, p_high):
    hx, hl, hh = halo_call(x, sl, sh)
    mism, grads = local_call(x, w1, w2, sl, sh, kl, kh, p_low, p_high, hx, hl, hh)
    a_low, k_low, a_high, k_high = reduce_call(grads)
    return (
        a_low,
        k_low[:, :27].T.reshape(3, 3, 3, 16),
        a_high,
        k_high[:, :27].T.reshape(3, 3, 3, 8),
        mism,
    )


def solution(mesh):
    rows = P("clip", None, "space", None, None)
    in_specs = (rows, P(), P(), rows, rows, P(), P(), P(), P())
    out_specs = (
        P("clip", None),
        P(None, None, None, "clip"),
        P("clip", None),
        P(None, None, None, "clip"),
        rows,
    )
    return jax.shard_map(
        on_device, mesh=mesh, in_specs=in_specs, out_specs=out_specs, check_vma=False
    )
```

```python
import functools

import jax
import jax.numpy as jnp
from jax import lax
from jax.experimental import pallas as pl
from jax.experimental.pallas import tpu as pltpu
from jax.sharding import PartitionSpec as P

F32 = jnp.float32
BF16 = jnp.bfloat16
MESH = pl.DeviceIdType.MESH
ANY = pl.BlockSpec(memory_space=pl.ANY)
VM = pl.BlockSpec(memory_space=pltpu.VMEM)
VMEM_LIMIT = 60 * 1024 * 1024


def dot(a, b):
    return jnp.dot(a, b, preferred_element_type=F32)


def row_ids(v, width):
    ids = lax.broadcasted_iota(jnp.int32, v.shape, 0)
    return ids if v.shape[0] == width else lax.rem(ids, width)


def from_left(v, width):
    return jnp.where(row_ids(v, width) == 0, 0.0, pltpu.roll(v, 1, 0))


def from_right(v, width):
    return jnp.where(row_ids(v, width) == width - 1, 0.0, pltpu.roll(v, v.shape[0] - 1, 0))


def build_taps(w2, v):
    def body(step, _):
        dt, chunk = step // 16, step % 16
        rows = pl.ds(pl.multiple_of(chunk * 16, 16), 16)
        out_rows = pl.ds(pl.multiple_of(dt * 256 + chunk * 16, 16), 16)
        tap = [[w2[dt, dh, dw, rows, :].astype(F32) for dw in range(3)] for dh in range(3)]
        for m in range(4):
            r = []
            for dw in range(3):
                a, b, c = tap[0][dw], tap[1][dw], tap[2][dw]
                r.append((a, b + c, a + b, c)[m])
            for j, col in enumerate((r[0], r[1] + r[2], r[0] + r[1], r[2])):
                v[m, out_rows, j * 256 : (j + 1) * 256] = col.astype(BF16)
        return 0

    lax.fori_loop(0, 48, body, 0)


def widen(src, dst, first, count):
    for f in range(2):

        def body(r, _):
            dst[f, first + r] = src[f, first + r].astype(F32)
            return 0

        lax.fori_loop(0, count, body, 0)


def depthwise(u, k, s, first, count):
    rows, width = u.shape[1] - 2, u.shape[2]
    for f in range(2):

        def body(step, _):
            r = first + step
            parts = [None, None, None]
            for g in range(2):
                for dh in range(3):
                    val = u[g, r + dh]
                    for dw in range(3):
                        term = val * k[g - f + 1, dh, dw : dw + 1, :]
                        parts[dw] = term if parts[dw] is None else parts[dw] + term
            total = u[f, r + 1] + (
                from_left(parts[0], width) + parts[1] + from_right(parts[2], width)
            )
            at = pl.multiple_of((f * rows + r) * width, width)
            s[pl.ds(at, width), :] = total.astype(BF16)
            return 0

        lax.fori_loop(0, count, body, 0)


def kernel_terms(u, back, kg):
    rows, width, ch = u.shape[1] - 2, u.shape[2], u.shape[3]
    kg[...] = jnp.zeros_like(kg)
    for f in range(2):

        def body(r, _):
            at = pl.multiple_of((f * rows + r) * width, width)
            b = back[pl.ds(at, width), :]
            shifted = (from_right(b, width), b, from_left(b, width))
            for g in range(2):
                for dh in range(3):
                    val = u[g, r + dh]
                    for dw in range(3):
                        tap = (g - f + 1) * 9 + dh * 3 + dw
                        prod = (shifted[dw] * val).reshape(width // 8, 8, ch)
                        kg[tap] += jnp.sum(prod, axis=0)
            return 0

        lax.fori_loop(0, rows, body, 0)


def kernel_rows(kg):
    ch = kg.shape[2]
    summed = jnp.sum(kg[...], axis=1)
    padded = jnp.concatenate([summed, jnp.zeros((128 - 27, ch), F32)], axis=0)
    return padded.T


class Where:
    def __init__(self):
        clip, space = lax.axis_index("clip"), lax.axis_index("space")
        self.space, self.last = space, lax.axis_size("space") - 1
        self.core = lax.rem(clip, 2)
        self.zh = lax.rem(clip // 2, 2)
        self.y = clip // 4
        self.zl = space // 4
        self.x = lax.rem(space, 4)
        self.z = self.zh * 4 + self.zl

    def dev(self, core=None, y=None, z=None, x=None):
        core = self.core if core is None else core
        y = self.y if y is None else y
        zh, zl = (self.zh, self.zl) if z is None else (z // 4, lax.rem(z, 4))
        x = self.x if x is None else x
        return ((y * 2 + zh) * 2 + core, zl * 4 + x)

    def partners(self):
        out = [self.dev(core=1 - self.core)]
        out += [self.dev(y=lax.rem(self.y + d, 4)) for d in range(1, 4)]
        out += [self.dev(z=lax.rem(self.z + d, 8)) for d in range(1, 8)]
        out += [self.dev(x=lax.rem(self.x + d, 4)) for d in range(1, 4)]
        return out


class Reduction:
    def __init__(self, here, g, bufs, snd, rcv):
        self.here, self.g = here, g
        self.s1, self.r1, self.h1, self.s2, self.r2, self.h2, self.r4, self.h4, self.r5 = bufs
        self.snd, self.rcv = snd, rcv

    def copy(self, src, dst, n, peer):
        return pltpu.make_async_remote_copy(
            src_ref=src, dst_ref=dst, send_sem=self.snd.at[n], recv_sem=self.rcv.at[n],
            device_id=peer, device_id_type=MESH,
        )

    def core_start(self):
        t = self.here
        self.s1[...] = self.g[pl.ds(pl.multiple_of((1 - t.core) * 128, 128), 128), :].astype(BF16)
        self.live = [self.copy(self.s1, self.r1, 0, t.dev(core=1 - t.core))]
        self.live[0].start()

    def core_end(self):
        t = self.here
        self.live[0].wait()
        self.h1[...] = self.g[pl.ds(pl.multiple_of(t.core * 128, 128), 128), :] + self.r1[
            ...
        ].astype(F32)

    def y_start(self):
        t = self.here
        self.s2[...] = self.h1[...].astype(BF16)
        self.live = []
        for d in range(1, 4):
            to = lax.rem(t.y + d, 4)
            rows = pl.ds(pl.multiple_of(to * 32, 32), 32)
            self.live.append(self.copy(self.s2.at[rows, :], self.r2.at[d - 1], d, t.dev(y=to)))
        for c in self.live:
            c.start()

    def y_end(self):
        t = self.here
        for c in self.live:
            c.wait()
        r2 = self.r2
        self.h2[...] = (
            self.h1[pl.ds(pl.multiple_of(t.y * 32, 32), 32), :]
            + (r2[0].astype(F32) + r2[1].astype(F32) + r2[2].astype(F32))
        ).astype(BF16)

    def share_start(self, source, slots, mine, size, base, peer):
        cs = []
        for d in range(1, size):
            to = lax.rem(mine + d, size)
            cs.append(self.copy(source(to), slots.at[mine], base + d, peer(to)))
        for c in cs:
            c.start()
        slots[mine] = source(mine)[...]
        self.live = cs

    def share_end(self, source, slots, mine, size, base, peer):
        for c in self.live:
            c.wait_send()
        for d in range(1, size):
            came = lax.rem(mine + size - d, size)
            self.copy(source(came), slots.at[came], base + d, peer(came)).wait_recv()
        vals = [slots[n].astype(F32) for n in range(size)]
        while len(vals) > 1:
            vals = [vals[n] + vals[n + 1] for n in range(0, len(vals), 2)]
        return vals[0]

    def z_args(self):
        t = self.here
        source = lambda z: self.h2.at[pl.ds(pl.multiple_of(z // 4 * 16, 16), 16), :]
        return source, self.r4, t.z, 8, 3, lambda z: t.dev(z=z)

    def x_args(self):
        t = self.here
        return lambda x: self.h4, self.r5, t.x, 4, 10, lambda x: t.dev(x=x)

    def z_start(self):
        self.share_start(*self.z_args())

    def z_end(self):
        self.h4[...] = self.share_end(*self.z_args()).astype(BF16)

    def x_start(self):
        self.share_start(*self.x_args())

    def x_end(self):
        return self.share_end(*self.x_args())


def step_kernel(
    x, w1, w2, sl, sh, kl_in, kh_in, al_in, ah_in,
    mism, o_al, o_kl, o_ah, o_kh,
    xs, w1s, w2s, vs, ys, tgt, fh, gate, kl, kh, p_low, p_high,
    ulb, uhb, ul, uh, s_low, s_high, r_low, r_high,
    b_low, b_high, kg_low, kg_high, fine, mism_s, g_low, g_high,
    *rest,
):
    bufs_low, bufs_high = rest[:9], rest[9:18]
    sem, out_sem, halo_snd, halo_rcv, snd_low, rcv_low, snd_high, rcv_high = rest[18:]
    here = Where()
    me, last = here.space, here.last
    scale_low = 1.0 / (16 * 2 * 128 * 32)
    scale_high = scale_low / 4

    barrier = pltpu.get_barrier_semaphore()
    partners = here.partners()
    for p in partners:
        pl.semaphore_signal(barrier, inc=1, device_id=p, device_id_type=MESH)

    @pl.when(me > 0)
    def _():
        pl.semaphore_signal(barrier, inc=1, device_id={"space": me - 1}, device_id_type=MESH)

    @pl.when(me < last)
    def _():
        pl.semaphore_signal(barrier, inc=1, device_id={"space": me + 1}, device_id_type=MESH)

    loads = []

    def load(src, dst):
        c = pltpu.make_async_copy(src, dst, sem.at[len(loads)])
        loads.append(c)
        c.start()
        return c

    c_w2 = load(w2, w2s)
    c_sl = load(sl.at[0], ulb.at[:, 1:9])
    c_sh = load(sh.at[0], uhb.at[:, 1:17])
    c_k = [load(kl_in, kl), load(kh_in, kh), load(al_in, p_low), load(ah_in, p_high)]
    c_x = [load(x.at[0, f], xs.at[1:9, :, f * 512 : (f + 1) * 512]) for f in range(2)]
    c_w1 = [
        load(w1.at[dt, :, dw], w1s.at[:, dt * 512 : (dt + 1) * 512, dw * 256 : (dw + 1) * 256])
        for dt in range(3)
        for dw in range(3)
    ]

    c_w2.wait()
    build_taps(w2s, vs)

    inner = jnp.logical_and(me > 0, me < last)

    @pl.when(inner)
    def _():
        pl.semaphore_wait(barrier, len(partners) + 2)

    @pl.when(jnp.logical_not(inner))
    def _():
        pl.semaphore_wait(barrier, len(partners) + 1)

    def border(side):
        peer = me + 1 if side == 0 else me - 1
        row, low, high = (7, 0, 0) if side == 0 else (0, 9, 17)
        fine_row = 15 if side == 0 else 0
        pairs = [
            (x.at[0, f, row : row + 1], xs.at[low : low + 1, :, f * 512 : (f + 1) * 512])
            for f in range(2)
        ]
        pairs.append((sh.at[0, :, fine_row : fine_row + 1], uhb.at[:, high : high + 1]))
        pairs.append((sl.at[0, :, row : row + 1], ulb.at[:, low : low + 1]))
        pairs.append((tgt.at[:, row * 32 : (row + 1) * 32], fh.at[side]))
        return [
            pltpu.make_async_remote_copy(
                src_ref=a, dst_ref=b, send_sem=halo_snd.at[side, n], recv_sem=halo_rcv.at[side, n],
                device_id={"space": peer}, device_id_type=MESH,
            )
            for n, (a, b) in enumerate(pairs)
        ]

    down, up = border(0), border(1)

    @pl.when(me < last)
    def _():
        for c in down[:4]:
            c.start()

    @pl.when(me > 0)
    def _():
        for c in up[:4]:
            c.start()

    c_sl.wait()
    c_sh.wait()
    for c in c_k:
        c.wait()
    widen(ulb, ul, 1, 8)
    widen(uhb, uh, 1, 16)
    depthwise(ul, kl, s_low, 1, 6)
    depthwise(uh, kh, s_high, 1, 14)

    for c in c_x + c_w1:
        c.wait()

    @pl.when(me > 0)
    def _():
        for c in down[:2]:
            c.wait_recv()

    @pl.when(me == 0)
    def _():
        xs[0] = jnp.zeros((32, 1024), BF16)

    @pl.when(me < last)
    def _():
        for c in up[:2]:
            c.wait_recv()

    @pl.when(me == last)
    def _():
        xs[9] = jnp.zeros((32, 1024), BF16)

    for f in range(2):
        acc = None
        for dh in range(3):
            part = dot(
                xs[dh : dh + 8].reshape(256, 1024), w1s[dh, (1 - f) * 512 : (1 - f) * 512 + 1024, :]
            )
            acc = part if acc is None else acc + part
        ys[:, :768] = acc
        tgt[f] = (
            from_left(ys[:, 0:256], 32) + ys[:, 256:512] + from_right(ys[:, 512:768], 32)
        ).astype(BF16)

    @pl.when(me < last)
    def _():
        down[4].start()

    @pl.when(me > 0)
    def _():
        up[4].start()

    def gated(v):
        wide = v.astype(F32)
        return (wide / (1.0 + jnp.exp(-wide))).astype(BF16)

    for f in range(2):
        gate[1:9, :, f * 256 : (f + 1) * 256] = gated(tgt[f]).reshape(8, 32, 256)

    @pl.when(me > 0)
    def _():
        for c in down[2:4]:
            c.wait_recv()

    @pl.when(me == 0)
    def _():
        for f in range(2):
            ulb[f, 0] = jnp.zeros((32, 256), BF16)
            uhb[f, 0] = jnp.zeros((64, 128), BF16)

    @pl.when(me < last)
    def _():
        for c in up[2:4]:
            c.wait_recv()

    @pl.when(me == last)
    def _():
        for f in range(2):
            ulb[f, 9] = jnp.zeros((32, 256), BF16)
            uhb[f, 17] = jnp.zeros((64, 128), BF16)

    for first in (0, 9):
        widen(ulb, ul, first, 1)
    for first in (0, 17):
        widen(uhb, uh, first, 1)
    for first in (0, 7):
        depthwise(ul, kl, s_low, first, 1)
    for first in (0, 15):
        depthwise(uh, kh, s_high, first, 1)

    for f in range(2):
        rows = slice(f * 256, (f + 1) * 256)
        res = dot(s_low[rows, :], p_low[...]) - tgt[f].astype(F32)
        resid = (res * scale_low).astype(BF16)
        r_low[rows, :] = resid
        b_low[rows, :] = lax.dot_general(
            resid, p_low[...], (((1,), (1,)), ((), ())), preferred_element_type=F32
        )
    a_low = lax.dot_general(
        s_low[...], r_low[...], (((0,), (0,)), ((), ())), preferred_element_type=F32
    )
    kernel_terms(ul, b_low, kg_low)
    k_low = kernel_rows(kg_low)
    for b in range(16):
        i = (b % 8) * 2 + b // 8
        g_low[b * 16 : (b + 1) * 16, 0:256] = a_low[i * 16 : (i + 1) * 16]
        g_low[b * 16 : (b + 1) * 16, 256:384] = k_low[i * 16 : (i + 1) * 16]
    red_low = Reduction(here, g_low, bufs_low, snd_low, rcv_low)
    red_low.core_start()

    @pl.when(me > 0)
    def _():
        down[4].wait_recv()
        for f in range(2):
            gate[0, :, f * 256 : (f + 1) * 256] = gated(fh[0, f])

    @pl.when(me == 0)
    def _():
        gate[0] = jnp.zeros((32, 512), BF16)

    @pl.when(me < last)
    def _():
        up[4].wait_recv()
        for f in range(2):
            gate[9, :, f * 256 : (f + 1) * 256] = gated(fh[1, f])

    @pl.when(me == last)
    def _():
        gate[9] = jnp.zeros((32, 512), BF16)

    for f in range(2):
        for pr in range(2):
            acc = None
            for a in range(2):
                part = dot(
                    gate[pr + a : pr + a + 8].reshape(256, 512),
                    vs[pr * 2 + a, (1 - f) * 256 : (1 - f) * 256 + 512, :],
                )
                acc = part if acc is None else acc + part
            ys[...] = acc
            even = from_left(ys[:, 0:256], 32) + ys[:, 256:512]
            odd = ys[:, 512:768] + from_right(ys[:, 768:1024], 32)
            for pc, val in enumerate((even, odd)):
                for r in range(8):
                    at = (f * 16 + 2 * r + pr) * 64 + pc
                    for half in range(2):
                        fine[half, pl.ds(at, 32, stride=2), :] = val[
                            r * 32 : (r + 1) * 32, half * 128 : (half + 1) * 128
                        ]
        if f == 0:
            red_low.core_end()
            red_low.y_start()
        else:
            red_low.y_end()
            red_low.z_start()

    def fine_body(q, _):
        rows = pl.ds(pl.multiple_of(q * 256, 256), 256)
        target = jnp.concatenate([fine[0, rows, :], fine[1, rows, :]], axis=1)
        target = target.astype(BF16).astype(F32)
        res = dot(s_high[rows, :], p_high[...]) - target
        mism_s[rows, :] = res.astype(BF16)
        resid = (res * scale_high).astype(BF16)
        r_high[rows, :] = resid
        b_high[rows, :] = lax.dot_general(
            resid, p_high[...], (((1,), (1,)), ((), ())), preferred_element_type=F32
        )
        return 0

    lax.fori_loop(0, 8, fine_body, 0)
    outs = []
    for f in range(2):
        c = pltpu.make_async_copy(
            mism_s.reshape(2, 16, 64, 256).at[f], mism.at[0, f], out_sem.at[f]
        )
        c.start()
        outs.append(c)
    red_low.z_end()
    red_low.x_start()
    a_high = lax.dot_general(
        s_high[...], r_high[...], (((0,), (0,)), ((), ())), preferred_element_type=F32
    )
    kernel_terms(uh, b_high, kg_high)
    k_high = kernel_rows(kg_high)
    for b in range(16):
        i = (b % 8) * 2 + b // 8
        g_high[b * 16 : b * 16 + 8, 0:128] = a_high[i * 8 : (i + 1) * 8, 0:128]
        g_high[b * 16 + 8 : b * 16 + 16, 0:128] = a_high[i * 8 : (i + 1) * 8, 128:256]
        g_high[b * 16 : b * 16 + 8, 128:256] = k_high[i * 8 : (i + 1) * 8]
        g_high[b * 16 + 8 : b * 16 + 16, 128:256] = jnp.zeros((8, 128), F32)
    red_high = Reduction(here, g_high, bufs_high, snd_high, rcv_high)
    red_high.core_start()
    low = red_low.x_end()
    o_al[...] = low[:, 0:256]
    low_k = jnp.concatenate([low[:, 256:384], jnp.zeros((112, 128), F32)], axis=0).T
    for dt in range(3):
        for dh in range(3):
            n = (dt * 3 + dh) * 3
            o_kl[dt, dh] = low_k[n : n + 3, 0:16]
    red_high.core_end()
    red_high.y_start()
    red_high.y_end()
    red_high.z_start()
    red_high.z_end()
    red_high.x_start()
    high = red_high.x_end()
    o_ah[...] = jnp.concatenate([high[0:8, 0:128], high[8:16, 0:128]], axis=1)
    high_k = jnp.concatenate([high[0:8, 128:256], jnp.zeros((120, 128), F32)], axis=0).T
    for dt in range(3):
        for dh in range(3):
            n = (dt * 3 + dh) * 3
            o_kh[dt, dh] = high_k[n : n + 3, 0:8]

    for c in outs:
        c.wait()

    @pl.when(me < last)
    def _():
        for c in down:
            c.wait_send()

    @pl.when(me > 0)
    def _():
        for c in up:
            c.wait_send()


def step_call(x, w1, w2, sl, sh, kl, kh, p_low, p_high):
    v = pltpu.VMEM
    dma = pltpu.SemaphoreType.DMA

    def reduction_buffers(lanes):
        return [
            v((128, lanes), BF16),
            v((128, lanes), BF16),
            v((128, lanes), F32),
            v((128, lanes), BF16),
            v((3, 32, lanes), BF16),
            v((32, lanes), BF16),
            v((8, 16, lanes), BF16),
            v((16, lanes), BF16),
            v((4, 16, lanes), BF16),
        ]

    return pl.pallas_call(
        step_kernel,
        out_shape=(
            jax.ShapeDtypeStruct((1, 2, 16, 64, 256), BF16),
            jax.ShapeDtypeStruct((16, 256), F32),
            jax.ShapeDtypeStruct((3, 3, 3, 16), F32),
            jax.ShapeDtypeStruct((8, 256), F32),
            jax.ShapeDtypeStruct((3, 3, 3, 8), F32),
        ),
        in_specs=[ANY] * 9,
        out_specs=(ANY, VM, VM, VM, VM),
        scratch_shapes=[
            v((10, 32, 1024), BF16),
            v((3, 1536, 768), BF16),
            v((3, 3, 3, 256, 256), BF16),
            v((4, 768, 1024), BF16),
            v((256, 1024), F32),
            v((2, 256, 256), BF16),
            v((2, 2, 32, 256), BF16),
            v((10, 32, 512), BF16),
            v((3, 3, 3, 256), F32),
            v((3, 3, 3, 128), F32),
            v((256, 256), BF16),
            v((128, 256), BF16),
            v((2, 10, 32, 256), BF16),
            v((2, 18, 64, 128), BF16),
            v((2, 10, 32, 256), F32),
            v((2, 18, 64, 128), F32),
            v((512, 256), BF16),
            v((2048, 128), BF16),
            v((512, 256), BF16),
            v((2048, 256), BF16),
            v((512, 256), F32),
            v((2048, 128), F32),
            v((27, 8, 256), F32),
            v((27, 8, 128), F32),
            v((2, 2048, 128), F32),
            v((2048, 256), BF16),
            v((256, 384), F32),
            v((256, 256), F32),
            *reduction_buffers(384),
            *reduction_buffers(256),
            dma((18,)),
            dma((2,)),
            dma((2, 5)),
            dma((2, 5)),
            dma((14,)),
            dma((14,)),
            dma((14,)),
            dma((14,)),
        ],
        compiler_params=pltpu.CompilerParams(
            collective_id=0, has_side_effects=True, vmem_limit_bytes=VMEM_LIMIT
        ),
        name="step",
    )(x, w1, w2, sl, sh, kl, kh, p_low, p_high)


def on_device(*args):
    mism, a_low, k_low, a_high, k_high = step_call(*args)
    return a_low, k_low, a_high, k_high, mism


def solution(mesh):
    rows = P("clip", None, "space", None, None)
    in_specs = (rows, P(), P(), rows, rows, P(), P(), P(), P())
    out_specs = (
        P("clip", None),
        P(None, None, None, "clip"),
        P("clip", None),
        P(None, None, None, "clip"),
        rows,
    )
    return jax.shard_map(
        on_device, mesh=mesh, in_specs=in_specs, out_specs=out_specs, check_vma=False
    )
```

```python
import functools

import jax
import jax.numpy as jnp
from jax import lax
from jax.experimental import pallas as pl
from jax.experimental.pallas import tpu as pltpu
from jax.sharding import PartitionSpec as P

F32 = jnp.float32
BF16 = jnp.bfloat16
MESH = pl.DeviceIdType.MESH
ANY = pl.BlockSpec(memory_space=pl.ANY)
HBM = pl.BlockSpec(memory_space=pltpu.HBM)
VM = pl.BlockSpec(memory_space=pltpu.VMEM)
STEP_VMEM = 40 * 1024 * 1024


def dot(a, b):
    return jnp.dot(a, b, preferred_element_type=F32)


def row_ids(v, width):
    ids = lax.broadcasted_iota(jnp.int32, v.shape, 0)
    return ids if v.shape[0] == width else lax.rem(ids, width)


def from_left(v, width):
    return jnp.where(row_ids(v, width) == 0, 0.0, pltpu.roll(v, 1, 0))


def from_right(v, width):
    return jnp.where(row_ids(v, width) == width - 1, 0.0, pltpu.roll(v, v.shape[0] - 1, 0))


def build_taps(w2, v):
    def body(step, _):
        dt, chunk = step // 16, step % 16
        rows = pl.ds(pl.multiple_of(chunk * 16, 16), 16)
        out_rows = pl.ds(pl.multiple_of(dt * 256 + chunk * 16, 16), 16)
        tap = [[w2[dt, dh, dw, rows, :].astype(F32) for dw in range(3)] for dh in range(3)]
        for m in range(4):
            r = []
            for dw in range(3):
                a, b, c = tap[0][dw], tap[1][dw], tap[2][dw]
                r.append((a, b + c, a + b, c)[m])
            for j, col in enumerate((r[0], r[1] + r[2], r[0] + r[1], r[2])):
                v[m, out_rows, j * 256 : (j + 1) * 256] = col.astype(BF16)
        return 0

    lax.fori_loop(0, 48, body, 0)


def widen(src, dst, first, count):
    for f in range(2):

        def body(r, _):
            dst[f, first + r] = src[f, first + r].astype(F32)
            return 0

        lax.fori_loop(0, count, body, 0)


def depthwise(u, k, s, first, count):
    rows, width = u.shape[1] - 2, u.shape[2]
    for f in range(2):

        def body(step, _):
            r = first + step
            parts = [None, None, None]
            for g in range(2):
                for dh in range(3):
                    val = u[g, r + dh]
                    for dw in range(3):
                        term = val * k[g - f + 1, dh, dw : dw + 1, :]
                        parts[dw] = term if parts[dw] is None else parts[dw] + term
            total = u[f, r + 1] + (
                from_left(parts[0], width) + parts[1] + from_right(parts[2], width)
            )
            at = pl.multiple_of((f * rows + r) * width, width)
            s[pl.ds(at, width), :] = total.astype(BF16)
            return 0

        lax.fori_loop(0, count, body, 0)


def kernel_terms(u, back, kg):
    rows, width, ch = u.shape[1] - 2, u.shape[2], u.shape[3]
    kg[...] = jnp.zeros_like(kg)
    for f in range(2):

        def body(r, _):
            at = pl.multiple_of((f * rows + r) * width, width)
            b = back[pl.ds(at, width), :]
            shifted = (from_right(b, width), b, from_left(b, width))
            for g in range(2):
                for dh in range(3):
                    val = u[g, r + dh]
                    for dw in range(3):
                        tap = (g - f + 1) * 9 + dh * 3 + dw
                        prod = (shifted[dw] * val).reshape(width // 8, 8, ch)
                        kg[tap] += jnp.sum(prod, axis=0)
            return 0

        lax.fori_loop(0, rows, body, 0)


def kernel_rows(kg):
    ch = kg.shape[2]
    summed = jnp.sum(kg[...], axis=1)
    padded = jnp.concatenate([summed, jnp.zeros((128 - 27, ch), F32)], axis=0)
    return padded.T


class Where:
    def __init__(self):
        clip, space = lax.axis_index("clip"), lax.axis_index("space")
        self.space, self.last = space, lax.axis_size("space") - 1
        self.core = lax.rem(clip, 2)
        self.zh = lax.rem(clip // 2, 2)
        self.y = clip // 4
        self.zl = space // 4
        self.x = lax.rem(space, 4)
        self.z = self.zh * 4 + self.zl

    def dev(self, core=None, y=None, z=None, x=None):
        core = self.core if core is None else core
        y = self.y if y is None else y
        zh, zl = (self.zh, self.zl) if z is None else (z // 4, lax.rem(z, 4))
        x = self.x if x is None else x
        return ((y * 2 + zh) * 2 + core, zl * 4 + x)

    def partners(self):
        out = [self.dev(core=1 - self.core)]
        out += [self.dev(y=lax.rem(self.y + d, 4)) for d in range(1, 4)]
        out += [self.dev(z=lax.rem(self.z + d, 8)) for d in range(1, 8)]
        out += [self.dev(x=lax.rem(self.x + d, 4)) for d in range(1, 4)]
        return out


class Reduction:
    def __init__(self, here, g, bufs, snd, rcv):
        self.here, self.g = here, g
        self.s1, self.r1, self.h1, self.s2, self.r2, self.h2, self.r4, self.h4, self.r5 = bufs
        self.snd, self.rcv = snd, rcv

    def copy(self, src, dst, n, peer):
        return pltpu.make_async_remote_copy(
            src_ref=src, dst_ref=dst, send_sem=self.snd.at[n], recv_sem=self.rcv.at[n],
            device_id=peer, device_id_type=MESH,
        )

    def core_start(self):
        t = self.here
        self.s1[...] = self.g[pl.ds(pl.multiple_of((1 - t.core) * 128, 128), 128), :].astype(BF16)
        self.live = [self.copy(self.s1, self.r1, 0, t.dev(core=1 - t.core))]
        self.live[0].start()

    def core_end(self):
        t = self.here
        self.live[0].wait()
        self.h1[...] = self.g[pl.ds(pl.multiple_of(t.core * 128, 128), 128), :] + self.r1[
            ...
        ].astype(F32)

    def y_start(self):
        t = self.here
        self.s2[...] = self.h1[...].astype(BF16)
        self.live = []
        for d in range(1, 4):
            to = lax.rem(t.y + d, 4)
            rows = pl.ds(pl.multiple_of(to * 32, 32), 32)
            self.live.append(self.copy(self.s2.at[rows, :], self.r2.at[d - 1], d, t.dev(y=to)))
        for c in self.live:
            c.start()

    def y_end(self):
        t = self.here
        for c in self.live:
            c.wait()
        r2 = self.r2
        self.h2[...] = (
            self.h1[pl.ds(pl.multiple_of(t.y * 32, 32), 32), :]
            + (r2[0].astype(F32) + r2[1].astype(F32) + r2[2].astype(F32))
        ).astype(BF16)

    def share_start(self, source, slots, mine, size, base, peer):
        cs = []
        for d in range(1, size):
            to = lax.rem(mine + d, size)
            cs.append(self.copy(source(to), slots.at[mine], base + d, peer(to)))
        for c in cs:
            c.start()
        slots[mine] = source(mine)[...]
        self.live = cs

    def share_end(self, source, slots, mine, size, base, peer):
        for c in self.live:
            c.wait_send()
        for d in range(1, size):
            came = lax.rem(mine + size - d, size)
            self.copy(source(came), slots.at[came], base + d, peer(came)).wait_recv()
        vals = [slots[n].astype(F32) for n in range(size)]
        while len(vals) > 1:
            vals = [vals[n] + vals[n + 1] for n in range(0, len(vals), 2)]
        return vals[0]

    def z_args(self):
        t = self.here
        source = lambda z: self.h2.at[pl.ds(pl.multiple_of(z // 4 * 16, 16), 16), :]
        return source, self.r4, t.z, 8, 3, lambda z: t.dev(z=z)

    def x_args(self):
        t = self.here
        return lambda x: self.h4, self.r5, t.x, 4, 10, lambda x: t.dev(x=x)

    def z_start(self):
        self.share_start(*self.z_args())

    def z_end(self):
        self.h4[...] = self.share_end(*self.z_args()).astype(BF16)

    def x_start(self):
        self.share_start(*self.x_args())

    def x_end(self):
        return self.share_end(*self.x_args())


def step_kernel(
    x, w1, w2, sl, sh, kl_in, kh_in, al_in, ah_in,
    mism_s, o_low, o_high,
    xs, w1s, w2s, vs, ys, tgt, fh, gate, kl, kh, p_low, p_high,
    ulb, uhb, ul, uh, s_low, s_high, r_low, r_high,
    b_low, b_high, kg_low, kg_high, fine, g_low, g_high,
    *rest,
):
    bufs_low, bufs_high = rest[:9], rest[9:18]
    sem, halo_snd, halo_rcv, snd_low, rcv_low, snd_high, rcv_high = rest[18:]
    here = Where()
    me, last = here.space, here.last
    scale_low = 1.0 / (16 * 2 * 128 * 32)
    scale_high = scale_low / 4

    barrier = pltpu.get_barrier_semaphore()
    partners = here.partners()
    for p in partners:
        pl.semaphore_signal(barrier, inc=1, device_id=p, device_id_type=MESH)

    @pl.when(me > 0)
    def _():
        pl.semaphore_signal(barrier, inc=1, device_id={"space": me - 1}, device_id_type=MESH)

    @pl.when(me < last)
    def _():
        pl.semaphore_signal(barrier, inc=1, device_id={"space": me + 1}, device_id_type=MESH)

    loads = []

    def load(src, dst):
        c = pltpu.make_async_copy(src, dst, sem.at[len(loads)])
        loads.append(c)
        c.start()
        return c

    c_w2 = load(w2, w2s)
    c_sl = load(sl.at[0], ulb.at[:, 1:9])
    c_sh = load(sh.at[0], uhb.at[:, 1:17])
    c_k = [load(kl_in, kl), load(kh_in, kh), load(al_in, p_low), load(ah_in, p_high)]
    c_x = [load(x.at[0, f], xs.at[1:9, :, f * 512 : (f + 1) * 512]) for f in range(2)]
    c_w1 = [
        load(w1.at[dt, :, dw], w1s.at[:, dt * 512 : (dt + 1) * 512, dw * 256 : (dw + 1) * 256])
        for dt in range(3)
        for dw in range(3)
    ]

    c_w2.wait()
    build_taps(w2s, vs)

    inner = jnp.logical_and(me > 0, me < last)

    @pl.when(inner)
    def _():
        pl.semaphore_wait(barrier, len(partners) + 2)

    @pl.when(jnp.logical_not(inner))
    def _():
        pl.semaphore_wait(barrier, len(partners) + 1)

    def border(side):
        peer = me + 1 if side == 0 else me - 1
        row, low, high = (7, 0, 0) if side == 0 else (0, 9, 17)
        fine_row = 15 if side == 0 else 0
        pairs = [
            (x.at[0, f, row : row + 1], xs.at[low : low + 1, :, f * 512 : (f + 1) * 512])
            for f in range(2)
        ]
        pairs.append((sh.at[0, :, fine_row : fine_row + 1], uhb.at[:, high : high + 1]))
        pairs.append((sl.at[0, :, row : row + 1], ulb.at[:, low : low + 1]))
        pairs.append((tgt.at[:, row * 32 : (row + 1) * 32], fh.at[side]))
        return [
            pltpu.make_async_remote_copy(
                src_ref=a, dst_ref=b, send_sem=halo_snd.at[side, n], recv_sem=halo_rcv.at[side, n],
                device_id={"space": peer}, device_id_type=MESH,
            )
            for n, (a, b) in enumerate(pairs)
        ]

    down, up = border(0), border(1)

    @pl.when(me < last)
    def _():
        for c in down[:4]:
            c.start()

    @pl.when(me > 0)
    def _():
        for c in up[:4]:
            c.start()

    c_sl.wait()
    c_sh.wait()
    for c in c_k:
        c.wait()
    widen(ulb, ul, 1, 8)
    widen(uhb, uh, 1, 16)
    depthwise(ul, kl, s_low, 1, 6)
    depthwise(uh, kh, s_high, 1, 14)

    for c in c_x + c_w1:
        c.wait()

    @pl.when(me > 0)
    def _():
        for c in down[:2]:
            c.wait_recv()

    @pl.when(me == 0)
    def _():
        xs[0] = jnp.zeros((32, 1024), BF16)

    @pl.when(me < last)
    def _():
        for c in up[:2]:
            c.wait_recv()

    @pl.when(me == last)
    def _():
        xs[9] = jnp.zeros((32, 1024), BF16)

    for f in range(2):
        acc = None
        for dh in range(3):
            part = dot(
                xs[dh : dh + 8].reshape(256, 1024), w1s[dh, (1 - f) * 512 : (1 - f) * 512 + 1024, :]
            )
            acc = part if acc is None else acc + part
        ys[:, :768] = acc
        tgt[f] = (
            from_left(ys[:, 0:256], 32) + ys[:, 256:512] + from_right(ys[:, 512:768], 32)
        ).astype(BF16)

    @pl.when(me < last)
    def _():
        down[4].start()

    @pl.when(me > 0)
    def _():
        up[4].start()

    def gated(v):
        wide = v.astype(F32)
        return (wide / (1.0 + jnp.exp(-wide))).astype(BF16)

    for f in range(2):
        gate[1:9, :, f * 256 : (f + 1) * 256] = gated(tgt[f]).reshape(8, 32, 256)

    @pl.when(me > 0)
    def _():
        for c in down[2:4]:
            c.wait_recv()

    @pl.when(me == 0)
    def _():
        for f in range(2):
            ulb[f, 0] = jnp.zeros((32, 256), BF16)
            uhb[f, 0] = jnp.zeros((64, 128), BF16)

    @pl.when(me < last)
    def _():
        for c in up[2:4]:
            c.wait_recv()

    @pl.when(me == last)
    def _():
        for f in range(2):
            ulb[f, 9] = jnp.zeros((32, 256), BF16)
            uhb[f, 17] = jnp.zeros((64, 128), BF16)

    for first in (0, 9):
        widen(ulb, ul, first, 1)
    for first in (0, 17):
        widen(uhb, uh, first, 1)
    for first in (0, 7):
        depthwise(ul, kl, s_low, first, 1)
    for first in (0, 15):
        depthwise(uh, kh, s_high, first, 1)

    for f in range(2):
        rows = slice(f * 256, (f + 1) * 256)
        res = dot(s_low[rows, :], p_low[...]) - tgt[f].astype(F32)
        resid = (res * scale_low).astype(BF16)
        r_low[rows, :] = resid
        b_low[rows, :] = lax.dot_general(
            resid, p_low[...], (((1,), (1,)), ((), ())), preferred_element_type=F32
        )
    a_low = lax.dot_general(
        s_low[...], r_low[...], (((0,), (0,)), ((), ())), preferred_element_type=F32
    )
    kernel_terms(ul, b_low, kg_low)
    k_low = kernel_rows(kg_low)
    for b in range(16):
        i = (b % 8) * 2 + b // 8
        g_low[b * 16 : (b + 1) * 16, 0:256] = a_low[i * 16 : (i + 1) * 16]
        g_low[b * 16 : (b + 1) * 16, 256:384] = k_low[i * 16 : (i + 1) * 16]
    red_low = Reduction(here, g_low, bufs_low, snd_low, rcv_low)
    red_low.core_start()

    @pl.when(me > 0)
    def _():
        down[4].wait_recv()
        for f in range(2):
            gate[0, :, f * 256 : (f + 1) * 256] = gated(fh[0, f])

    @pl.when(me == 0)
    def _():
        gate[0] = jnp.zeros((32, 512), BF16)

    @pl.when(me < last)
    def _():
        up[4].wait_recv()
        for f in range(2):
            gate[9, :, f * 256 : (f + 1) * 256] = gated(fh[1, f])

    @pl.when(me == last)
    def _():
        gate[9] = jnp.zeros((32, 512), BF16)

    for f in range(2):
        for pr in range(2):
            acc = None
            for a in range(2):
                part = dot(
                    gate[pr + a : pr + a + 8].reshape(256, 512),
                    vs[pr * 2 + a, (1 - f) * 256 : (1 - f) * 256 + 512, :],
                )
                acc = part if acc is None else acc + part
            ys[...] = acc
            even = from_left(ys[:, 0:256], 32) + ys[:, 256:512]
            odd = ys[:, 512:768] + from_right(ys[:, 768:1024], 32)
            for pc, val in enumerate((even, odd)):
                for r in range(8):
                    at = (f * 16 + 2 * r + pr) * 64 + pc
                    for half in range(2):
                        fine[half, pl.ds(at, 32, stride=2), :] = val[
                            r * 32 : (r + 1) * 32, half * 128 : (half + 1) * 128
                        ]
        if f == 0:
            red_low.core_end()
            red_low.y_start()
        else:
            red_low.y_end()
            red_low.z_start()

    def fine_body(q, _):
        rows = pl.ds(pl.multiple_of(q * 256, 256), 256)
        target = jnp.concatenate([fine[0, rows, :], fine[1, rows, :]], axis=1)
        target = target.astype(BF16).astype(F32)
        res = dot(s_high[rows, :], p_high[...]) - target
        mism_s[rows, :] = res.astype(BF16)
        resid = (res * scale_high).astype(BF16)
        r_high[rows, :] = resid
        b_high[rows, :] = lax.dot_general(
            resid, p_high[...], (((1,), (1,)), ((), ())), preferred_element_type=F32
        )
        return 0

    lax.fori_loop(0, 8, fine_body, 0)
    red_low.z_end()
    red_low.x_start()
    a_high = lax.dot_general(
        s_high[...], r_high[...], (((0,), (0,)), ((), ())), preferred_element_type=F32
    )
    kernel_terms(uh, b_high, kg_high)
    k_high = kernel_rows(kg_high)
    for b in range(16):
        i = (b % 8) * 2 + b // 8
        g_high[b * 16 : b * 16 + 8, 0:128] = a_high[i * 8 : (i + 1) * 8, 0:128]
        g_high[b * 16 + 8 : b * 16 + 16, 0:128] = a_high[i * 8 : (i + 1) * 8, 128:256]
        g_high[b * 16 : b * 16 + 8, 128:256] = k_high[i * 8 : (i + 1) * 8]
        g_high[b * 16 + 8 : b * 16 + 16, 128:256] = jnp.zeros((8, 128), F32)
    red_high = Reduction(here, g_high, bufs_high, snd_high, rcv_high)
    red_high.core_start()
    o_low[...] = red_low.x_end()
    red_high.core_end()
    red_high.y_start()
    red_high.y_end()
    red_high.z_start()
    red_high.z_end()
    red_high.x_start()
    o_high[...] = red_high.x_end()

    @pl.when(me < last)
    def _():
        for c in down:
            c.wait_send()

    @pl.when(me > 0)
    def _():
        for c in up:
            c.wait_send()


def step_call(x, w1, w2, sl, sh, kl, kh, p_low, p_high):
    v = pltpu.VMEM
    dma = pltpu.SemaphoreType.DMA

    def reduction_buffers(lanes):
        return [
            v((128, lanes), BF16),
            v((128, lanes), BF16),
            v((128, lanes), F32),
            v((128, lanes), BF16),
            v((3, 32, lanes), BF16),
            v((32, lanes), BF16),
            v((8, 16, lanes), BF16),
            v((16, lanes), BF16),
            v((4, 16, lanes), BF16),
        ]

    return pl.pallas_call(
        step_kernel,
        out_shape=(
            jax.ShapeDtypeStruct((2048, 256), BF16),
            jax.ShapeDtypeStruct((16, 384), F32),
            jax.ShapeDtypeStruct((16, 256), F32),
        ),
        in_specs=[HBM] * 9,
        out_specs=(VM, VM, VM),
        scratch_shapes=[
            v((10, 32, 1024), BF16),
            v((3, 1536, 768), BF16),
            v((3, 3, 3, 256, 256), BF16),
            v((4, 768, 1024), BF16),
            v((256, 1024), F32),
            v((2, 256, 256), BF16),
            v((2, 2, 32, 256), BF16),
            v((10, 32, 512), BF16),
            v((3, 3, 3, 256), F32),
            v((3, 3, 3, 128), F32),
            v((256, 256), BF16),
            v((128, 256), BF16),
            v((2, 10, 32, 256), BF16),
            v((2, 18, 64, 128), BF16),
            v((2, 10, 32, 256), F32),
            v((2, 18, 64, 128), F32),
            v((512, 256), BF16),
            v((2048, 128), BF16),
            v((512, 256), BF16),
            v((2048, 256), BF16),
            v((512, 256), F32),
            v((2048, 128), F32),
            v((27, 8, 256), F32),
            v((27, 8, 128), F32),
            v((2, 2048, 128), F32),
            v((256, 384), F32),
            v((256, 256), F32),
            *reduction_buffers(384),
            *reduction_buffers(256),
            dma((18,)),
            dma((2, 5)),
            dma((2, 5)),
            dma((14,)),
            dma((14,)),
            dma((14,)),
            dma((14,)),
        ],
        compiler_params=pltpu.CompilerParams(
            collective_id=0, has_side_effects=True, vmem_limit_bytes=STEP_VMEM
        ),
        name="step",
    )(*(pltpu.with_memory_space_constraint(v, pltpu.HBM) for v in (x, w1, w2, sl, sh, kl, kh, p_low, p_high)))


def unpack_kernel(mism_s, low, high, mism, o_al, o_kl, o_ah, o_kh, sem):
    cs = [
        pltpu.make_async_copy(
            mism_s.reshape(2, 16, 64, 256).at[f], mism.at[0, f], sem.at[f]
        )
        for f in range(2)
    ]
    for c in cs:
        c.start()
    o_al[...] = low[:, 0:256]
    o_ah[...] = jnp.concatenate([high[0:8, 0:128], high[8:16, 0:128]], axis=1)
    low_k = jnp.concatenate([low[:, 256:384], jnp.zeros((112, 128), F32)], axis=0).T
    high_k = jnp.concatenate([high[0:8, 128:256], jnp.zeros((120, 128), F32)], axis=0).T
    for dt in range(3):
        for dh in range(3):
            n = (dt * 3 + dh) * 3
            o_kl[dt, dh] = low_k[n : n + 3, 0:16]
            o_kh[dt, dh] = high_k[n : n + 3, 0:8]
    for c in cs:
        c.wait()


def on_device(*args):
    mism, a_low, k_low, a_high, k_high = pl.pallas_call(
        unpack_kernel,
        out_shape=(
            jax.ShapeDtypeStruct((1, 2, 16, 64, 256), BF16),
            jax.ShapeDtypeStruct((16, 256), F32),
            jax.ShapeDtypeStruct((3, 3, 3, 16), F32),
            jax.ShapeDtypeStruct((8, 256), F32),
            jax.ShapeDtypeStruct((3, 3, 3, 8), F32),
        ),
        in_specs=[VM] * 3,
        out_specs=(HBM, VM, VM, VM, VM),
        scratch_shapes=[pltpu.SemaphoreType.DMA((2,))],
        compiler_params=pltpu.CompilerParams(vmem_limit_bytes=4 << 20),
        name="unpack",
    )(*step_call(*args))
    return a_low, k_low, a_high, k_high, mism


def solution(mesh):
    rows = P("clip", None, "space", None, None)
    in_specs = (rows, P(), P(), rows, rows, P(), P(), P(), P())
    out_specs = (
        P("clip", None),
        P(None, None, None, "clip"),
        P("clip", None),
        P(None, None, None, "clip"),
        rows,
    )
    return jax.shard_map(
        on_device, mesh=mesh, in_specs=in_specs, out_specs=out_specs, check_vma=False
    )
```

```python
import functools

import jax
import jax.numpy as jnp
from jax import lax
from jax.experimental import pallas as pl
from jax.experimental.pallas import tpu as pltpu
from jax.sharding import PartitionSpec as P

F32 = jnp.float32
BF16 = jnp.bfloat16
MESH = pl.DeviceIdType.MESH
ANY = pl.BlockSpec(memory_space=pl.ANY)
HBM = pl.BlockSpec(memory_space=pltpu.HBM)
VM = pl.BlockSpec(memory_space=pltpu.VMEM)
STEP_VMEM = 40 * 1024 * 1024


def dot(a, b):
    return jnp.dot(a, b, preferred_element_type=F32)


def row_ids(v, width):
    ids = lax.broadcasted_iota(jnp.int32, v.shape, 0)
    return ids if v.shape[0] == width else lax.rem(ids, width)


def from_left(v, width):
    return jnp.where(row_ids(v, width) == 0, 0.0, pltpu.roll(v, 1, 0))


def from_right(v, width):
    return jnp.where(row_ids(v, width) == width - 1, 0.0, pltpu.roll(v, v.shape[0] - 1, 0))


def build_taps(w2, v):
    def body(step, _):
        dt, chunk = step // 16, step % 16
        rows = pl.ds(pl.multiple_of(chunk * 16, 16), 16)
        out_rows = pl.ds(pl.multiple_of(dt * 256 + chunk * 16, 16), 16)
        tap = [[w2[dt, dh, dw, rows, :].astype(F32) for dw in range(3)] for dh in range(3)]
        for m in range(4):
            r = []
            for dw in range(3):
                a, b, c = tap[0][dw], tap[1][dw], tap[2][dw]
                r.append((a, b + c, a + b, c)[m])
            for j, col in enumerate((r[0], r[1] + r[2], r[0] + r[1], r[2])):
                v[m, out_rows, j * 256 : (j + 1) * 256] = (-col).astype(BF16)
        return 0

    lax.fori_loop(0, 48, body, 0)


def widen(src, dst, first, count):
    for f in range(2):

        def body(r, _):
            dst[f, first + r] = src[f, first + r].astype(F32)
            return 0

        lax.fori_loop(0, count, body, 0)


def depthwise(u, k, s, first, count):
    rows, width = u.shape[1] - 2, u.shape[2]
    for f in range(2):

        def body(step, _):
            r = first + step
            parts = [None, None, None]
            for g in range(2):
                for dh in range(3):
                    val = u[g, r + dh]
                    for dw in range(3):
                        term = val * k[g - f + 1, dh, dw : dw + 1, :]
                        parts[dw] = term if parts[dw] is None else parts[dw] + term
            total = u[f, r + 1] + (
                from_left(parts[0], width) + parts[1] + from_right(parts[2], width)
            )
            at = pl.multiple_of((f * rows + r) * width, width)
            s[pl.ds(at, width), :] = total.astype(BF16)
            return 0

        lax.fori_loop(0, count, body, 0)


def widen_fine(src, tmp, dst, first, count):
    for f in range(2):

        def body(step, _):
            r = first + step
            tmp[...] = src[f, r].astype(F32)
            for pc in range(2):
                dst[pc, f, r] = tmp[pl.ds(pc, 32, stride=2), :]
            return 0

        lax.fori_loop(0, count, body, 0)


def fine_rows(f, r, pc):
    return pl.ds(pl.multiple_of((f * 4 + lax.rem(r, 2) * 2 + pc) * 256 + r // 2 * 32, 32), 32)


def depthwise_fine(u, k, s, first, count):
    for f in range(2):

        def body(step, _):
            r = first + step
            left = even = odd = right = 0.0
            for g in range(2):
                for dh in range(3):
                    e, o = u[0, g, r + dh], u[1, g, r + dh]
                    k0, k1, k2 = (k[g - f + 1, dh, dw : dw + 1, :] for dw in range(3))
                    left += o * k0
                    even += e * k1 + o * k2
                    odd += e * k0 + o * k1
                    right += e * k2
            s[fine_rows(f, r, 0), :] = (u[0, f, r + 1] + (from_left(left, 32) + even)).astype(BF16)
            s[fine_rows(f, r, 1), :] = (u[1, f, r + 1] + (odd + from_right(right, 32))).astype(BF16)
            return 0

        lax.fori_loop(0, count, body, 0)


def kernel_terms_fine(u, back, kg):
    kg[...] = jnp.zeros_like(kg)
    for f in range(2):

        def body(r, _):
            be, bo = back[fine_rows(f, r, 0), :], back[fine_rows(f, r, 1), :]
            be_right, bo_left = from_right(be, 32), from_left(bo, 32)
            for g in range(2):
                for dh in range(3):
                    e, o = u[0, g, r + dh], u[1, g, r + dh]
                    terms = (be_right * o + bo * e, be * e + bo * o, be * o + bo_left * e)
                    for dw in range(3):
                        tap = (g - f + 1) * 9 + dh * 3 + dw
                        kg[tap] += jnp.sum(terms[dw].reshape(4, 8, 128), axis=0)
            return 0

        lax.fori_loop(0, 16, body, 0)


def kernel_terms(u, back, kg):
    rows, width, ch = u.shape[1] - 2, u.shape[2], u.shape[3]
    kg[...] = jnp.zeros_like(kg)
    for f in range(2):

        def body(r, _):
            at = pl.multiple_of((f * rows + r) * width, width)
            b = back[pl.ds(at, width), :]
            shifted = (from_right(b, width), b, from_left(b, width))
            for g in range(2):
                for dh in range(3):
                    val = u[g, r + dh]
                    for dw in range(3):
                        tap = (g - f + 1) * 9 + dh * 3 + dw
                        prod = (shifted[dw] * val).reshape(width // 8, 8, ch)
                        kg[tap] += jnp.sum(prod, axis=0)
            return 0

        lax.fori_loop(0, rows, body, 0)


def kernel_rows(kg):
    ch = kg.shape[2]
    summed = jnp.sum(kg[...], axis=1)
    padded = jnp.concatenate([summed, jnp.zeros((128 - 27, ch), F32)], axis=0)
    return padded.T


class Where:
    def __init__(self):
        clip, space = lax.axis_index("clip"), lax.axis_index("space")
        self.space, self.last = space, lax.axis_size("space") - 1
        self.core = lax.rem(clip, 2)
        self.zh = lax.rem(clip // 2, 2)
        self.y = clip // 4
        self.zl = space // 4
        self.x = lax.rem(space, 4)
        self.z = self.zh * 4 + self.zl

    def dev(self, core=None, y=None, z=None, x=None):
        core = self.core if core is None else core
        y = self.y if y is None else y
        zh, zl = (self.zh, self.zl) if z is None else (z // 4, lax.rem(z, 4))
        x = self.x if x is None else x
        return ((y * 2 + zh) * 2 + core, zl * 4 + x)

    def partners(self):
        out = [self.dev(core=1 - self.core)]
        out += [self.dev(y=lax.rem(self.y + d, 4)) for d in range(1, 4)]
        out += [self.dev(z=lax.rem(self.z + d, 8)) for d in range(1, 8)]
        out += [self.dev(x=lax.rem(self.x + d, 4)) for d in range(1, 4)]
        return out


class Reduction:
    def __init__(self, here, g, bufs, snd, rcv):
        self.here, self.g = here, g
        self.s1, self.r1, self.h1, self.s2, self.r2, self.h2, self.r4, self.h4, self.r5 = bufs
        self.snd, self.rcv = snd, rcv

    def copy(self, src, dst, n, peer):
        return pltpu.make_async_remote_copy(
            src_ref=src, dst_ref=dst, send_sem=self.snd.at[n], recv_sem=self.rcv.at[n],
            device_id=peer, device_id_type=MESH,
        )

    def core_start(self):
        t = self.here
        self.s1[...] = self.g[pl.ds(pl.multiple_of((1 - t.core) * 128, 128), 128), :].astype(BF16)
        self.live = [self.copy(self.s1, self.r1, 0, t.dev(core=1 - t.core))]
        self.live[0].start()

    def core_end(self):
        t = self.here
        self.live[0].wait()
        self.h1[...] = self.g[pl.ds(pl.multiple_of(t.core * 128, 128), 128), :] + self.r1[
            ...
        ].astype(F32)

    def y_start(self):
        t = self.here
        self.s2[...] = self.h1[...].astype(BF16)
        self.live = []
        for d in range(1, 4):
            to = lax.rem(t.y + d, 4)
            rows = pl.ds(pl.multiple_of(to * 32, 32), 32)
            self.live.append(self.copy(self.s2.at[rows, :], self.r2.at[d - 1], d, t.dev(y=to)))
        for c in self.live:
            c.start()

    def y_end(self):
        t = self.here
        for c in self.live:
            c.wait()
        r2 = self.r2
        self.h2[...] = (
            self.h1[pl.ds(pl.multiple_of(t.y * 32, 32), 32), :]
            + (r2[0].astype(F32) + r2[1].astype(F32) + r2[2].astype(F32))
        ).astype(BF16)

    def share_start(self, source, slots, mine, size, base, peer):
        cs = []
        for d in range(1, size):
            to = lax.rem(mine + d, size)
            cs.append(self.copy(source(to), slots.at[mine], base + d, peer(to)))
        for c in cs:
            c.start()
        slots[mine] = source(mine)[...]
        self.live = cs

    def share_end(self, source, slots, mine, size, base, peer):
        for c in self.live:
            c.wait_send()
        for d in range(1, size):
            came = lax.rem(mine + size - d, size)
            self.copy(source(came), slots.at[came], base + d, peer(came)).wait_recv()
        vals = [slots[n].astype(F32) for n in range(size)]
        while len(vals) > 1:
            vals = [vals[n] + vals[n + 1] for n in range(0, len(vals), 2)]
        return vals[0]

    def z_args(self):
        t = self.here
        source = lambda z: self.h2.at[pl.ds(pl.multiple_of(z // 4 * 16, 16), 16), :]
        return source, self.r4, t.z, 8, 3, lambda z: t.dev(z=z)

    def x_args(self):
        t = self.here
        return lambda x: self.h4, self.r5, t.x, 4, 10, lambda x: t.dev(x=x)

    def z_start(self):
        self.share_start(*self.z_args())

    def z_end(self):
        self.h4[...] = self.share_end(*self.z_args()).astype(BF16)

    def x_start(self):
        self.share_start(*self.x_args())

    def x_end(self):
        return self.share_end(*self.x_args())


def step_kernel(
    x, w1, w2, sl, sh, kl_in, kh_in, al_in, ah_in,
    mism_s, o_low, o_high,
    xs, w1s, w2s, vs, tmp, tgt, fh, gate, kl, kh, p_low, p_high, pt_low, pt_high,
    ulb, uhb, ul, uh, s_low, s_high, r_low, r_high,
    b_low, b_high, kg_low, kg_high, fine, g_low, g_high,
    *rest,
):
    bufs_low, bufs_high = rest[:9], rest[9:18]
    sem, halo_snd, halo_rcv, snd_low, rcv_low, snd_high, rcv_high = rest[18:]
    here = Where()
    me, last = here.space, here.last
    scale_low = 1.0 / (16 * 2 * 128 * 32)
    scale_high = scale_low / 4

    barrier = pltpu.get_barrier_semaphore()
    partners = here.partners()
    for p in partners:
        pl.semaphore_signal(barrier, inc=1, device_id=p, device_id_type=MESH)

    @pl.when(me > 0)
    def _():
        pl.semaphore_signal(barrier, inc=1, device_id={"space": me - 1}, device_id_type=MESH)

    @pl.when(me < last)
    def _():
        pl.semaphore_signal(barrier, inc=1, device_id={"space": me + 1}, device_id_type=MESH)

    loads = []

    def load(src, dst):
        c = pltpu.make_async_copy(src, dst, sem.at[len(loads)])
        loads.append(c)
        c.start()
        return c

    c_w2 = load(w2, w2s)
    c_sl = load(sl.at[0], ulb.at[:, 1:9])
    c_sh = load(sh.at[0], uhb.at[:, 1:17])
    c_k = [load(kl_in, kl), load(kh_in, kh), load(al_in, p_low), load(ah_in, p_high)]
    c_x = [load(x.at[0, f], xs.at[1:9, :, f * 512 : (f + 1) * 512]) for f in range(2)]
    c_w1 = [
        load(w1.at[dt, :, dw], w1s.at[:, dt * 512 : (dt + 1) * 512, dw * 256 : (dw + 1) * 256])
        for dt in range(3)
        for dw in range(3)
    ]

    c_w2.wait()
    build_taps(w2s, vs)

    inner = jnp.logical_and(me > 0, me < last)

    @pl.when(inner)
    def _():
        pl.semaphore_wait(barrier, len(partners) + 2)

    @pl.when(jnp.logical_not(inner))
    def _():
        pl.semaphore_wait(barrier, len(partners) + 1)

    def border(side):
        peer = me + 1 if side == 0 else me - 1
        row, low, high = (7, 0, 0) if side == 0 else (0, 9, 17)
        fine_row = 15 if side == 0 else 0
        pairs = [
            (x.at[0, f, row : row + 1], xs.at[low : low + 1, :, f * 512 : (f + 1) * 512])
            for f in range(2)
        ]
        pairs.append((sh.at[0, :, fine_row : fine_row + 1], uhb.at[:, high : high + 1]))
        pairs.append((sl.at[0, :, row : row + 1], ulb.at[:, low : low + 1]))
        pairs.append((tgt.at[:, row * 32 : (row + 1) * 32], fh.at[side]))
        return [
            pltpu.make_async_remote_copy(
                src_ref=a, dst_ref=b, send_sem=halo_snd.at[side, n], recv_sem=halo_rcv.at[side, n],
                device_id={"space": peer}, device_id_type=MESH,
            )
            for n, (a, b) in enumerate(pairs)
        ]

    down, up = border(0), border(1)

    @pl.when(me < last)
    def _():
        for c in down[:4]:
            c.start()

    @pl.when(me > 0)
    def _():
        for c in up[:4]:
            c.start()

    c_sl.wait()
    c_sh.wait()
    for c in c_k:
        c.wait()
    pt_low[...] = p_low[...].astype(F32).T.astype(BF16)
    pt_high[...] = p_high[...].astype(F32).T.astype(BF16)
    widen(ulb, ul, 1, 8)
    widen_fine(uhb, tmp, uh, 1, 16)
    depthwise(ul, kl, s_low, 1, 6)
    depthwise_fine(uh, kh, s_high, 1, 14)

    for c in c_x + c_w1:
        c.wait()

    @pl.when(me > 0)
    def _():
        for c in down[:2]:
            c.wait_recv()

    @pl.when(me == 0)
    def _():
        xs[0] = jnp.zeros((32, 1024), BF16)

    @pl.when(me < last)
    def _():
        for c in up[:2]:
            c.wait_recv()

    @pl.when(me == last)
    def _():
        xs[9] = jnp.zeros((32, 1024), BF16)

    for f in range(2):
        col = []
        for j in range(3):
            acc = None
            for dh in range(3):
                part = dot(
                    xs[dh : dh + 8].reshape(256, 1024),
                    w1s[dh, (1 - f) * 512 : (1 - f) * 512 + 1024, j * 256 : (j + 1) * 256],
                )
                acc = part if acc is None else acc + part
            col.append(acc)
        tgt[f] = (from_left(col[0], 32) + col[1] + from_right(col[2], 32)).astype(BF16)

    @pl.when(me < last)
    def _():
        down[4].start()

    @pl.when(me > 0)
    def _():
        up[4].start()

    def gate_rows(v, lo, hi, f):
        wide = v.astype(F32)
        val = wide / (1.0 + jnp.exp(-wide))
        for n, moved in enumerate((from_left(val, 32), val, from_right(val, 32))):
            gate[n, lo:hi, :, f * 256 : (f + 1) * 256] = moved.astype(BF16).reshape(
                hi - lo, 32, 256
            )

    for f in range(2):
        gate_rows(tgt[f], 1, 9, f)

    @pl.when(me > 0)
    def _():
        for c in down[2:4]:
            c.wait_recv()

    @pl.when(me == 0)
    def _():
        for f in range(2):
            ulb[f, 0] = jnp.zeros((32, 256), BF16)
            uhb[f, 0] = jnp.zeros((64, 128), BF16)

    @pl.when(me < last)
    def _():
        for c in up[2:4]:
            c.wait_recv()

    @pl.when(me == last)
    def _():
        for f in range(2):
            ulb[f, 9] = jnp.zeros((32, 256), BF16)
            uhb[f, 17] = jnp.zeros((64, 128), BF16)

    for first in (0, 9):
        widen(ulb, ul, first, 1)
    for first in (0, 17):
        widen_fine(uhb, tmp, uh, first, 1)
    for first in (0, 7):
        depthwise(ul, kl, s_low, first, 1)
    for first in (0, 15):
        depthwise_fine(uh, kh, s_high, first, 1)

    for f in range(2):
        rows = slice(f * 256, (f + 1) * 256)
        res = dot(s_low[rows, :], p_low[...]) - tgt[f].astype(F32)
        resid = (res * scale_low).astype(BF16)
        r_low[rows, :] = resid
    b_low[...] = dot(r_low[...], pt_low[...])
    a_low = lax.dot_general(
        s_low[...], r_low[...], (((0,), (0,)), ((), ())), preferred_element_type=F32
    )
    kernel_terms(ul, b_low, kg_low)
    k_low = kernel_rows(kg_low)
    for b in range(16):
        i = (b % 8) * 2 + b // 8
        g_low[b * 16 : (b + 1) * 16, 0:256] = a_low[i * 16 : (i + 1) * 16]
        g_low[b * 16 : (b + 1) * 16, 256:384] = k_low[i * 16 : (i + 1) * 16]
    red_low = Reduction(here, g_low, bufs_low, snd_low, rcv_low)
    red_low.core_start()

    @pl.when(me > 0)
    def _():
        down[4].wait_recv()
        for f in range(2):
            gate_rows(fh[0, f], 0, 1, f)

    @pl.when(me == 0)
    def _():
        for n in range(3):
            gate[n, 0] = jnp.zeros((32, 512), BF16)

    @pl.when(me < last)
    def _():
        up[4].wait_recv()
        for f in range(2):
            gate_rows(fh[1, f], 9, 10, f)

    @pl.when(me == last)
    def _():
        for n in range(3):
            gate[n, 9] = jnp.zeros((32, 512), BF16)

    for f in range(2):
        for pr in range(2):
            for pc in range(2):
                at = (f * 4 + pr * 2 + pc) * 256
                rows = slice(at, at + 256)
                res = dot(s_high[rows, :], p_high[...])
                for a in range(2):
                    for b in range(2):
                        j = pc * 2 + b
                        res += dot(
                            gate[pc + b, pr + a : pr + a + 8].reshape(256, 512),
                            vs[
                                pr * 2 + a,
                                (1 - f) * 256 : (1 - f) * 256 + 512,
                                j * 256 : (j + 1) * 256,
                            ],
                        )
                resid = (res * scale_high).astype(BF16)
                r_high[rows, :] = resid
                for r in range(8):
                    to = (f * 16 + 2 * r + pr) * 64 + pc
                    for half in range(2):
                        fine[half, pl.ds(to, 32, stride=2), :] = res[
                            r * 32 : (r + 1) * 32, half * 128 : (half + 1) * 128
                        ]
        half = slice(f * 1024, (f + 1) * 1024)
        b_high[half, :] = dot(r_high[half, :], pt_high[...])
        if f == 0:
            red_low.core_end()
            red_low.y_start()
        else:
            red_low.y_end()
            red_low.z_start()

    def emit(first, count):
        def body(q, _):
            rows = pl.ds(pl.multiple_of(q * 128, 128), 128)
            mism_s[rows, :] = jnp.concatenate(
                [fine[0, rows, :], fine[1, rows, :]], axis=1
            ).astype(BF16)
            return 0

        lax.fori_loop(first, first + count, body, 0)

    red_low.z_end()
    red_low.x_start()
    a_high = lax.dot_general(
        s_high[...], r_high[...], (((0,), (0,)), ((), ())), preferred_element_type=F32
    )
    kernel_terms_fine(uh, b_high, kg_high)
    k_high = kernel_rows(kg_high)
    for b in range(16):
        i = (b % 8) * 2 + b // 8
        g_high[b * 16 : b * 16 + 8, 0:128] = a_high[i * 8 : (i + 1) * 8, 0:128]
        g_high[b * 16 + 8 : b * 16 + 16, 0:128] = a_high[i * 8 : (i + 1) * 8, 128:256]
        g_high[b * 16 : b * 16 + 8, 128:256] = k_high[i * 8 : (i + 1) * 8]
        g_high[b * 16 + 8 : b * 16 + 16, 128:256] = jnp.zeros((8, 128), F32)
    red_high = Reduction(here, g_high, bufs_high, snd_high, rcv_high)
    red_high.core_start()
    o_low[...] = red_low.x_end()
    red_high.core_end()
    red_high.y_start()
    emit(0, 6)
    red_high.y_end()
    red_high.z_start()
    emit(6, 10)
    red_high.z_end()
    red_high.x_start()
    o_high[...] = red_high.x_end()

    @pl.when(me < last)
    def _():
        for c in down:
            c.wait_send()

    @pl.when(me > 0)
    def _():
        for c in up:
            c.wait_send()


def step_call(x, w1, w2, sl, sh, kl, kh, p_low, p_high):
    v = pltpu.VMEM
    dma = pltpu.SemaphoreType.DMA

    def reduction_buffers(lanes):
        return [
            v((128, lanes), BF16),
            v((128, lanes), BF16),
            v((128, lanes), F32),
            v((128, lanes), BF16),
            v((3, 32, lanes), BF16),
            v((32, lanes), BF16),
            v((8, 16, lanes), BF16),
            v((16, lanes), BF16),
            v((4, 16, lanes), BF16),
        ]

    return pl.pallas_call(
        step_kernel,
        out_shape=(
            jax.ShapeDtypeStruct((2048, 256), BF16),
            jax.ShapeDtypeStruct((16, 384), F32),
            jax.ShapeDtypeStruct((16, 256), F32),
        ),
        in_specs=[HBM] * 9,
        out_specs=(VM, VM, VM),
        scratch_shapes=[
            v((10, 32, 1024), BF16),
            v((3, 1536, 768), BF16),
            v((3, 3, 3, 256, 256), BF16),
            v((4, 768, 1024), BF16),
            v((64, 128), F32),
            v((2, 256, 256), BF16),
            v((2, 2, 32, 256), BF16),
            v((3, 10, 32, 512), BF16),
            v((3, 3, 3, 256), F32),
            v((3, 3, 3, 128), F32),
            v((256, 256), BF16),
            v((128, 256), BF16),
            v((256, 256), BF16),
            v((256, 128), BF16),
            v((2, 10, 32, 256), BF16),
            v((2, 18, 64, 128), BF16),
            v((2, 10, 32, 256), F32),
            v((2, 2, 18, 32, 128), F32),
            v((512, 256), BF16),
            v((2048, 128), BF16),
            v((512, 256), BF16),
            v((2048, 256), BF16),
            v((512, 256), F32),
            v((2048, 128), F32),
            v((27, 8, 256), F32),
            v((27, 8, 128), F32),
            v((2, 2048, 128), F32),
            v((256, 384), F32),
            v((256, 256), F32),
            *reduction_buffers(384),
            *reduction_buffers(256),
            dma((18,)),
            dma((2, 5)),
            dma((2, 5)),
            dma((14,)),
            dma((14,)),
            dma((14,)),
            dma((14,)),
        ],
        compiler_params=pltpu.CompilerParams(
            collective_id=0, has_side_effects=True, vmem_limit_bytes=STEP_VMEM
        ),
        name="step",
    )(*(pltpu.with_memory_space_constraint(v, pltpu.HBM) for v in (x, w1, w2, sl, sh, kl, kh, p_low, p_high)))


def unpack_kernel(mism_s, low, high, mism, o_al, o_kl, o_ah, o_kh, sem):
    cs = [
        pltpu.make_async_copy(
            mism_s.reshape(2, 16, 64, 256).at[f], mism.at[0, f], sem.at[f]
        )
        for f in range(2)
    ]
    for c in cs:
        c.start()
    o_al[...] = low[:, 0:256]
    o_ah[...] = jnp.concatenate([high[0:8, 0:128], high[8:16, 0:128]], axis=1)
    low_k = jnp.concatenate([low[:, 256:384], jnp.zeros((112, 128), F32)], axis=0).T
    high_k = jnp.concatenate([high[0:8, 128:256], jnp.zeros((120, 128), F32)], axis=0).T
    for dt in range(3):
        for dh in range(3):
            n = (dt * 3 + dh) * 3
            o_kl[dt, dh] = low_k[n : n + 3, 0:16]
            o_kh[dt, dh] = high_k[n : n + 3, 0:8]
    for c in cs:
        c.wait()


def on_device(*args):
    mism, a_low, k_low, a_high, k_high = pl.pallas_call(
        unpack_kernel,
        out_shape=(
            jax.ShapeDtypeStruct((1, 2, 16, 64, 256), BF16),
            jax.ShapeDtypeStruct((16, 256), F32),
            jax.ShapeDtypeStruct((3, 3, 3, 16), F32),
            jax.ShapeDtypeStruct((8, 256), F32),
            jax.ShapeDtypeStruct((3, 3, 3, 8), F32),
        ),
        in_specs=[VM] * 3,
        out_specs=(HBM, VM, VM, VM, VM),
        scratch_shapes=[pltpu.SemaphoreType.DMA((2,))],
        compiler_params=pltpu.CompilerParams(vmem_limit_bytes=4 << 20),
        name="unpack",
    )(*step_call(*args))
    return a_low, k_low, a_high, k_high, mism


def solution(mesh):
    rows = P("clip", None, "space", None, None)
    in_specs = (rows, P(), P(), rows, rows, P(), P(), P(), P())
    out_specs = (
        P("clip", None),
        P(None, None, None, "clip"),
        P("clip", None),
        P(None, None, None, "clip"),
        rows,
    )
    return jax.shard_map(
        on_device, mesh=mesh, in_specs=in_specs, out_specs=out_specs, check_vma=False
    )
```

```python
import functools

import jax
import jax.numpy as jnp
from jax import lax
from jax.experimental import pallas as pl
from jax.experimental.pallas import tpu as pltpu
from jax.sharding import PartitionSpec as P

F32 = jnp.float32
BF16 = jnp.bfloat16
MESH = pl.DeviceIdType.MESH
ANY = pl.BlockSpec(memory_space=pl.ANY)
HBM = pl.BlockSpec(memory_space=pltpu.HBM)
VM = pl.BlockSpec(memory_space=pltpu.VMEM)
STEP_VMEM = 40 * 1024 * 1024


def dot(a, b):
    return jnp.dot(a, b, preferred_element_type=F32)


def row_ids(v, width):
    ids = lax.broadcasted_iota(jnp.int32, v.shape, 0)
    return ids if v.shape[0] == width else lax.rem(ids, width)


def from_left(v, width):
    return jnp.where(row_ids(v, width) == 0, 0.0, pltpu.roll(v, 1, 0))


def from_right(v, width):
    return jnp.where(row_ids(v, width) == width - 1, 0.0, pltpu.roll(v, v.shape[0] - 1, 0))


def build_taps(w2, v):
    def body(step, _):
        dt, chunk = step // 16, step % 16
        rows = pl.ds(pl.multiple_of(chunk * 16, 16), 16)
        out_rows = pl.ds(pl.multiple_of(dt * 256 + chunk * 16, 16), 16)
        tap = [[w2[dt, dh, dw, rows, :].astype(F32) for dw in range(3)] for dh in range(3)]
        for m in range(4):
            r = []
            for dw in range(3):
                a, b, c = tap[0][dw], tap[1][dw], tap[2][dw]
                r.append((a, b + c, a + b, c)[m])
            for j, col in enumerate((r[0], r[1] + r[2], r[0] + r[1], r[2])):
                v[m, out_rows, j * 256 : (j + 1) * 256] = (-col).astype(BF16)
        return 0

    lax.fori_loop(0, 48, body, 0)


def widen(src, dst, first, count):
    for f in range(2):

        def body(r, _):
            dst[f, first + r] = src[f, first + r].astype(F32)
            return 0

        lax.fori_loop(0, count, body, 0)


def depthwise(u, k, s, first, count):
    rows, width = u.shape[1] - 2, u.shape[2]
    for f in range(2):

        def body(step, _):
            r = first + step
            parts = [None, None, None]
            for g in range(2):
                for dh in range(3):
                    val = u[g, r + dh]
                    for dw in range(3):
                        term = val * k[g - f + 1, dh, dw : dw + 1, :]
                        parts[dw] = term if parts[dw] is None else parts[dw] + term
            total = u[f, r + 1] + (
                from_left(parts[0], width) + parts[1] + from_right(parts[2], width)
            )
            at = pl.multiple_of((f * rows + r) * width, width)
            s[pl.ds(at, width), :] = total.astype(BF16)
            return 0

        lax.fori_loop(0, count, body, 0)


def widen_fine(src, tmp, dst, first, count):
    for f in range(2):

        def body(step, _):
            r = first + step
            tmp[...] = src[f, r].astype(F32)
            for pc in range(2):
                dst[pc, f, r] = tmp[pl.ds(pc, 32, stride=2), :]
            return 0

        lax.fori_loop(0, count, body, 0)


def fine_rows(f, r, pc):
    return pl.ds(pl.multiple_of((f * 4 + lax.rem(r, 2) * 2 + pc) * 256 + r // 2 * 32, 32), 32)


def depthwise_fine(u, k, s, first, count):
    for f in range(2):

        def body(step, _):
            r = first + step
            left = even = odd = right = 0.0
            for g in range(2):
                for dh in range(3):
                    e, o = u[0, g, r + dh], u[1, g, r + dh]
                    k0, k1, k2 = (k[g - f + 1, dh, dw : dw + 1, :] for dw in range(3))
                    left += o * k0
                    even += e * k1 + o * k2
                    odd += e * k0 + o * k1
                    right += e * k2
            s[fine_rows(f, r, 0), :] = (u[0, f, r + 1] + (from_left(left, 32) + even)).astype(BF16)
            s[fine_rows(f, r, 1), :] = (u[1, f, r + 1] + (odd + from_right(right, 32))).astype(BF16)
            return 0

        lax.fori_loop(0, count, body, 0)


def kernel_terms_fine(u, back, kg, frames):
    for f in frames:

        def body(r, _):
            be, bo = back[fine_rows(f, r, 0), :], back[fine_rows(f, r, 1), :]
            be_right, bo_left = from_right(be, 32), from_left(bo, 32)
            for g in range(2):
                for dh in range(3):
                    e, o = u[0, g, r + dh], u[1, g, r + dh]
                    terms = (be_right * o + bo * e, be * e + bo * o, be * o + bo_left * e)
                    for dw in range(3):
                        tap = (g - f + 1) * 9 + dh * 3 + dw
                        kg[tap] += jnp.sum(terms[dw].reshape(4, 8, 128), axis=0)
            return 0

        lax.fori_loop(0, 16, body, 0)


def kernel_terms(u, back, kg):
    rows, width, ch = u.shape[1] - 2, u.shape[2], u.shape[3]
    kg[...] = jnp.zeros_like(kg)
    for f in range(2):

        def body(r, _):
            at = pl.multiple_of((f * rows + r) * width, width)
            b = back[pl.ds(at, width), :]
            shifted = (from_right(b, width), b, from_left(b, width))
            for g in range(2):
                for dh in range(3):
                    val = u[g, r + dh]
                    for dw in range(3):
                        tap = (g - f + 1) * 9 + dh * 3 + dw
                        prod = (shifted[dw] * val).reshape(width // 8, 8, ch)
                        kg[tap] += jnp.sum(prod, axis=0)
            return 0

        lax.fori_loop(0, rows, body, 0)


def kernel_rows(kg):
    ch = kg.shape[2]
    summed = jnp.sum(kg[...], axis=1)
    padded = jnp.concatenate([summed, jnp.zeros((128 - 27, ch), F32)], axis=0)
    return padded.T


class Where:
    def __init__(self):
        clip, space = lax.axis_index("clip"), lax.axis_index("space")
        self.space, self.last = space, lax.axis_size("space") - 1
        self.core = lax.rem(clip, 2)
        self.zh = lax.rem(clip // 2, 2)
        self.y = clip // 4
        self.zl = space // 4
        self.x = lax.rem(space, 4)
        self.z = self.zh * 4 + self.zl

    def dev(self, core=None, y=None, z=None, x=None):
        core = self.core if core is None else core
        y = self.y if y is None else y
        zh, zl = (self.zh, self.zl) if z is None else (z // 4, lax.rem(z, 4))
        x = self.x if x is None else x
        return ((y * 2 + zh) * 2 + core, zl * 4 + x)

    def partners(self):
        out = []
        for d in range(1, 8):
            to = lax.rem(self.core * 4 + self.y + d, 8)
            out.append(self.dev(core=to // 4, y=lax.rem(to, 4)))
        out += [self.dev(z=lax.rem(self.z + d, 8)) for d in range(1, 8)]
        out += [self.dev(x=lax.rem(self.x + d, 4)) for d in range(1, 4)]
        return out


class Reduction:
    def __init__(self, here, g, bufs, snd, rcv):
        self.here, self.g = here, g
        self.s1, self.r1, self.h1, self.s2, self.r2, self.h2, self.r4, self.h4, self.r5 = bufs
        self.snd, self.rcv = snd, rcv

    def copy(self, src, dst, n, peer):
        return pltpu.make_async_remote_copy(
            src_ref=src, dst_ref=dst, send_sem=self.snd.at[n], recv_sem=self.rcv.at[n],
            device_id=peer, device_id_type=MESH,
        )

    def core_start(self):
        t = self.here
        self.s1[...] = self.g[pl.ds(pl.multiple_of((1 - t.core) * 128, 128), 128), :].astype(BF16)
        self.live = [self.copy(self.s1, self.r1, 0, t.dev(core=1 - t.core))]
        self.live[0].start()

    def core_end(self):
        t = self.here
        self.live[0].wait()
        self.h1[...] = self.g[pl.ds(pl.multiple_of(t.core * 128, 128), 128), :] + self.r1[
            ...
        ].astype(F32)

    def y_start(self):
        t = self.here
        self.s2[...] = self.h1[...].astype(BF16)
        self.live = []
        for d in range(1, 4):
            to = lax.rem(t.y + d, 4)
            rows = pl.ds(pl.multiple_of(to * 32, 32), 32)
            self.live.append(self.copy(self.s2.at[rows, :], self.r2.at[d - 1], d, t.dev(y=to)))
        for c in self.live:
            c.start()

    def y_end(self):
        t = self.here
        for c in self.live:
            c.wait()
        r2 = self.r2
        self.h2[:, 0 : r2.shape[2]] = (
            self.h1[pl.ds(pl.multiple_of(t.y * 32, 32), 32), :]
            + (r2[0].astype(F32) + r2[1].astype(F32) + r2[2].astype(F32))
        ).astype(BF16)

    def direct_start(self, g, sk, rk):
        t = self.here
        sk[...] = g[...].astype(BF16)
        self.direct = []
        for d in range(1, 8):
            to = lax.rem(t.core * 4 + t.y + d, 8)
            rows = pl.ds(pl.multiple_of(to * 32, 32), 32)
            peer = t.dev(core=to // 4, y=lax.rem(to, 4))
            self.direct.append(self.copy(sk.at[rows, :], rk.at[d - 1], 13 + d, peer))
        for c in self.direct:
            c.start()

    def direct_end(self, g, rk):
        t = self.here
        for c in self.direct:
            c.wait()
        total = g[pl.ds(pl.multiple_of((t.core * 4 + t.y) * 32, 32), 32), :]
        for d in range(7):
            total += rk[d].astype(F32)
        self.h2[:, 128:256] = total.astype(BF16)

    def share_start(self, source, slots, mine, size, base, peer):
        cs = []
        for d in range(1, size):
            to = lax.rem(mine + d, size)
            cs.append(self.copy(source(to), slots.at[mine], base + d, peer(to)))
        for c in cs:
            c.start()
        slots[mine] = source(mine)[...]
        self.shared = cs

    def share_end(self, source, slots, mine, size, base, peer):
        for c in self.shared:
            c.wait_send()
        for d in range(1, size):
            came = lax.rem(mine + size - d, size)
            self.copy(source(came), slots.at[came], base + d, peer(came)).wait_recv()
        vals = [slots[n].astype(F32) for n in range(size)]
        while len(vals) > 1:
            vals = [vals[n] + vals[n + 1] for n in range(0, len(vals), 2)]
        return vals[0]

    def z_args(self):
        t = self.here
        source = lambda z: self.h2.at[pl.ds(pl.multiple_of(z // 4 * 16, 16), 16), :]
        return source, self.r4, t.z, 8, 3, lambda z: t.dev(z=z)

    def x_args(self):
        t = self.here
        return lambda x: self.h4, self.r5, t.x, 4, 10, lambda x: t.dev(x=x)

    def z_start(self):
        self.share_start(*self.z_args())

    def z_end(self):
        self.h4[...] = self.share_end(*self.z_args()).astype(BF16)

    def x_start(self):
        self.share_start(*self.x_args())

    def x_end(self):
        return self.share_end(*self.x_args())


def step_kernel(
    x, w1, w2, sl, sh, kl_in, kh_in, al_in, ah_in,
    mism_s, o_low, o_high,
    xs, w1s, w2s, vs, tmp, tgt, fh, gate, kl, kh, p_low, p_high, pt_low, pt_high,
    ulb, uhb, ul, uh, s_low, s_high, r_low, r_high,
    b_low, b_high, kg_low, kg_high, fine, g_low, g_high,
    g_kern, s_kern, r_kern, *rest,
):
    bufs_low, bufs_high = rest[:9], rest[9:18]
    sem, halo_snd, halo_rcv, snd_low, rcv_low, snd_high, rcv_high = rest[18:]
    here = Where()
    me, last = here.space, here.last
    scale_low = 1.0 / (16 * 2 * 128 * 32)
    scale_high = scale_low / 4

    barrier = pltpu.get_barrier_semaphore()
    partners = here.partners()
    for p in partners:
        pl.semaphore_signal(barrier, inc=1, device_id=p, device_id_type=MESH)

    @pl.when(me > 0)
    def _():
        pl.semaphore_signal(barrier, inc=1, device_id={"space": me - 1}, device_id_type=MESH)

    @pl.when(me < last)
    def _():
        pl.semaphore_signal(barrier, inc=1, device_id={"space": me + 1}, device_id_type=MESH)

    loads = []

    def load(src, dst):
        c = pltpu.make_async_copy(src, dst, sem.at[len(loads)])
        loads.append(c)
        c.start()
        return c

    c_w2 = load(w2, w2s)
    c_sl = load(sl.at[0], ulb.at[:, 1:9])
    c_sh = load(sh.at[0], uhb.at[:, 1:17])
    c_k = [load(kl_in, kl), load(kh_in, kh), load(al_in, p_low), load(ah_in, p_high)]
    c_x = [load(x.at[0, f], xs.at[1:9, :, f * 512 : (f + 1) * 512]) for f in range(2)]
    c_w1 = [
        load(w1.at[dt, :, dw], w1s.at[:, dt * 512 : (dt + 1) * 512, dw * 256 : (dw + 1) * 256])
        for dt in range(3)
        for dw in range(3)
    ]

    inner = jnp.logical_and(me > 0, me < last)

    @pl.when(inner)
    def _():
        pl.semaphore_wait(barrier, len(partners) + 2)

    @pl.when(jnp.logical_not(inner))
    def _():
        pl.semaphore_wait(barrier, len(partners) + 1)

    def border(side):
        peer = me + 1 if side == 0 else me - 1
        row, low, high = (7, 0, 0) if side == 0 else (0, 9, 17)
        fine_row = 15 if side == 0 else 0
        pairs = [
            (x.at[0, f, row : row + 1], xs.at[low : low + 1, :, f * 512 : (f + 1) * 512])
            for f in range(2)
        ]
        pairs.append((sh.at[0, :, fine_row : fine_row + 1], uhb.at[:, high : high + 1]))
        pairs.append((sl.at[0, :, row : row + 1], ulb.at[:, low : low + 1]))
        pairs.append((tgt.at[:, row * 32 : (row + 1) * 32], fh.at[side]))
        return [
            pltpu.make_async_remote_copy(
                src_ref=a, dst_ref=b, send_sem=halo_snd.at[side, n], recv_sem=halo_rcv.at[side, n],
                device_id={"space": peer}, device_id_type=MESH,
            )
            for n, (a, b) in enumerate(pairs)
        ]

    down, up = border(0), border(1)

    @pl.when(me < last)
    def _():
        for c in down[:4]:
            c.start()

    @pl.when(me > 0)
    def _():
        for c in up[:4]:
            c.start()

    c_w2.wait()
    build_taps(w2s, vs)

    c_sl.wait()
    c_sh.wait()
    for c in c_k:
        c.wait()
    pt_low[...] = p_low[...].astype(F32).T.astype(BF16)
    pt_high[...] = p_high[...].astype(F32).T.astype(BF16)
    widen(ulb, ul, 1, 8)
    widen_fine(uhb, tmp, uh, 1, 16)
    depthwise(ul, kl, s_low, 1, 6)
    depthwise_fine(uh, kh, s_high, 1, 14)

    for c in c_x + c_w1:
        c.wait()

    @pl.when(me > 0)
    def _():
        for c in down[:2]:
            c.wait_recv()

    @pl.when(me == 0)
    def _():
        xs[0] = jnp.zeros((32, 1024), BF16)

    @pl.when(me < last)
    def _():
        for c in up[:2]:
            c.wait_recv()

    @pl.when(me == last)
    def _():
        xs[9] = jnp.zeros((32, 1024), BF16)

    for f in range(2):
        col = []
        for j in range(3):
            acc = None
            for dh in range(3):
                part = dot(
                    xs[dh : dh + 8].reshape(256, 1024),
                    w1s[dh, (1 - f) * 512 : (1 - f) * 512 + 1024, j * 256 : (j + 1) * 256],
                )
                acc = part if acc is None else acc + part
            col.append(acc)
        tgt[f] = (from_left(col[0], 32) + col[1] + from_right(col[2], 32)).astype(BF16)

    @pl.when(me < last)
    def _():
        down[4].start()

    @pl.when(me > 0)
    def _():
        up[4].start()

    def gate_rows(v, lo, hi, f):
        wide = v.astype(F32)
        val = wide / (1.0 + jnp.exp(-wide))
        for n, moved in enumerate((from_left(val, 32), val, from_right(val, 32))):
            gate[n, lo:hi, :, f * 256 : (f + 1) * 256] = moved.astype(BF16).reshape(
                hi - lo, 32, 256
            )

    for f in range(2):
        gate_rows(tgt[f], 1, 9, f)

    @pl.when(me > 0)
    def _():
        for c in down[2:4]:
            c.wait_recv()

    @pl.when(me == 0)
    def _():
        for f in range(2):
            ulb[f, 0] = jnp.zeros((32, 256), BF16)
            uhb[f, 0] = jnp.zeros((64, 128), BF16)

    @pl.when(me < last)
    def _():
        for c in up[2:4]:
            c.wait_recv()

    @pl.when(me == last)
    def _():
        for f in range(2):
            ulb[f, 9] = jnp.zeros((32, 256), BF16)
            uhb[f, 17] = jnp.zeros((64, 128), BF16)

    for first in (0, 9):
        widen(ulb, ul, first, 1)
    for first in (0, 17):
        widen_fine(uhb, tmp, uh, first, 1)
    for first in (0, 7):
        depthwise(ul, kl, s_low, first, 1)
    for first in (0, 15):
        depthwise_fine(uh, kh, s_high, first, 1)

    for f in range(2):
        rows = slice(f * 256, (f + 1) * 256)
        res = dot(s_low[rows, :], p_low[...]) - tgt[f].astype(F32)
        resid = (res * scale_low).astype(BF16)
        r_low[rows, :] = resid
    b_low[...] = dot(r_low[...], pt_low[...])
    a_low = lax.dot_general(
        s_low[...], r_low[...], (((0,), (0,)), ((), ())), preferred_element_type=F32
    )
    kernel_terms(ul, b_low, kg_low)
    k_low = kernel_rows(kg_low)
    for b in range(16):
        i = (b % 8) * 2 + b // 8
        g_low[b * 16 : (b + 1) * 16, 0:256] = a_low[i * 16 : (i + 1) * 16]
        g_low[b * 16 : (b + 1) * 16, 256:384] = k_low[i * 16 : (i + 1) * 16]
    red_low = Reduction(here, g_low, bufs_low, snd_low, rcv_low)
    red_low.core_start()

    @pl.when(me > 0)
    def _():
        down[4].wait_recv()
        for f in range(2):
            gate_rows(fh[0, f], 0, 1, f)

    @pl.when(me == 0)
    def _():
        for n in range(3):
            gate[n, 0] = jnp.zeros((32, 512), BF16)

    @pl.when(me < last)
    def _():
        up[4].wait_recv()
        for f in range(2):
            gate_rows(fh[1, f], 9, 10, f)

    @pl.when(me == last)
    def _():
        for n in range(3):
            gate[n, 9] = jnp.zeros((32, 512), BF16)

    for f in range(2):
        for pr in range(2):
            for pc in range(2):
                at = (f * 4 + pr * 2 + pc) * 256
                rows = slice(at, at + 256)
                res = dot(s_high[rows, :], p_high[...])
                for a in range(2):
                    for b in range(2):
                        j = pc * 2 + b
                        res += dot(
                            gate[pc + b, pr + a : pr + a + 8].reshape(256, 512),
                            vs[
                                pr * 2 + a,
                                (1 - f) * 256 : (1 - f) * 256 + 512,
                                j * 256 : (j + 1) * 256,
                            ],
                        )
                resid = (res * scale_high).astype(BF16)
                r_high[rows, :] = resid
                for r in range(8):
                    to = (f * 16 + 2 * r + pr) * 64 + pc
                    for half in range(2):
                        fine[half, pl.ds(to, 32, stride=2), :] = res[
                            r * 32 : (r + 1) * 32, half * 128 : (half + 1) * 128
                        ]
        half = slice(f * 1024, (f + 1) * 1024)
        b_high[half, :] = dot(r_high[half, :], pt_high[...])
        if f == 0:
            red_low.core_end()
            red_low.y_start()
        else:
            red_low.y_end()
            red_low.z_start()

    def emit(first, count):
        def body(q, _):
            rows = pl.ds(pl.multiple_of(q * 128, 128), 128)
            mism_s[rows, :] = jnp.concatenate(
                [fine[0, rows, :], fine[1, rows, :]], axis=1
            ).astype(BF16)
            return 0

        lax.fori_loop(first, first + count, body, 0)

    a_high = lax.dot_general(
        s_high[...], r_high[...], (((0,), (0,)), ((), ())), preferred_element_type=F32
    )
    for b in range(16):
        i = (b % 8) * 2 + b // 8
        g_high[b * 16 : b * 16 + 8, :] = a_high[i * 8 : (i + 1) * 8, 0:128]
        g_high[b * 16 + 8 : b * 16 + 16, :] = a_high[i * 8 : (i + 1) * 8, 128:256]
    red_high = Reduction(here, g_high, bufs_high, snd_high, rcv_high)
    red_high.core_start()
    kg_high[...] = jnp.zeros_like(kg_high)
    kernel_terms_fine(uh, b_high, kg_high, (0,))
    red_high.core_end()
    red_high.y_start()
    kernel_terms_fine(uh, b_high, kg_high, (1,))
    k_high = kernel_rows(kg_high)
    for b in range(16):
        i = (b % 8) * 2 + b // 8
        g_kern[b * 16 : b * 16 + 8, :] = k_high[i * 8 : (i + 1) * 8]
        g_kern[b * 16 + 8 : b * 16 + 16, :] = jnp.zeros((8, 128), F32)
    red_high.direct_start(g_kern, s_kern, r_kern)
    red_high.y_end()
    emit(0, 8)
    red_high.direct_end(g_kern, r_kern)
    red_high.z_start()
    red_low.z_end()
    red_low.x_start()
    emit(8, 8)
    red_high.z_end()
    red_high.x_start()
    o_low[...] = red_low.x_end()
    o_high[...] = red_high.x_end()

    @pl.when(me < last)
    def _():
        for c in down:
            c.wait_send()

    @pl.when(me > 0)
    def _():
        for c in up:
            c.wait_send()


def step_call(x, w1, w2, sl, sh, kl, kh, p_low, p_high):
    v = pltpu.VMEM
    dma = pltpu.SemaphoreType.DMA

    def reduction_buffers(lanes, later):
        return [
            v((128, lanes), BF16),
            v((128, lanes), BF16),
            v((128, lanes), F32),
            v((128, lanes), BF16),
            v((3, 32, lanes), BF16),
            v((32, later), BF16),
            v((8, 16, later), BF16),
            v((16, later), BF16),
            v((4, 16, later), BF16),
        ]

    return pl.pallas_call(
        step_kernel,
        out_shape=(
            jax.ShapeDtypeStruct((2048, 256), BF16),
            jax.ShapeDtypeStruct((16, 384), F32),
            jax.ShapeDtypeStruct((16, 256), F32),
        ),
        in_specs=[HBM] * 9,
        out_specs=(VM, VM, VM),
        scratch_shapes=[
            v((10, 32, 1024), BF16),
            v((3, 1536, 768), BF16),
            v((3, 3, 3, 256, 256), BF16),
            v((4, 768, 1024), BF16),
            v((64, 128), F32),
            v((2, 256, 256), BF16),
            v((2, 2, 32, 256), BF16),
            v((3, 10, 32, 512), BF16),
            v((3, 3, 3, 256), F32),
            v((3, 3, 3, 128), F32),
            v((256, 256), BF16),
            v((128, 256), BF16),
            v((256, 256), BF16),
            v((256, 128), BF16),
            v((2, 10, 32, 256), BF16),
            v((2, 18, 64, 128), BF16),
            v((2, 10, 32, 256), F32),
            v((2, 2, 18, 32, 128), F32),
            v((512, 256), BF16),
            v((2048, 128), BF16),
            v((512, 256), BF16),
            v((2048, 256), BF16),
            v((512, 256), F32),
            v((2048, 128), F32),
            v((27, 8, 256), F32),
            v((27, 8, 128), F32),
            v((2, 2048, 128), F32),
            v((256, 384), F32),
            v((256, 128), F32),
            v((256, 128), F32),
            v((256, 128), BF16),
            v((7, 32, 128), BF16),
            *reduction_buffers(384, 384),
            *reduction_buffers(128, 256),
            dma((18,)),
            dma((2, 5)),
            dma((2, 5)),
            dma((14,)),
            dma((14,)),
            dma((21,)),
            dma((21,)),
        ],
        compiler_params=pltpu.CompilerParams(
            collective_id=0, has_side_effects=True, vmem_limit_bytes=STEP_VMEM
        ),
        name="step",
    )(*(pltpu.with_memory_space_constraint(v, pltpu.HBM) for v in (x, w1, w2, sl, sh, kl, kh, p_low, p_high)))


def unpack_kernel(mism_s, low, high, mism, o_al, o_kl, o_ah, o_kh, sem):
    cs = [
        pltpu.make_async_copy(
            mism_s.reshape(2, 16, 64, 256).at[f], mism.at[0, f], sem.at[f]
        )
        for f in range(2)
    ]
    for c in cs:
        c.start()
    o_al[...] = low[:, 0:256]
    o_ah[...] = jnp.concatenate([high[0:8, 0:128], high[8:16, 0:128]], axis=1)
    low_k = jnp.concatenate([low[:, 256:384], jnp.zeros((112, 128), F32)], axis=0).T
    high_k = jnp.concatenate([high[0:8, 128:256], jnp.zeros((120, 128), F32)], axis=0).T
    for dt in range(3):
        for dh in range(3):
            n = (dt * 3 + dh) * 3
            o_kl[dt, dh] = low_k[n : n + 3, 0:16]
            o_kh[dt, dh] = high_k[n : n + 3, 0:8]
    for c in cs:
        c.wait()


def on_device(*args):
    mism, a_low, k_low, a_high, k_high = pl.pallas_call(
        unpack_kernel,
        out_shape=(
            jax.ShapeDtypeStruct((1, 2, 16, 64, 256), BF16),
            jax.ShapeDtypeStruct((16, 256), F32),
            jax.ShapeDtypeStruct((3, 3, 3, 16), F32),
            jax.ShapeDtypeStruct((8, 256), F32),
            jax.ShapeDtypeStruct((3, 3, 3, 8), F32),
        ),
        in_specs=[VM] * 3,
        out_specs=(HBM, VM, VM, VM, VM),
        scratch_shapes=[pltpu.SemaphoreType.DMA((2,))],
        compiler_params=pltpu.CompilerParams(vmem_limit_bytes=4 << 20),
        name="unpack",
    )(*step_call(*args))
    return a_low, k_low, a_high, k_high, mism


def solution(mesh):
    rows = P("clip", None, "space", None, None)
    in_specs = (rows, P(), P(), rows, rows, P(), P(), P(), P())
    out_specs = (
        P("clip", None),
        P(None, None, None, "clip"),
        P("clip", None),
        P(None, None, None, "clip"),
        rows,
    )
    return jax.shard_map(
        on_device, mesh=mesh, in_specs=in_specs, out_specs=out_specs, check_vma=False
    )
```

```python
import functools

import jax
import jax.numpy as jnp
from jax import lax
from jax.experimental import pallas as pl
from jax.experimental.pallas import tpu as pltpu
from jax.sharding import PartitionSpec as P

F32 = jnp.float32
BF16 = jnp.bfloat16
MESH = pl.DeviceIdType.MESH
ANY = pl.BlockSpec(memory_space=pl.ANY)
HBM = pl.BlockSpec(memory_space=pltpu.HBM)
VM = pl.BlockSpec(memory_space=pltpu.VMEM)
STEP_VMEM = 40 * 1024 * 1024


def dot(a, b):
    return jnp.dot(a, b, preferred_element_type=F32)


def row_ids(v, width):
    ids = lax.broadcasted_iota(jnp.int32, v.shape, 0)
    return ids if v.shape[0] == width else lax.rem(ids, width)


def from_left(v, width):
    return jnp.where(row_ids(v, width) == 0, 0.0, pltpu.roll(v, 1, 0))


def from_right(v, width):
    return jnp.where(row_ids(v, width) == width - 1, 0.0, pltpu.roll(v, v.shape[0] - 1, 0))


def build_taps(w2, v):
    def body(step, _):
        dt, chunk = step // 16, step % 16
        rows = pl.ds(pl.multiple_of(chunk * 16, 16), 16)
        out_rows = pl.ds(pl.multiple_of(dt * 256 + chunk * 16, 16), 16)
        tap = [[w2[dt, dh, dw, rows, :].astype(F32) for dw in range(3)] for dh in range(3)]
        for m in range(4):
            r = []
            for dw in range(3):
                a, b, c = tap[0][dw], tap[1][dw], tap[2][dw]
                r.append((a, b + c, a + b, c)[m])
            for j, col in enumerate((r[0], r[1] + r[2], r[0] + r[1], r[2])):
                v[m, out_rows, j * 256 : (j + 1) * 256] = (-col).astype(BF16)
        return 0

    lax.fori_loop(0, 48, body, 0)


def widen(src, dst, first, count):
    for f in range(2):

        def body(r, _):
            dst[f, first + r] = src[f, first + r].astype(F32)
            return 0

        lax.fori_loop(0, count, body, 0)


def depthwise(u, k, s, first, count):
    rows, width = u.shape[1] - 2, u.shape[2]
    for f in range(2):

        def body(step, _):
            r = first + step
            parts = [None, None, None]
            for g in range(2):
                for dh in range(3):
                    val = u[g, r + dh]
                    for dw in range(3):
                        term = val * k[g - f + 1, dh, dw : dw + 1, :]
                        parts[dw] = term if parts[dw] is None else parts[dw] + term
            total = u[f, r + 1] + (
                from_left(parts[0], width) + parts[1] + from_right(parts[2], width)
            )
            at = pl.multiple_of((f * rows + r) * width, width)
            s[pl.ds(at, width), :] = total.astype(BF16)
            return 0

        lax.fori_loop(0, count, body, 0)


def widen_fine(src, tmp, dst, first, count):
    for f in range(2):

        def body(step, _):
            r = first + step
            tmp[...] = src[f, r].astype(F32)
            for pc in range(2):
                dst[pc, f, r] = tmp[pl.ds(pc, 32, stride=2), :]
            return 0

        lax.fori_loop(0, count, body, 0)


def fine_rows(f, r, pc):
    if isinstance(r, int):
        return pl.ds((f * 4 + r % 2 * 2 + pc) * 256 + r // 2 * 32, 32)
    return pl.ds(pl.multiple_of((f * 4 + lax.rem(r, 2) * 2 + pc) * 256 + r // 2 * 32, 32), 32)


def depthwise_fine(u, k, s, first, count):
    for f in range(2):

        def body(step, _):
            r = first + step
            left = even = odd = right = 0.0
            for g in range(2):
                for dh in range(3):
                    e, o = u[0, g, r + dh], u[1, g, r + dh]
                    k0, k1, k2 = (k[g - f + 1, dh, dw : dw + 1, :] for dw in range(3))
                    left += o * k0
                    even += e * k1 + o * k2
                    odd += e * k0 + o * k1
                    right += e * k2
            s[fine_rows(f, r, 0), :] = (u[0, f, r + 1] + (from_left(left, 32) + even)).astype(BF16)
            s[fine_rows(f, r, 1), :] = (u[1, f, r + 1] + (odd + from_right(right, 32))).astype(BF16)
            return 0

        lax.fori_loop(0, count, body, 0)


def kernel_term_row_fine(u, back, kg, f, r):
    be, bo = back[fine_rows(f, r, 0), :], back[fine_rows(f, r, 1), :]
    be_right, bo_left = from_right(be, 32), from_left(bo, 32)
    for g in range(2):
        for dh in range(3):
            e, o = u[0, g, r + dh], u[1, g, r + dh]
            terms = (be_right * o + bo * e, be * e + bo * o, be * o + bo_left * e)
            for dw in range(3):
                tap = (g - f + 1) * 9 + dh * 3 + dw
                kg[tap] += jnp.sum(terms[dw].reshape(4, 8, 128), axis=0)


def kernel_terms_fine(u, back, kg, f, first, count):
    def body(step, _):
        kernel_term_row_fine(u, back, kg, f, first + step)
        return 0

    lax.fori_loop(0, count, body, 0)


def kernel_terms(u, back, kg):
    rows, width, ch = u.shape[1] - 2, u.shape[2], u.shape[3]
    kg[...] = jnp.zeros_like(kg)
    for f in range(2):

        def body(r, _):
            at = pl.multiple_of((f * rows + r) * width, width)
            b = back[pl.ds(at, width), :]
            shifted = (from_right(b, width), b, from_left(b, width))
            for g in range(2):
                for dh in range(3):
                    val = u[g, r + dh]
                    for dw in range(3):
                        tap = (g - f + 1) * 9 + dh * 3 + dw
                        prod = (shifted[dw] * val).reshape(width // 8, 8, ch)
                        kg[tap] += jnp.sum(prod, axis=0)
            return 0

        lax.fori_loop(0, rows, body, 0)


def kernel_rows(kg):
    ch = kg.shape[2]
    summed = jnp.sum(kg[...], axis=1)
    padded = jnp.concatenate([summed, jnp.zeros((128 - 27, ch), F32)], axis=0)
    return padded.T


class Where:
    def __init__(self):
        clip, space = lax.axis_index("clip"), lax.axis_index("space")
        self.space, self.last = space, lax.axis_size("space") - 1
        self.core = lax.rem(clip, 2)
        self.zh = lax.rem(clip // 2, 2)
        self.y = clip // 4
        self.zl = space // 4
        self.x = lax.rem(space, 4)
        self.z = self.zh * 4 + self.zl

    def dev(self, core=None, y=None, z=None, x=None):
        core = self.core if core is None else core
        y = self.y if y is None else y
        zh, zl = (self.zh, self.zl) if z is None else (z // 4, lax.rem(z, 4))
        x = self.x if x is None else x
        return ((y * 2 + zh) * 2 + core, zl * 4 + x)

    def partners(self):
        out = []
        for d in range(1, 8):
            to = lax.rem(self.core * 4 + self.y + d, 8)
            out.append(self.dev(core=to // 4, y=lax.rem(to, 4)))
        out += [self.dev(z=lax.rem(self.z + d, 8)) for d in range(1, 8)]
        out += [self.dev(x=lax.rem(self.x + d, 4)) for d in range(1, 4)]
        return out


class Reduction:
    def __init__(self, here, g, bufs, snd, rcv):
        self.here, self.g = here, g
        self.s1, self.r1, self.h1, self.s2, self.r2, self.h2, self.r4, self.h4, self.r5 = bufs
        self.snd, self.rcv = snd, rcv

    def copy(self, src, dst, n, peer):
        return pltpu.make_async_remote_copy(
            src_ref=src, dst_ref=dst, send_sem=self.snd.at[n], recv_sem=self.rcv.at[n],
            device_id=peer, device_id_type=MESH,
        )

    def core_start(self):
        t = self.here
        self.s1[...] = self.g[pl.ds(pl.multiple_of((1 - t.core) * 128, 128), 128), :].astype(BF16)
        self.live = [self.copy(self.s1, self.r1, 0, t.dev(core=1 - t.core))]
        self.live[0].start()

    def core_end(self):
        t = self.here
        self.live[0].wait()
        self.h1[...] = self.g[pl.ds(pl.multiple_of(t.core * 128, 128), 128), :] + self.r1[
            ...
        ].astype(F32)

    def y_start(self):
        t = self.here
        self.s2[...] = self.h1[...].astype(BF16)
        self.live = []
        for d in range(1, 4):
            to = lax.rem(t.y + d, 4)
            rows = pl.ds(pl.multiple_of(to * 32, 32), 32)
            self.live.append(self.copy(self.s2.at[rows, :], self.r2.at[d - 1], d, t.dev(y=to)))
        for c in self.live:
            c.start()

    def y_end(self):
        t = self.here
        for c in self.live:
            c.wait()
        r2 = self.r2
        self.h2[:, 0 : r2.shape[2]] = (
            self.h1[pl.ds(pl.multiple_of(t.y * 32, 32), 32), :]
            + (r2[0].astype(F32) + r2[1].astype(F32) + r2[2].astype(F32))
        ).astype(BF16)

    def direct_start(self, g, sk, rk):
        t = self.here
        sk[...] = g[...].astype(BF16)
        self.direct = []
        for d in range(1, 8):
            to = lax.rem(t.core * 4 + t.y + d, 8)
            rows = pl.ds(pl.multiple_of(to * 16, 16), 16)
            peer = t.dev(core=to // 4, y=lax.rem(to, 4))
            self.direct.append(self.copy(sk.at[rows, :], rk.at[d - 1], 13 + d, peer))
        for c in self.direct:
            c.start()

    def direct_end(self, g, rk):
        t = self.here
        for c in self.direct:
            c.wait()
        total = g[pl.ds(pl.multiple_of((t.core * 4 + t.y) * 16, 16), 16), :]
        for d in range(7):
            total += rk[d].astype(F32)
        self.h2[0:8, 128:256] = total[0:8].astype(BF16)
        self.h2[16:24, 128:256] = total[8:16].astype(BF16)

    def share_start(self, source, slots, mine, size, base, peer):
        cs = []
        for d in range(1, size):
            to = lax.rem(mine + d, size)
            cs.append(self.copy(source(to), slots.at[mine], base + d, peer(to)))
        for c in cs:
            c.start()
        slots[mine] = source(mine)[...]
        self.shared = cs

    def share_end(self, source, slots, mine, size, base, peer):
        for c in self.shared:
            c.wait_send()
        for d in range(1, size):
            came = lax.rem(mine + size - d, size)
            self.copy(source(came), slots.at[came], base + d, peer(came)).wait_recv()
        vals = [slots[n].astype(F32) for n in range(size)]
        while len(vals) > 1:
            vals = [vals[n] + vals[n + 1] for n in range(0, len(vals), 2)]
        return vals[0]

    def z_args(self):
        t = self.here
        source = lambda z: self.h2.at[pl.ds(pl.multiple_of(z // 4 * 16, 16), 16), :]
        return source, self.r4, t.z, 8, 3, lambda z: t.dev(z=z)

    def x_args(self):
        t = self.here
        return lambda x: self.h4, self.r5, t.x, 4, 10, lambda x: t.dev(x=x)

    def z_start(self):
        self.share_start(*self.z_args())

    def z_end(self):
        self.h4[...] = self.share_end(*self.z_args()).astype(BF16)

    def x_start(self):
        self.share_start(*self.x_args())

    def x_end(self):
        return self.share_end(*self.x_args())


def step_kernel(
    x, w1, w2, sl, sh, kl_in, kh_in, al_in, ah_in,
    mism_s, o_low, o_high,
    xs, w1s, w2s, vs, tmp, tgt, fh, gate, kl, kh, p_low, p_high, pt_low, pt_high,
    ulb, uhb, ul, uh, s_low, s_high, r_low, r_high,
    b_low, b_high, kg_low, kg_high, fine, g_low, g_high,
    g_kern, s_kern, r_kern, *rest,
):
    bufs_low, bufs_high = rest[:9], rest[9:18]
    sem, halo_snd, halo_rcv, snd_low, rcv_low, snd_high, rcv_high = rest[18:]
    here = Where()
    me, last = here.space, here.last
    scale_low = 1.0 / (16 * 2 * 128 * 32)
    scale_high = scale_low / 4

    barrier = pltpu.get_barrier_semaphore()
    partners = here.partners()
    for p in partners:
        pl.semaphore_signal(barrier, inc=1, device_id=p, device_id_type=MESH)

    @pl.when(me > 0)
    def _():
        pl.semaphore_signal(barrier, inc=1, device_id={"space": me - 1}, device_id_type=MESH)

    @pl.when(me < last)
    def _():
        pl.semaphore_signal(barrier, inc=1, device_id={"space": me + 1}, device_id_type=MESH)

    loads = []

    def load(src, dst):
        c = pltpu.make_async_copy(src, dst, sem.at[len(loads)])
        loads.append(c)
        c.start()
        return c

    c_w2 = load(w2, w2s)
    c_sl = load(sl.at[0], ulb.at[:, 1:9])
    c_sh = load(sh.at[0], uhb.at[:, 1:17])
    c_k = [load(kl_in, kl), load(kh_in, kh), load(al_in, p_low), load(ah_in, p_high)]
    c_x = [load(x.at[0, f], xs.at[1:9, :, f * 512 : (f + 1) * 512]) for f in range(2)]
    c_w1 = [
        load(w1.at[dt, :, dw], w1s.at[:, dt * 512 : (dt + 1) * 512, dw * 256 : (dw + 1) * 256])
        for dt in range(3)
        for dw in range(3)
    ]

    inner = jnp.logical_and(me > 0, me < last)

    @pl.when(inner)
    def _():
        pl.semaphore_wait(barrier, len(partners) + 2)

    @pl.when(jnp.logical_not(inner))
    def _():
        pl.semaphore_wait(barrier, len(partners) + 1)

    def border(side):
        peer = me + 1 if side == 0 else me - 1
        row, low, high = (7, 0, 0) if side == 0 else (0, 9, 17)
        fine_row = 15 if side == 0 else 0
        pairs = [
            (x.at[0, f, row : row + 1], xs.at[low : low + 1, :, f * 512 : (f + 1) * 512])
            for f in range(2)
        ]
        pairs.append((sh.at[0, :, fine_row : fine_row + 1], uhb.at[:, high : high + 1]))
        pairs.append((sl.at[0, :, row : row + 1], ulb.at[:, low : low + 1]))
        pairs.append((tgt.at[:, row * 32 : (row + 1) * 32], fh.at[side]))
        return [
            pltpu.make_async_remote_copy(
                src_ref=a, dst_ref=b, send_sem=halo_snd.at[side, n], recv_sem=halo_rcv.at[side, n],
                device_id={"space": peer}, device_id_type=MESH,
            )
            for n, (a, b) in enumerate(pairs)
        ]

    down, up = border(0), border(1)

    @pl.when(me < last)
    def _():
        for c in down[:4]:
            c.start()

    @pl.when(me > 0)
    def _():
        for c in up[:4]:
            c.start()

    c_w2.wait()
    build_taps(w2s, vs)

    c_sl.wait()
    c_sh.wait()
    for c in c_k:
        c.wait()
    pt_low[...] = p_low[...].astype(F32).T.astype(BF16)
    pt_high[...] = p_high[...].astype(F32).T.astype(BF16)
    widen(ulb, ul, 1, 8)
    widen_fine(uhb, tmp, uh, 1, 16)
    depthwise(ul, kl, s_low, 1, 6)
    depthwise_fine(uh, kh, s_high, 1, 14)

    for c in c_x + c_w1:
        c.wait()

    @pl.when(me > 0)
    def _():
        for c in down[:2]:
            c.wait_recv()

    @pl.when(me == 0)
    def _():
        xs[0] = jnp.zeros((32, 1024), BF16)

    @pl.when(me < last)
    def _():
        for c in up[:2]:
            c.wait_recv()

    @pl.when(me == last)
    def _():
        xs[9] = jnp.zeros((32, 1024), BF16)

    for f in range(2):
        col = []
        for j in range(3):
            acc = None
            for dh in range(3):
                part = dot(
                    xs[dh : dh + 8].reshape(256, 1024),
                    w1s[dh, (1 - f) * 512 : (1 - f) * 512 + 1024, j * 256 : (j + 1) * 256],
                )
                acc = part if acc is None else acc + part
            col.append(acc)
        tgt[f] = (from_left(col[0], 32) + col[1] + from_right(col[2], 32)).astype(BF16)

    @pl.when(me < last)
    def _():
        down[4].start()

    @pl.when(me > 0)
    def _():
        up[4].start()

    def gate_rows(v, lo, hi, f):
        wide = v.astype(F32)
        val = wide / (1.0 + jnp.exp(-wide))
        for n, moved in enumerate((from_left(val, 32), val, from_right(val, 32))):
            gate[n, lo:hi, :, f * 256 : (f + 1) * 256] = moved.astype(BF16).reshape(
                hi - lo, 32, 256
            )

    for f in range(2):
        gate_rows(tgt[f], 1, 9, f)

    @pl.when(me > 0)
    def _():
        for c in down[2:4]:
            c.wait_recv()

    @pl.when(me == 0)
    def _():
        for f in range(2):
            ulb[f, 0] = jnp.zeros((32, 256), BF16)
            uhb[f, 0] = jnp.zeros((64, 128), BF16)

    @pl.when(me < last)
    def _():
        for c in up[2:4]:
            c.wait_recv()

    @pl.when(me == last)
    def _():
        for f in range(2):
            ulb[f, 9] = jnp.zeros((32, 256), BF16)
            uhb[f, 17] = jnp.zeros((64, 128), BF16)

    for first in (0, 9):
        widen(ulb, ul, first, 1)
    for first in (0, 17):
        widen_fine(uhb, tmp, uh, first, 1)
    for first in (0, 7):
        depthwise(ul, kl, s_low, first, 1)
    for first in (0, 15):
        depthwise_fine(uh, kh, s_high, first, 1)

    for f in range(2):
        rows = slice(f * 256, (f + 1) * 256)
        res = dot(s_low[rows, :], p_low[...]) - tgt[f].astype(F32)
        resid = (res * scale_low).astype(BF16)
        r_low[rows, :] = resid
    b_low[...] = dot(r_low[...], pt_low[...])
    a_low = lax.dot_general(
        s_low[...], r_low[...], (((0,), (0,)), ((), ())), preferred_element_type=F32
    )
    kernel_terms(ul, b_low, kg_low)
    k_low = kernel_rows(kg_low)
    for b in range(16):
        i = (b % 8) * 2 + b // 8
        g_low[b * 16 : (b + 1) * 16, 0:256] = a_low[i * 16 : (i + 1) * 16]
        g_low[b * 16 : (b + 1) * 16, 256:384] = k_low[i * 16 : (i + 1) * 16]
    red_low = Reduction(here, g_low, bufs_low, snd_low, rcv_low)
    red_low.core_start()
    kg_high[...] = jnp.zeros_like(kg_high)
    bufs_high[5][...] = jnp.zeros((32, 256), BF16)

    @pl.when(me > 0)
    def _():
        down[4].wait_recv()
        for f in range(2):
            gate_rows(fh[0, f], 0, 1, f)

    @pl.when(me == 0)
    def _():
        for n in range(3):
            gate[n, 0] = jnp.zeros((32, 512), BF16)

    @pl.when(me < last)
    def _():
        up[4].wait_recv()
        for f in range(2):
            gate_rows(fh[1, f], 9, 10, f)

    @pl.when(me == last)
    def _():
        for n in range(3):
            gate[n, 9] = jnp.zeros((32, 512), BF16)

    for f in range(2):
        for pr in range(2):
            for pc in range(2):
                at = (f * 4 + pr * 2 + pc) * 256
                rows = slice(at, at + 256)
                res = dot(s_high[rows, :], p_high[...])
                for a in range(2):
                    for b in range(2):
                        j = pc * 2 + b
                        res += dot(
                            gate[pc + b, pr + a : pr + a + 8].reshape(256, 512),
                            vs[
                                pr * 2 + a,
                                (1 - f) * 256 : (1 - f) * 256 + 512,
                                j * 256 : (j + 1) * 256,
                            ],
                        )
                resid = (res * scale_high).astype(BF16)
                r_high[rows, :] = resid
                if f == 1:
                    for n in range(4):
                        kernel_term_row_fine(uh, b_high, kg_high, 0, (pr * 2 + pc) * 4 + n)
                for r in range(8):
                    to = (f * 16 + 2 * r + pr) * 64 + pc
                    for half in range(2):
                        fine[half, pl.ds(to, 32, stride=2), :] = res[
                            r * 32 : (r + 1) * 32, half * 128 : (half + 1) * 128
                        ]
        half = slice(f * 1024, (f + 1) * 1024)
        b_high[half, :] = dot(r_high[half, :], pt_high[...])
        if f == 0:
            red_low.core_end()
            red_low.y_start()

    def emit(first, count):
        def body(q, _):
            rows = pl.ds(pl.multiple_of(q * 128, 128), 128)
            mism_s[rows, :] = jnp.concatenate(
                [fine[0, rows, :], fine[1, rows, :]], axis=1
            ).astype(BF16)
            return 0

        lax.fori_loop(first, first + count, body, 0)

    a_high = lax.dot_general(
        s_high[...], r_high[...], (((0,), (0,)), ((), ())), preferred_element_type=F32
    )
    for b in range(16):
        i = (b % 8) * 2 + b // 8
        g_high[b * 16 : b * 16 + 8, :] = a_high[i * 8 : (i + 1) * 8, 0:128]
        g_high[b * 16 + 8 : b * 16 + 16, :] = a_high[i * 8 : (i + 1) * 8, 128:256]
    red_high = Reduction(here, g_high, bufs_high, snd_high, rcv_high)
    red_high.core_start()
    kernel_terms_fine(uh, b_high, kg_high, 1, 0, 12)
    red_high.core_end()
    red_high.y_start()
    red_low.y_end()
    red_low.z_start()
    kernel_terms_fine(uh, b_high, kg_high, 1, 12, 4)
    k_high = kernel_rows(kg_high)
    for b in range(16):
        i = (b % 8) * 2 + b // 8
        g_kern[b * 8 : (b + 1) * 8, :] = k_high[i * 8 : (i + 1) * 8]
    red_high.direct_start(g_kern, s_kern, r_kern)
    red_high.y_end()
    emit(0, 8)
    red_high.direct_end(g_kern, r_kern)
    red_high.z_start()
    red_low.z_end()
    red_low.x_start()
    emit(8, 8)
    red_high.z_end()
    red_high.x_start()
    o_low[...] = red_low.x_end()
    o_high[...] = red_high.x_end()

    @pl.when(me < last)
    def _():
        for c in down:
            c.wait_send()

    @pl.when(me > 0)
    def _():
        for c in up:
            c.wait_send()


def step_call(x, w1, w2, sl, sh, kl, kh, p_low, p_high):
    v = pltpu.VMEM
    dma = pltpu.SemaphoreType.DMA

    def reduction_buffers(lanes, later):
        return [
            v((128, lanes), BF16),
            v((128, lanes), BF16),
            v((128, lanes), F32),
            v((128, lanes), BF16),
            v((3, 32, lanes), BF16),
            v((32, later), BF16),
            v((8, 16, later), BF16),
            v((16, later), BF16),
            v((4, 16, later), BF16),
        ]

    return pl.pallas_call(
        step_kernel,
        out_shape=(
            jax.ShapeDtypeStruct((2048, 256), BF16),
            jax.ShapeDtypeStruct((16, 384), F32),
            jax.ShapeDtypeStruct((16, 256), F32),
        ),
        in_specs=[HBM] * 9,
        out_specs=(VM, VM, VM),
        scratch_shapes=[
            v((10, 32, 1024), BF16),
            v((3, 1536, 768), BF16),
            v((3, 3, 3, 256, 256), BF16),
            v((4, 768, 1024), BF16),
            v((64, 128), F32),
            v((2, 256, 256), BF16),
            v((2, 2, 32, 256), BF16),
            v((3, 10, 32, 512), BF16),
            v((3, 3, 3, 256), F32),
            v((3, 3, 3, 128), F32),
            v((256, 256), BF16),
            v((128, 256), BF16),
            v((256, 256), BF16),
            v((256, 128), BF16),
            v((2, 10, 32, 256), BF16),
            v((2, 18, 64, 128), BF16),
            v((2, 10, 32, 256), F32),
            v((2, 2, 18, 32, 128), F32),
            v((512, 256), BF16),
            v((2048, 128), BF16),
            v((512, 256), BF16),
            v((2048, 256), BF16),
            v((512, 256), F32),
            v((2048, 128), F32),
            v((27, 8, 256), F32),
            v((27, 8, 128), F32),
            v((2, 2048, 128), F32),
            v((256, 384), F32),
            v((256, 128), F32),
            v((128, 128), F32),
            v((128, 128), BF16),
            v((7, 16, 128), BF16),
            *reduction_buffers(384, 384),
            *reduction_buffers(128, 256),
            dma((18,)),
            dma((2, 5)),
            dma((2, 5)),
            dma((14,)),
            dma((14,)),
            dma((21,)),
            dma((21,)),
        ],
        compiler_params=pltpu.CompilerParams(
            collective_id=0, has_side_effects=True, vmem_limit_bytes=STEP_VMEM
        ),
        name="step",
    )(*(pltpu.with_memory_space_constraint(v, pltpu.HBM) for v in (x, w1, w2, sl, sh, kl, kh, p_low, p_high)))


def unpack_kernel(mism_s, low, high, mism, o_al, o_kl, o_ah, o_kh, sem):
    cs = [
        pltpu.make_async_copy(
            mism_s.reshape(2, 16, 64, 256).at[f, q * 4 : q * 4 + 4],
            mism.at[0, f, q * 4 : q * 4 + 4],
            sem.at[f * 4 + q],
        )
        for f in range(2)
        for q in range(4)
    ]
    for c in cs:
        c.start()
    o_al[...] = low[:, 0:256]
    o_ah[...] = jnp.concatenate([high[0:8, 0:128], high[8:16, 0:128]], axis=1)
    low_k = jnp.concatenate([low[:, 256:384], jnp.zeros((112, 128), F32)], axis=0).T
    high_k = jnp.concatenate([high[0:8, 128:256], jnp.zeros((120, 128), F32)], axis=0).T
    for dt in range(3):
        for dh in range(3):
            n = (dt * 3 + dh) * 3
            o_kl[dt, dh] = low_k[n : n + 3, 0:16]
            o_kh[dt, dh] = high_k[n : n + 3, 0:8]
    for c in cs:
        c.wait()


def on_device(*args):
    mism, a_low, k_low, a_high, k_high = pl.pallas_call(
        unpack_kernel,
        out_shape=(
            jax.ShapeDtypeStruct((1, 2, 16, 64, 256), BF16),
            jax.ShapeDtypeStruct((16, 256), F32),
            jax.ShapeDtypeStruct((3, 3, 3, 16), F32),
            jax.ShapeDtypeStruct((8, 256), F32),
            jax.ShapeDtypeStruct((3, 3, 3, 8), F32),
        ),
        in_specs=[VM] * 3,
        out_specs=(HBM, VM, VM, VM, VM),
        scratch_shapes=[pltpu.SemaphoreType.DMA((8,))],
        compiler_params=pltpu.CompilerParams(vmem_limit_bytes=4 << 20),
        name="unpack",
    )(*step_call(*args))
    return a_low, k_low, a_high, k_high, mism


def solution(mesh):
    rows = P("clip", None, "space", None, None)
    in_specs = (rows, P(), P(), rows, rows, P(), P(), P(), P())
    out_specs = (
        P("clip", None),
        P(None, None, None, "clip"),
        P("clip", None),
        P(None, None, None, "clip"),
        rows,
    )
    return jax.shard_map(
        on_device, mesh=mesh, in_specs=in_specs, out_specs=out_specs, check_vma=False
    )
```

```python
import functools

import jax
import jax.numpy as jnp
from jax import lax
from jax.experimental import pallas as pl
from jax.experimental.pallas import tpu as pltpu
from jax.sharding import PartitionSpec as P

F32 = jnp.float32
BF16 = jnp.bfloat16
MESH = pl.DeviceIdType.MESH
ANY = pl.BlockSpec(memory_space=pl.ANY)
HBM = pl.BlockSpec(memory_space=pltpu.HBM)
VM = pl.BlockSpec(memory_space=pltpu.VMEM)
STEP_VMEM = 40 * 1024 * 1024


def dot(a, b):
    return jnp.dot(a, b, preferred_element_type=F32)


def row_ids(v, width):
    ids = lax.broadcasted_iota(jnp.int32, v.shape, 0)
    return ids if v.shape[0] == width else lax.rem(ids, width)


def from_left(v, width):
    return jnp.where(row_ids(v, width) == 0, 0.0, pltpu.roll(v, 1, 0))


def from_right(v, width):
    return jnp.where(row_ids(v, width) == width - 1, 0.0, pltpu.roll(v, v.shape[0] - 1, 0))


def build_taps(w2, v):
    def body(step, _):
        dt, chunk = step // 16, step % 16
        rows = pl.ds(pl.multiple_of(chunk * 16, 16), 16)
        out_rows = pl.ds(pl.multiple_of(dt * 256 + chunk * 16, 16), 16)
        tap = [[w2[dt, dh, dw, rows, :].astype(F32) for dw in range(3)] for dh in range(3)]
        for m in range(4):
            r = []
            for dw in range(3):
                a, b, c = tap[0][dw], tap[1][dw], tap[2][dw]
                r.append((a, b + c, a + b, c)[m])
            for j, col in enumerate((r[0], r[1] + r[2], r[0] + r[1], r[2])):
                v[m, out_rows, j * 256 : (j + 1) * 256] = (-col).astype(BF16)
        return 0

    lax.fori_loop(0, 48, body, 0)


def widen(src, dst, first, count):
    for f in range(2):

        def body(r, _):
            dst[f, first + r] = src[f, first + r].astype(F32)
            return 0

        lax.fori_loop(0, count, body, 0)


def depthwise(u, k, s, first, count):
    rows, width = u.shape[1] - 2, u.shape[2]
    for f in range(2):

        def body(step, _):
            r = first + step
            parts = [None, None, None]
            for g in range(2):
                for dh in range(3):
                    val = u[g, r + dh]
                    for dw in range(3):
                        term = val * k[g - f + 1, dh, dw : dw + 1, :]
                        parts[dw] = term if parts[dw] is None else parts[dw] + term
            total = u[f, r + 1] + (
                from_left(parts[0], width) + parts[1] + from_right(parts[2], width)
            )
            at = pl.multiple_of((f * rows + r) * width, width)
            s[pl.ds(at, width), :] = total.astype(BF16)
            return 0

        lax.fori_loop(0, count, body, 0)


def widen_fine(src, tmp, dst, first, count):
    for f in range(2):

        def body(step, _):
            r = first + step
            tmp[...] = src[f, r].astype(F32)
            for pc in range(2):
                dst[pc, f, r] = tmp[pl.ds(pc, 32, stride=2), :]
            return 0

        lax.fori_loop(0, count, body, 0)


def fine_rows(f, r, pc):
    if isinstance(r, int):
        return pl.ds((f * 4 + r % 2 * 2 + pc) * 256 + r // 2 * 32, 32)
    return pl.ds(pl.multiple_of((f * 4 + lax.rem(r, 2) * 2 + pc) * 256 + r // 2 * 32, 32), 32)


def depthwise_fine(u, k, s, first, count):
    for f in range(2):

        def body(step, _):
            r = first + step
            left = even = odd = right = 0.0
            for g in range(2):
                for dh in range(3):
                    e, o = u[0, g, r + dh], u[1, g, r + dh]
                    k0, k1, k2 = (k[g - f + 1, dh, dw : dw + 1, :] for dw in range(3))
                    left += o * k0
                    even += e * k1 + o * k2
                    odd += e * k0 + o * k1
                    right += e * k2
            s[fine_rows(f, r, 0), :] = (u[0, f, r + 1] + (from_left(left, 32) + even)).astype(BF16)
            s[fine_rows(f, r, 1), :] = (u[1, f, r + 1] + (odd + from_right(right, 32))).astype(BF16)
            return 0

        lax.fori_loop(0, count, body, 0)


def kernel_term_row_fine(u, back, kg, f, r):
    be, bo = back[fine_rows(f, r, 0), :], back[fine_rows(f, r, 1), :]
    be_right, bo_left = from_right(be, 32), from_left(bo, 32)
    for g in range(2):
        for dh in range(3):
            e, o = u[0, g, r + dh], u[1, g, r + dh]
            terms = (be_right * o + bo * e, be * e + bo * o, be * o + bo_left * e)
            for dw in range(3):
                tap = (g - f + 1) * 9 + dh * 3 + dw
                kg[tap] += jnp.sum(terms[dw].reshape(4, 8, 128), axis=0)


def kernel_terms_fine(u, back, kg, f, first, count):
    def body(step, _):
        kernel_term_row_fine(u, back, kg, f, first + step)
        return 0

    lax.fori_loop(0, count, body, 0)


def kernel_terms(u, back, kg):
    rows, width, ch = u.shape[1] - 2, u.shape[2], u.shape[3]
    kg[...] = jnp.zeros_like(kg)
    for f in range(2):

        def body(r, _):
            at = pl.multiple_of((f * rows + r) * width, width)
            b = back[pl.ds(at, width), :]
            shifted = (from_right(b, width), b, from_left(b, width))
            for g in range(2):
                for dh in range(3):
                    val = u[g, r + dh]
                    for dw in range(3):
                        tap = (g - f + 1) * 9 + dh * 3 + dw
                        prod = (shifted[dw] * val).reshape(width // 8, 8, ch)
                        kg[tap] += jnp.sum(prod, axis=0)
            return 0

        lax.fori_loop(0, rows, body, 0)


def kernel_rows(kg):
    ch = kg.shape[2]
    summed = jnp.sum(kg[...], axis=1)
    padded = jnp.concatenate([summed, jnp.zeros((128 - 27, ch), F32)], axis=0)
    return padded.T


class Where:
    def __init__(self):
        clip, space = lax.axis_index("clip"), lax.axis_index("space")
        self.space, self.last = space, lax.axis_size("space") - 1
        self.core = lax.rem(clip, 2)
        self.zh = lax.rem(clip // 2, 2)
        self.y = clip // 4
        self.zl = space // 4
        self.x = lax.rem(space, 4)
        self.z = self.zh * 4 + self.zl

    def dev(self, core=None, y=None, z=None, x=None):
        core = self.core if core is None else core
        y = self.y if y is None else y
        zh, zl = (self.zh, self.zl) if z is None else (z // 4, lax.rem(z, 4))
        x = self.x if x is None else x
        return ((y * 2 + zh) * 2 + core, zl * 4 + x)

    def partners(self):
        out = []
        for d in range(1, 8):
            to = lax.rem(self.core * 4 + self.y + d, 8)
            out.append(self.dev(core=to // 4, y=lax.rem(to, 4)))
        out += [self.dev(z=lax.rem(self.z + d, 8)) for d in range(1, 8)]
        out += [self.dev(x=lax.rem(self.x + d, 4)) for d in range(1, 4)]
        return out


class Reduction:
    def __init__(self, here, g, bufs, snd, rcv):
        self.here, self.g = here, g
        self.s1, self.r1, self.h1, self.s2, self.r2, self.h2, self.r4, self.h4, self.r5 = bufs
        self.snd, self.rcv = snd, rcv

    def copy(self, src, dst, n, peer):
        return pltpu.make_async_remote_copy(
            src_ref=src, dst_ref=dst, send_sem=self.snd.at[n], recv_sem=self.rcv.at[n],
            device_id=peer, device_id_type=MESH,
        )

    def core_start(self):
        t = self.here
        self.s1[...] = self.g[pl.ds(pl.multiple_of((1 - t.core) * 128, 128), 128), :].astype(BF16)
        self.live = [self.copy(self.s1, self.r1, 0, t.dev(core=1 - t.core))]
        self.live[0].start()

    def core_end(self):
        t = self.here
        self.live[0].wait()
        self.h1[...] = self.g[pl.ds(pl.multiple_of(t.core * 128, 128), 128), :] + self.r1[
            ...
        ].astype(F32)

    def y_start(self):
        t = self.here
        self.s2[...] = self.h1[...].astype(BF16)
        self.live = []
        for d in range(1, 4):
            to = lax.rem(t.y + d, 4)
            rows = pl.ds(pl.multiple_of(to * 32, 32), 32)
            self.live.append(self.copy(self.s2.at[rows, :], self.r2.at[d - 1], d, t.dev(y=to)))
        for c in self.live:
            c.start()

    def y_end(self):
        t = self.here
        for c in self.live:
            c.wait()
        r2 = self.r2
        self.h2[:, 0 : r2.shape[2]] = (
            self.h1[pl.ds(pl.multiple_of(t.y * 32, 32), 32), :]
            + (r2[0].astype(F32) + r2[1].astype(F32) + r2[2].astype(F32))
        ).astype(BF16)

    def direct_start(self, g, sk, rk):
        t = self.here
        sk[...] = g[...].astype(BF16)
        self.direct = []
        for d in range(1, 8):
            to = lax.rem(t.core * 4 + t.y + d, 8)
            rows = pl.ds(pl.multiple_of(to * 16, 16), 16)
            peer = t.dev(core=to // 4, y=lax.rem(to, 4))
            self.direct.append(self.copy(sk.at[rows, :], rk.at[d - 1], 13 + d, peer))
        for c in self.direct:
            c.start()

    def direct_end(self, g, rk):
        t = self.here
        for c in self.direct:
            c.wait()
        total = g[pl.ds(pl.multiple_of((t.core * 4 + t.y) * 16, 16), 16), :]
        for d in range(7):
            total += rk[d].astype(F32)
        self.h2[0:8, 128:256] = total[0:8].astype(BF16)
        self.h2[16:24, 128:256] = total[8:16].astype(BF16)

    def share_start(self, source, slots, mine, size, base, peer):
        cs = []
        for d in range(1, size):
            to = lax.rem(mine + d, size)
            cs.append(self.copy(source(to), slots.at[mine], base + d, peer(to)))
        for c in cs:
            c.start()
        slots[mine] = source(mine)[...]
        self.shared = cs

    def share_end(self, source, slots, mine, size, base, peer):
        for c in self.shared:
            c.wait_send()
        for d in range(1, size):
            came = lax.rem(mine + size - d, size)
            self.copy(source(came), slots.at[came], base + d, peer(came)).wait_recv()
        vals = [slots[n].astype(F32) for n in range(size)]
        while len(vals) > 1:
            vals = [vals[n] + vals[n + 1] for n in range(0, len(vals), 2)]
        return vals[0]

    def z_args(self):
        t = self.here
        source = lambda z: self.h2.at[pl.ds(pl.multiple_of(z // 4 * 16, 16), 16), :]
        return source, self.r4, t.z, 8, 3, lambda z: t.dev(z=z)

    def x_args(self):
        t = self.here
        return lambda x: self.h4, self.r5, t.x, 4, 10, lambda x: t.dev(x=x)

    def z_start(self):
        self.share_start(*self.z_args())

    def z_end(self):
        self.h4[...] = self.share_end(*self.z_args()).astype(BF16)

    def x_start(self):
        self.share_start(*self.x_args())

    def x_end(self):
        return self.share_end(*self.x_args())


def step_kernel(
    x, w1, w2, sl, sh, kl_in, kh_in, al_in, ah_in,
    mism_s, o_low, o_high,
    xs, w1s, w2s, vs, tmp, mid, tgt, fh, gate, kl, kh, p_low, p_high, pt_low, pt_high,
    ulb, uhb, ul, uh, s_low, s_high, r_low, r_high,
    b_low, b_high, kg_low, kg_high, fine, g_low, g_high,
    g_kern, s_kern, r_kern, *rest,
):
    bufs_low, bufs_high = rest[:9], rest[9:18]
    sem, halo_snd, halo_rcv, snd_low, rcv_low, snd_high, rcv_high = rest[18:]
    here = Where()
    me, last = here.space, here.last
    scale_low = 1.0 / (16 * 2 * 128 * 32)
    scale_high = scale_low / 4

    barrier = pltpu.get_barrier_semaphore()
    partners = here.partners()
    for p in partners:
        pl.semaphore_signal(barrier, inc=1, device_id=p, device_id_type=MESH)

    @pl.when(me > 0)
    def _():
        pl.semaphore_signal(barrier, inc=1, device_id={"space": me - 1}, device_id_type=MESH)

    @pl.when(me < last)
    def _():
        pl.semaphore_signal(barrier, inc=1, device_id={"space": me + 1}, device_id_type=MESH)

    loads = []

    def load(src, dst):
        c = pltpu.make_async_copy(src, dst, sem.at[len(loads)])
        loads.append(c)
        c.start()
        return c

    c_w2 = load(w2, w2s)
    c_sl = load(sl.at[0], ulb.at[:, 1:9])
    c_sh = load(sh.at[0], uhb.at[:, 1:17])
    c_k = [load(kl_in, kl), load(kh_in, kh), load(al_in, p_low), load(ah_in, p_high)]
    c_x = [load(x.at[0, f], xs.at[1:9, :, f * 512 : (f + 1) * 512]) for f in range(2)]
    c_w1 = [
        load(w1.at[dt, :, dw], w1s.at[:, dt * 512 : (dt + 1) * 512, dw * 256 : (dw + 1) * 256])
        for dt in range(3)
        for dw in range(3)
    ]

    inner = jnp.logical_and(me > 0, me < last)

    @pl.when(inner)
    def _():
        pl.semaphore_wait(barrier, len(partners) + 2)

    @pl.when(jnp.logical_not(inner))
    def _():
        pl.semaphore_wait(barrier, len(partners) + 1)

    def border(side):
        peer = me + 1 if side == 0 else me - 1
        row, low, high = (7, 0, 0) if side == 0 else (0, 9, 17)
        fine_row = 15 if side == 0 else 0
        pairs = [
            (x.at[0, f, row : row + 1], xs.at[low : low + 1, :, f * 512 : (f + 1) * 512])
            for f in range(2)
        ]
        pairs.append((sh.at[0, :, fine_row : fine_row + 1], uhb.at[:, high : high + 1]))
        pairs.append((sl.at[0, :, row : row + 1], ulb.at[:, low : low + 1]))
        pairs.append((tgt.at[:, row * 32 : (row + 1) * 32], fh.at[side]))
        return [
            pltpu.make_async_remote_copy(
                src_ref=a, dst_ref=b, send_sem=halo_snd.at[side, n], recv_sem=halo_rcv.at[side, n],
                device_id={"space": peer}, device_id_type=MESH,
            )
            for n, (a, b) in enumerate(pairs)
        ]

    down, up = border(0), border(1)

    @pl.when(me < last)
    def _():
        for c in down[:4]:
            c.start()

    @pl.when(me > 0)
    def _():
        for c in up[:4]:
            c.start()

    c_w2.wait()
    build_taps(w2s, vs)

    c_sl.wait()
    c_sh.wait()
    for c in c_k:
        c.wait()
    pt_low[...] = p_low[...].astype(F32).T.astype(BF16)
    pt_high[...] = p_high[...].astype(F32).T.astype(BF16)
    widen(ulb, ul, 1, 8)
    widen_fine(uhb, tmp, uh, 1, 16)
    depthwise(ul, kl, s_low, 1, 6)
    depthwise_fine(uh, kh, s_high, 1, 14)

    for c in c_x + c_w1:
        c.wait()

    def conv_part(f, j, dh):
        return dot(
            xs[dh : dh + 8].reshape(256, 1024),
            w1s[dh, (1 - f) * 512 : (1 - f) * 512 + 1024, j * 256 : (j + 1) * 256],
        )

    for f in range(2):
        for j in range(3):
            mid[f, j] = conv_part(f, j, 1)

    @pl.when(me > 0)
    def _():
        for c in down[:2]:
            c.wait_recv()

    @pl.when(me == 0)
    def _():
        xs[0] = jnp.zeros((32, 1024), BF16)

    @pl.when(me < last)
    def _():
        for c in up[:2]:
            c.wait_recv()

    @pl.when(me == last)
    def _():
        xs[9] = jnp.zeros((32, 1024), BF16)

    for f in range(2):
        col = [mid[f, j] + conv_part(f, j, 0) + conv_part(f, j, 2) for j in range(3)]
        tgt[f] = (from_left(col[0], 32) + col[1] + from_right(col[2], 32)).astype(BF16)

    @pl.when(me < last)
    def _():
        down[4].start()

    @pl.when(me > 0)
    def _():
        up[4].start()

    def gate_rows(v, lo, hi, f):
        wide = v.astype(F32)
        val = wide / (1.0 + jnp.exp(-wide))
        for n, moved in enumerate((from_left(val, 32), val, from_right(val, 32))):
            gate[n, lo:hi, :, f * 256 : (f + 1) * 256] = moved.astype(BF16).reshape(
                hi - lo, 32, 256
            )

    for f in range(2):
        gate_rows(tgt[f], 1, 9, f)

    @pl.when(me > 0)
    def _():
        for c in down[2:4]:
            c.wait_recv()

    @pl.when(me == 0)
    def _():
        for f in range(2):
            ulb[f, 0] = jnp.zeros((32, 256), BF16)
            uhb[f, 0] = jnp.zeros((64, 128), BF16)

    @pl.when(me < last)
    def _():
        for c in up[2:4]:
            c.wait_recv()

    @pl.when(me == last)
    def _():
        for f in range(2):
            ulb[f, 9] = jnp.zeros((32, 256), BF16)
            uhb[f, 17] = jnp.zeros((64, 128), BF16)

    for first in (0, 9):
        widen(ulb, ul, first, 1)
    for first in (0, 17):
        widen_fine(uhb, tmp, uh, first, 1)
    for first in (0, 7):
        depthwise(ul, kl, s_low, first, 1)
    for first in (0, 15):
        depthwise_fine(uh, kh, s_high, first, 1)

    for f in range(2):
        rows = slice(f * 256, (f + 1) * 256)
        res = dot(s_low[rows, :], p_low[...]) - tgt[f].astype(F32)
        resid = (res * scale_low).astype(BF16)
        r_low[rows, :] = resid
    b_low[...] = dot(r_low[...], pt_low[...])
    a_low = lax.dot_general(
        s_low[...], r_low[...], (((0,), (0,)), ((), ())), preferred_element_type=F32
    )
    kernel_terms(ul, b_low, kg_low)
    k_low = kernel_rows(kg_low)
    for b in range(16):
        i = (b % 8) * 2 + b // 8
        g_low[b * 16 : (b + 1) * 16, 0:256] = a_low[i * 16 : (i + 1) * 16]
        g_low[b * 16 : (b + 1) * 16, 256:384] = k_low[i * 16 : (i + 1) * 16]
    red_low = Reduction(here, g_low, bufs_low, snd_low, rcv_low)
    red_low.core_start()
    kg_high[...] = jnp.zeros_like(kg_high)
    bufs_high[5][...] = jnp.zeros((32, 256), BF16)

    @pl.when(me > 0)
    def _():
        down[4].wait_recv()
        for f in range(2):
            gate_rows(fh[0, f], 0, 1, f)

    @pl.when(me == 0)
    def _():
        for n in range(3):
            gate[n, 0] = jnp.zeros((32, 512), BF16)

    @pl.when(me < last)
    def _():
        up[4].wait_recv()
        for f in range(2):
            gate_rows(fh[1, f], 9, 10, f)

    @pl.when(me == last)
    def _():
        for n in range(3):
            gate[n, 9] = jnp.zeros((32, 512), BF16)

    for f in range(2):
        for pr in range(2):
            for pc in range(2):
                at = (f * 4 + pr * 2 + pc) * 256
                rows = slice(at, at + 256)
                res = dot(s_high[rows, :], p_high[...])
                for a in range(2):
                    for b in range(2):
                        j = pc * 2 + b
                        res += dot(
                            gate[pc + b, pr + a : pr + a + 8].reshape(256, 512),
                            vs[
                                pr * 2 + a,
                                (1 - f) * 256 : (1 - f) * 256 + 512,
                                j * 256 : (j + 1) * 256,
                            ],
                        )
                resid = (res * scale_high).astype(BF16)
                r_high[rows, :] = resid
                if f == 1:
                    for n in range(4):
                        kernel_term_row_fine(uh, b_high, kg_high, 0, (pr * 2 + pc) * 4 + n)
                for r in range(8):
                    to = (f * 16 + 2 * r + pr) * 64 + pc
                    for half in range(2):
                        fine[half, pl.ds(to, 32, stride=2), :] = res[
                            r * 32 : (r + 1) * 32, half * 128 : (half + 1) * 128
                        ]
        half = slice(f * 1024, (f + 1) * 1024)
        b_high[half, :] = dot(r_high[half, :], pt_high[...])
        if f == 0:
            red_low.core_end()
            red_low.y_start()

    def emit(first, count):
        def body(q, _):
            rows = pl.ds(pl.multiple_of(q * 128, 128), 128)
            mism_s[rows, :] = jnp.concatenate(
                [fine[0, rows, :], fine[1, rows, :]], axis=1
            ).astype(BF16)
            return 0

        lax.fori_loop(first, first + count, body, 0)

    a_high = lax.dot_general(
        s_high[...], r_high[...], (((0,), (0,)), ((), ())), preferred_element_type=F32
    )
    for b in range(16):
        i = (b % 8) * 2 + b // 8
        g_high[b * 16 : b * 16 + 8, :] = a_high[i * 8 : (i + 1) * 8, 0:128]
        g_high[b * 16 + 8 : b * 16 + 16, :] = a_high[i * 8 : (i + 1) * 8, 128:256]
    red_high = Reduction(here, g_high, bufs_high, snd_high, rcv_high)
    red_high.core_start()
    kernel_terms_fine(uh, b_high, kg_high, 1, 0, 12)
    red_high.core_end()
    red_high.y_start()
    kernel_terms_fine(uh, b_high, kg_high, 1, 12, 4)
    k_high = kernel_rows(kg_high)
    for b in range(16):
        i = (b % 8) * 2 + b // 8
        g_kern[b * 8 : (b + 1) * 8, :] = k_high[i * 8 : (i + 1) * 8]
    red_high.direct_start(g_kern, s_kern, r_kern)
    red_low.y_end()
    red_low.z_start()
    red_high.y_end()
    emit(0, 8)
    red_high.direct_end(g_kern, r_kern)
    red_high.z_start()
    red_low.z_end()
    red_low.x_start()
    emit(8, 8)
    red_high.z_end()
    red_high.x_start()
    o_low[...] = red_low.x_end()
    o_high[...] = red_high.x_end()

    @pl.when(me < last)
    def _():
        for c in down:
            c.wait_send()

    @pl.when(me > 0)
    def _():
        for c in up:
            c.wait_send()


def step_call(x, w1, w2, sl, sh, kl, kh, p_low, p_high):
    v = pltpu.VMEM
    dma = pltpu.SemaphoreType.DMA

    def reduction_buffers(lanes, later):
        return [
            v((128, lanes), BF16),
            v((128, lanes), BF16),
            v((128, lanes), F32),
            v((128, lanes), BF16),
            v((3, 32, lanes), BF16),
            v((32, later), BF16),
            v((8, 16, later), BF16),
            v((16, later), BF16),
            v((4, 16, later), BF16),
        ]

    return pl.pallas_call(
        step_kernel,
        out_shape=(
            jax.ShapeDtypeStruct((2048, 256), BF16),
            jax.ShapeDtypeStruct((16, 384), F32),
            jax.ShapeDtypeStruct((16, 256), F32),
        ),
        in_specs=[HBM] * 9,
        out_specs=(VM, VM, VM),
        scratch_shapes=[
            v((10, 32, 1024), BF16),
            v((3, 1536, 768), BF16),
            v((3, 3, 3, 256, 256), BF16),
            v((4, 768, 1024), BF16),
            v((64, 128), F32),
            v((2, 3, 256, 256), F32),
            v((2, 256, 256), BF16),
            v((2, 2, 32, 256), BF16),
            v((3, 10, 32, 512), BF16),
            v((3, 3, 3, 256), F32),
            v((3, 3, 3, 128), F32),
            v((256, 256), BF16),
            v((128, 256), BF16),
            v((256, 256), BF16),
            v((256, 128), BF16),
            v((2, 10, 32, 256), BF16),
            v((2, 18, 64, 128), BF16),
            v((2, 10, 32, 256), F32),
            v((2, 2, 18, 32, 128), F32),
            v((512, 256), BF16),
            v((2048, 128), BF16),
            v((512, 256), BF16),
            v((2048, 256), BF16),
            v((512, 256), F32),
            v((2048, 128), F32),
            v((27, 8, 256), F32),
            v((27, 8, 128), F32),
            v((2, 2048, 128), F32),
            v((256, 384), F32),
            v((256, 128), F32),
            v((128, 128), F32),
            v((128, 128), BF16),
            v((7, 16, 128), BF16),
            *reduction_buffers(384, 384),
            *reduction_buffers(128, 256),
            dma((18,)),
            dma((2, 5)),
            dma((2, 5)),
            dma((14,)),
            dma((14,)),
            dma((21,)),
            dma((21,)),
        ],
        compiler_params=pltpu.CompilerParams(
            collective_id=0, has_side_effects=True, vmem_limit_bytes=STEP_VMEM
        ),
        name="step",
    )(*(pltpu.with_memory_space_constraint(v, pltpu.HBM) for v in (x, w1, w2, sl, sh, kl, kh, p_low, p_high)))


def unpack_kernel(mism_s, low, high, mism, o_al, o_kl, o_ah, o_kh, s_al, s_kl, s_ah, s_kh, sem):
    cs = [
        pltpu.make_async_copy(
            mism_s.reshape(2, 16, 64, 256).at[f, q * 4 : q * 4 + 4],
            mism.at[0, f, q * 4 : q * 4 + 4],
            sem.at[f * 4 + q],
        )
        for f in range(2)
        for q in range(4)
    ]
    for c in cs:
        c.start()
    s_al[...] = low[:, 0:256]
    s_ah[...] = jnp.concatenate([high[0:8, 0:128], high[8:16, 0:128]], axis=1)
    low_k = jnp.concatenate([low[:, 256:384], jnp.zeros((112, 128), F32)], axis=0).T
    high_k = jnp.concatenate([high[0:8, 128:256], jnp.zeros((120, 128), F32)], axis=0).T
    for dt in range(3):
        for dh in range(3):
            n = (dt * 3 + dh) * 3
            s_kl[dt, dh] = low_k[n : n + 3, 0:16]
            s_kh[dt, dh] = high_k[n : n + 3, 0:8]
    for n, (a, b) in enumerate(((s_al, o_al), (s_kl, o_kl), (s_ah, o_ah), (s_kh, o_kh))):
        cs.append(pltpu.make_async_copy(a, b, sem.at[8 + n]))
        cs[-1].start()
    for c in cs:
        c.wait()


def on_device(*args):
    shapes = ((16, 256), (3, 3, 3, 16), (8, 256), (3, 3, 3, 8))
    mism, a_low, k_low, a_high, k_high = pl.pallas_call(
        unpack_kernel,
        out_shape=(
            jax.ShapeDtypeStruct((1, 2, 16, 64, 256), BF16),
            *(jax.ShapeDtypeStruct(n, F32) for n in shapes),
        ),
        in_specs=[VM] * 3,
        out_specs=(HBM,) * 5,
        scratch_shapes=[
            *(pltpu.VMEM(n, F32) for n in shapes),
            pltpu.SemaphoreType.DMA((12,)),
        ],
        compiler_params=pltpu.CompilerParams(vmem_limit_bytes=4 << 20),
        name="unpack",
    )(*step_call(*args))
    return a_low, k_low, a_high, k_high, mism


def solution(mesh):
    rows = P("clip", None, "space", None, None)
    in_specs = (rows, P(), P(), rows, rows, P(), P(), P(), P())
    out_specs = (
        P("clip", None),
        P(None, None, None, "clip"),
        P("clip", None),
        P(None, None, None, "clip"),
        rows,
    )
    return jax.shard_map(
        on_device, mesh=mesh, in_specs=in_specs, out_specs=out_specs, check_vma=False
    )
```

```python
import functools

import jax
import jax.numpy as jnp
from jax import lax
from jax.experimental import pallas as pl
from jax.experimental.pallas import tpu as pltpu
from jax.sharding import PartitionSpec as P

F32 = jnp.float32
BF16 = jnp.bfloat16
MESH = pl.DeviceIdType.MESH
ANY = pl.BlockSpec(memory_space=pl.ANY)
HBM = pl.BlockSpec(memory_space=pltpu.HBM)
VM = pl.BlockSpec(memory_space=pltpu.VMEM)
STEP_VMEM = 40 * 1024 * 1024


def dot(a, b):
    return jnp.dot(a, b, preferred_element_type=F32)


def row_ids(v, width):
    ids = lax.broadcasted_iota(jnp.int32, v.shape, 0)
    return ids if v.shape[0] == width else lax.rem(ids, width)


def from_left(v, width):
    return jnp.where(row_ids(v, width) == 0, 0.0, pltpu.roll(v, 1, 0))


def from_right(v, width):
    return jnp.where(row_ids(v, width) == width - 1, 0.0, pltpu.roll(v, v.shape[0] - 1, 0))


def build_taps(w2, v):
    def body(step, _):
        dt, chunk = step // 16, step % 16
        rows = pl.ds(pl.multiple_of(chunk * 16, 16), 16)
        out_rows = pl.ds(pl.multiple_of(dt * 256 + chunk * 16, 16), 16)
        tap = [[w2[dt, dh, dw, rows, :].astype(F32) for dw in range(3)] for dh in range(3)]
        for m in range(4):
            r = []
            for dw in range(3):
                a, b, c = tap[0][dw], tap[1][dw], tap[2][dw]
                r.append((a, b + c, a + b, c)[m])
            for j, col in enumerate((r[0], r[1] + r[2], r[0] + r[1], r[2])):
                v[m, out_rows, j * 256 : (j + 1) * 256] = (-col).astype(BF16)
        return 0

    lax.fori_loop(0, 48, body, 0)


def widen(src, dst, first, count):
    for f in range(2):

        def body(r, _):
            dst[f, first + r] = src[f, first + r].astype(F32)
            return 0

        lax.fori_loop(0, count, body, 0)


def depthwise(u, k, s, first, count):
    rows, width = u.shape[1] - 2, u.shape[2]
    for f in range(2):

        def body(step, _):
            r = first + step
            parts = [None, None, None]
            for g in range(2):
                for dh in range(3):
                    val = u[g, r + dh]
                    for dw in range(3):
                        term = val * k[g - f + 1, dh, dw : dw + 1, :]
                        parts[dw] = term if parts[dw] is None else parts[dw] + term
            total = u[f, r + 1] + (
                from_left(parts[0], width) + parts[1] + from_right(parts[2], width)
            )
            at = pl.multiple_of((f * rows + r) * width, width)
            s[pl.ds(at, width), :] = total.astype(BF16)
            return 0

        lax.fori_loop(0, count, body, 0)


def widen_fine(src, tmp, dst, first, count):
    for f in range(2):

        def body(step, _):
            r = first + step
            tmp[...] = src[f, r].astype(F32)
            for pc in range(2):
                dst[pc, f, r] = tmp[pl.ds(pc, 32, stride=2), :]
            return 0

        lax.fori_loop(0, count, body, 0)


def fine_rows(f, r, pc):
    if isinstance(r, int):
        return pl.ds((f * 4 + r % 2 * 2 + pc) * 256 + r // 2 * 32, 32)
    return pl.ds(pl.multiple_of((f * 4 + lax.rem(r, 2) * 2 + pc) * 256 + r // 2 * 32, 32), 32)


def depthwise_fine(u, k, s, first, count):
    for f in range(2):

        def body(step, _):
            r = first + step
            left = even = odd = right = 0.0
            for g in range(2):
                for dh in range(3):
                    e, o = u[0, g, r + dh], u[1, g, r + dh]
                    k0, k1, k2 = (k[g - f + 1, dh, dw : dw + 1, :] for dw in range(3))
                    left += o * k0
                    even += e * k1 + o * k2
                    odd += e * k0 + o * k1
                    right += e * k2
            s[fine_rows(f, r, 0), :] = (u[0, f, r + 1] + (from_left(left, 32) + even)).astype(BF16)
            s[fine_rows(f, r, 1), :] = (u[1, f, r + 1] + (odd + from_right(right, 32))).astype(BF16)
            return 0

        lax.fori_loop(0, count, body, 0)


def kernel_term_row_fine(u, back, kg, f, r):
    be, bo = back[fine_rows(f, r, 0), :], back[fine_rows(f, r, 1), :]
    be_right, bo_left = from_right(be, 32), from_left(bo, 32)
    for g in range(2):
        for dh in range(3):
            e, o = u[0, g, r + dh], u[1, g, r + dh]
            terms = (be_right * o + bo * e, be * e + bo * o, be * o + bo_left * e)
            for dw in range(3):
                tap = (g - f + 1) * 9 + dh * 3 + dw
                kg[tap] += jnp.sum(terms[dw].reshape(4, 8, 128), axis=0)


def kernel_terms_fine(u, back, kg, f, first, count):
    def body(step, _):
        kernel_term_row_fine(u, back, kg, f, first + step)
        return 0

    lax.fori_loop(0, count, body, 0)


def kernel_terms(u, back, kg):
    rows, width, ch = u.shape[1] - 2, u.shape[2], u.shape[3]
    kg[...] = jnp.zeros_like(kg)
    for f in range(2):

        def body(r, _):
            at = pl.multiple_of((f * rows + r) * width, width)
            b = back[pl.ds(at, width), :]
            shifted = (from_right(b, width), b, from_left(b, width))
            for g in range(2):
                for dh in range(3):
                    val = u[g, r + dh]
                    for dw in range(3):
                        tap = (g - f + 1) * 9 + dh * 3 + dw
                        prod = (shifted[dw] * val).reshape(width // 8, 8, ch)
                        kg[tap] += jnp.sum(prod, axis=0)
            return 0

        lax.fori_loop(0, rows, body, 0)


def kernel_rows(kg):
    ch = kg.shape[2]
    summed = jnp.sum(kg[...], axis=1)
    padded = jnp.concatenate([summed, jnp.zeros((128 - 27, ch), F32)], axis=0)
    return padded.T


class Where:
    def __init__(self):
        clip, space = lax.axis_index("clip"), lax.axis_index("space")
        self.space, self.last = space, lax.axis_size("space") - 1
        self.core = lax.rem(clip, 2)
        self.zh = lax.rem(clip // 2, 2)
        self.y = clip // 4
        self.zl = space // 4
        self.x = lax.rem(space, 4)
        self.z = self.zh * 4 + self.zl

    def dev(self, core=None, y=None, z=None, x=None):
        core = self.core if core is None else core
        y = self.y if y is None else y
        zh, zl = (self.zh, self.zl) if z is None else (z // 4, lax.rem(z, 4))
        x = self.x if x is None else x
        return ((y * 2 + zh) * 2 + core, zl * 4 + x)

    def partners(self):
        out = []
        for d in range(1, 8):
            to = lax.rem(self.core * 4 + self.y + d, 8)
            out.append(self.dev(core=to // 4, y=lax.rem(to, 4)))
        out += [self.dev(z=lax.rem(self.z + d, 8)) for d in range(1, 8)]
        out += [self.dev(x=lax.rem(self.x + d, 4)) for d in range(1, 4)]
        return out


class Reduction:
    def __init__(self, here, bufs, snd, rcv):
        self.here = here
        self.h2, self.r4, self.h4, self.r5 = bufs
        self.snd, self.rcv = snd, rcv

    def copy(self, src, dst, n, peer):
        return pltpu.make_async_remote_copy(
            src_ref=src, dst_ref=dst, send_sem=self.snd.at[n], recv_sem=self.rcv.at[n],
            device_id=peer, device_id_type=MESH,
        )

    def direct_start(self, g, sent, slots, base):
        t = self.here
        size = slots.shape[1]
        sent[...] = g[...].astype(BF16)
        cs = []
        for d in range(1, 8):
            to = lax.rem(t.core * 4 + t.y + d, 8)
            rows = pl.ds(pl.multiple_of(to * size, size), size)
            peer = t.dev(core=to // 4, y=lax.rem(to, 4))
            cs.append(self.copy(sent.at[rows, :], slots.at[d - 1], base + d, peer))
        for c in cs:
            c.start()
        return cs

    def direct_end(self, cs, g, slots):
        t = self.here
        size = slots.shape[1]
        for c in cs:
            c.wait()
        total = g[pl.ds(pl.multiple_of((t.core * 4 + t.y) * size, size), size), :]
        for d in range(7):
            total += slots[d].astype(F32)
        return total

    def share_start(self, source, slots, mine, size, base, peer):
        cs = []
        for d in range(1, size):
            to = lax.rem(mine + d, size)
            cs.append(self.copy(source(to), slots.at[mine], base + d, peer(to)))
        for c in cs:
            c.start()
        slots[mine] = source(mine)[...]
        self.shared = cs

    def share_end(self, source, slots, mine, size, base, peer):
        for c in self.shared:
            c.wait_send()
        for d in range(1, size):
            came = lax.rem(mine + size - d, size)
            self.copy(source(came), slots.at[came], base + d, peer(came)).wait_recv()
        vals = [slots[n].astype(F32) for n in range(size)]
        while len(vals) > 1:
            vals = [vals[n] + vals[n + 1] for n in range(0, len(vals), 2)]
        return vals[0]

    def z_args(self):
        t = self.here
        source = lambda z: self.h2.at[pl.ds(pl.multiple_of(z // 4 * 16, 16), 16), :]
        return source, self.r4, t.z, 8, 3, lambda z: t.dev(z=z)

    def x_args(self):
        t = self.here
        return lambda x: self.h4, self.r5, t.x, 4, 10, lambda x: t.dev(x=x)

    def z_start(self):
        self.share_start(*self.z_args())

    def z_end(self):
        self.h4[...] = self.share_end(*self.z_args()).astype(BF16)

    def x_start(self):
        self.share_start(*self.x_args())

    def x_end(self):
        return self.share_end(*self.x_args())


def step_kernel(
    x, w1, w2, sl, sh, kl_in, kh_in, al_in, ah_in,
    mism_s, o_low, o_high,
    xs, w1s, w2s, vs, tmp, mid, tgt, fh, gate, kl, kh, p_low, p_high, pt_low, pt_high,
    ulb, uhb, ul, uh, s_low, s_high, r_low, r_high,
    b_low, b_high, kg_low, kg_high, fine, g_low, g_high,
    g_kern, s_lowg, r_lowg, s_highg, r_highg, s_kern, r_kern, *rest,
):
    bufs_low, bufs_high = rest[:4], rest[4:8]
    sem, halo_snd, halo_rcv, snd_low, rcv_low, snd_high, rcv_high = rest[8:]
    here = Where()
    me, last = here.space, here.last
    scale_low = 1.0 / (16 * 2 * 128 * 32)
    scale_high = scale_low / 4

    barrier = pltpu.get_barrier_semaphore()
    partners = here.partners()
    for p in partners:
        pl.semaphore_signal(barrier, inc=1, device_id=p, device_id_type=MESH)

    @pl.when(me > 0)
    def _():
        pl.semaphore_signal(barrier, inc=1, device_id={"space": me - 1}, device_id_type=MESH)

    @pl.when(me < last)
    def _():
        pl.semaphore_signal(barrier, inc=1, device_id={"space": me + 1}, device_id_type=MESH)

    loads = []

    def load(src, dst):
        c = pltpu.make_async_copy(src, dst, sem.at[len(loads)])
        loads.append(c)
        c.start()
        return c

    c_w2 = load(w2, w2s)
    inner = jnp.logical_and(me > 0, me < last)

    @pl.when(inner)
    def _():
        pl.semaphore_wait(barrier, len(partners) + 2)

    @pl.when(jnp.logical_not(inner))
    def _():
        pl.semaphore_wait(barrier, len(partners) + 1)

    def border(side):
        peer = me + 1 if side == 0 else me - 1
        row, low, high = (7, 0, 0) if side == 0 else (0, 9, 17)
        fine_row = 15 if side == 0 else 0
        pairs = [
            (x.at[0, f, row : row + 1], xs.at[low : low + 1, :, f * 512 : (f + 1) * 512])
            for f in range(2)
        ]
        pairs.append((sh.at[0, :, fine_row : fine_row + 1], uhb.at[:, high : high + 1]))
        pairs.append((sl.at[0, :, row : row + 1], ulb.at[:, low : low + 1]))
        pairs.append((tgt.at[:, row * 32 : (row + 1) * 32], fh.at[side]))
        return [
            pltpu.make_async_remote_copy(
                src_ref=a, dst_ref=b, send_sem=halo_snd.at[side, n], recv_sem=halo_rcv.at[side, n],
                device_id={"space": peer}, device_id_type=MESH,
            )
            for n, (a, b) in enumerate(pairs)
        ]

    down, up = border(0), border(1)

    @pl.when(me < last)
    def _():
        for c in down[:4]:
            c.start()

    @pl.when(me > 0)
    def _():
        for c in up[:4]:
            c.start()

    c_sl = load(sl.at[0], ulb.at[:, 1:9])
    c_sh = load(sh.at[0], uhb.at[:, 1:17])
    c_k = [load(kl_in, kl), load(kh_in, kh), load(al_in, p_low), load(ah_in, p_high)]
    c_x = [load(x.at[0, f], xs.at[1:9, :, f * 512 : (f + 1) * 512]) for f in range(2)]
    c_w1 = [
        load(w1.at[dt, :, dw], w1s.at[:, dt * 512 : (dt + 1) * 512, dw * 256 : (dw + 1) * 256])
        for dt in range(3)
        for dw in range(3)
    ]

    c_w2.wait()
    build_taps(w2s, vs)

    c_sl.wait()
    c_sh.wait()
    for c in c_k:
        c.wait()
    pt_low[...] = p_low[...].astype(F32).T.astype(BF16)
    pt_high[...] = p_high[...].astype(F32).T.astype(BF16)
    widen(ulb, ul, 1, 8)
    widen_fine(uhb, tmp, uh, 1, 16)
    depthwise(ul, kl, s_low, 1, 6)
    depthwise_fine(uh, kh, s_high, 1, 14)

    for c in c_x + c_w1:
        c.wait()

    def conv_part(f, j, dh):
        return dot(
            xs[dh : dh + 8].reshape(256, 1024),
            w1s[dh, (1 - f) * 512 : (1 - f) * 512 + 1024, j * 256 : (j + 1) * 256],
        )

    for f in range(2):
        for j in range(3):
            mid[f, j] = conv_part(f, j, 1)

    @pl.when(me > 0)
    def _():
        for c in down[:2]:
            c.wait_recv()

    @pl.when(me == 0)
    def _():
        xs[0] = jnp.zeros((32, 1024), BF16)

    @pl.when(me < last)
    def _():
        for c in up[:2]:
            c.wait_recv()

    @pl.when(me == last)
    def _():
        xs[9] = jnp.zeros((32, 1024), BF16)

    for f in range(2):
        col = [mid[f, j] + conv_part(f, j, 0) + conv_part(f, j, 2) for j in range(3)]
        tgt[f] = (from_left(col[0], 32) + col[1] + from_right(col[2], 32)).astype(BF16)

    @pl.when(me < last)
    def _():
        down[4].start()

    @pl.when(me > 0)
    def _():
        up[4].start()

    def gate_rows(v, lo, hi, f):
        wide = v.astype(F32)
        val = wide / (1.0 + jnp.exp(-wide))
        for n, moved in enumerate((from_left(val, 32), val, from_right(val, 32))):
            gate[n, lo:hi, :, f * 256 : (f + 1) * 256] = moved.astype(BF16).reshape(
                hi - lo, 32, 256
            )

    for f in range(2):
        gate_rows(tgt[f], 1, 9, f)

    @pl.when(me > 0)
    def _():
        for c in down[2:4]:
            c.wait_recv()

    @pl.when(me == 0)
    def _():
        for f in range(2):
            ulb[f, 0] = jnp.zeros((32, 256), BF16)
            uhb[f, 0] = jnp.zeros((64, 128), BF16)

    @pl.when(me < last)
    def _():
        for c in up[2:4]:
            c.wait_recv()

    @pl.when(me == last)
    def _():
        for f in range(2):
            ulb[f, 9] = jnp.zeros((32, 256), BF16)
            uhb[f, 17] = jnp.zeros((64, 128), BF16)

    for first in (0, 9):
        widen(ulb, ul, first, 1)
    for first in (0, 17):
        widen_fine(uhb, tmp, uh, first, 1)
    for first in (0, 7):
        depthwise(ul, kl, s_low, first, 1)
    for first in (0, 15):
        depthwise_fine(uh, kh, s_high, first, 1)

    for f in range(2):
        rows = slice(f * 256, (f + 1) * 256)
        res = dot(s_low[rows, :], p_low[...]) - tgt[f].astype(F32)
        resid = (res * scale_low).astype(BF16)
        r_low[rows, :] = resid
    b_low[...] = dot(r_low[...], pt_low[...])
    a_low = lax.dot_general(
        s_low[...], r_low[...], (((0,), (0,)), ((), ())), preferred_element_type=F32
    )
    kernel_terms(ul, b_low, kg_low)
    k_low = kernel_rows(kg_low)
    for b in range(16):
        i = (b % 8) * 2 + b // 8
        g_low[b * 16 : (b + 1) * 16, 0:256] = a_low[i * 16 : (i + 1) * 16]
        g_low[b * 16 : (b + 1) * 16, 256:384] = k_low[i * 16 : (i + 1) * 16]
    red_low = Reduction(here, bufs_low, snd_low, rcv_low)
    low_direct = red_low.direct_start(g_low, s_lowg, r_lowg, 13)
    kg_high[...] = jnp.zeros_like(kg_high)
    bufs_high[0][...] = jnp.zeros((32, 256), BF16)

    @pl.when(me > 0)
    def _():
        down[4].wait_recv()
        for f in range(2):
            gate_rows(fh[0, f], 0, 1, f)

    @pl.when(me == 0)
    def _():
        for n in range(3):
            gate[n, 0] = jnp.zeros((32, 512), BF16)

    @pl.when(me < last)
    def _():
        up[4].wait_recv()
        for f in range(2):
            gate_rows(fh[1, f], 9, 10, f)

    @pl.when(me == last)
    def _():
        for n in range(3):
            gate[n, 9] = jnp.zeros((32, 512), BF16)

    for f in range(2):
        for pr in range(2):
            for pc in range(2):
                at = (f * 4 + pr * 2 + pc) * 256
                rows = slice(at, at + 256)
                res = dot(s_high[rows, :], p_high[...])
                for a in range(2):
                    for b in range(2):
                        j = pc * 2 + b
                        res += dot(
                            gate[pc + b, pr + a : pr + a + 8].reshape(256, 512),
                            vs[
                                pr * 2 + a,
                                (1 - f) * 256 : (1 - f) * 256 + 512,
                                j * 256 : (j + 1) * 256,
                            ],
                        )
                resid = (res * scale_high).astype(BF16)
                r_high[rows, :] = resid
                if f == 1:
                    for n in range(4):
                        kernel_term_row_fine(uh, b_high, kg_high, 0, (pr * 2 + pc) * 4 + n)
                for r in range(8):
                    to = (f * 16 + 2 * r + pr) * 64 + pc
                    for half in range(2):
                        fine[half, pl.ds(to, 32, stride=2), :] = res[
                            r * 32 : (r + 1) * 32, half * 128 : (half + 1) * 128
                        ]
        half = slice(f * 1024, (f + 1) * 1024)
        b_high[half, :] = dot(r_high[half, :], pt_high[...])
    def emit(first, count):
        def body(q, _):
            rows = pl.ds(pl.multiple_of(q * 128, 128), 128)
            mism_s[rows, :] = jnp.concatenate(
                [fine[0, rows, :], fine[1, rows, :]], axis=1
            ).astype(BF16)
            return 0

        lax.fori_loop(first, first + count, body, 0)

    a_high = lax.dot_general(
        s_high[...], r_high[...], (((0,), (0,)), ((), ())), preferred_element_type=F32
    )
    for b in range(16):
        i = (b % 8) * 2 + b // 8
        g_high[b * 16 : b * 16 + 8, :] = a_high[i * 8 : (i + 1) * 8, 0:128]
        g_high[b * 16 + 8 : b * 16 + 16, :] = a_high[i * 8 : (i + 1) * 8, 128:256]
    red_high = Reduction(here, bufs_high, snd_high, rcv_high)
    high_direct = red_high.direct_start(g_high, s_highg, r_highg, 13)
    kernel_terms_fine(uh, b_high, kg_high, 1, 0, 16)
    k_high = kernel_rows(kg_high)
    for b in range(16):
        i = (b % 8) * 2 + b // 8
        g_kern[b * 8 : (b + 1) * 8, :] = k_high[i * 8 : (i + 1) * 8]
    kern_direct = red_high.direct_start(g_kern, s_kern, r_kern, 20)
    red_low.h2[...] = red_low.direct_end(low_direct, g_low, r_lowg).astype(BF16)
    red_low.z_start()
    emit(0, 8)
    red_high.h2[:, 0:128] = red_high.direct_end(high_direct, g_high, r_highg).astype(BF16)
    total = red_high.direct_end(kern_direct, g_kern, r_kern).astype(BF16)
    red_high.h2[0:8, 128:256] = total[0:8]
    red_high.h2[16:24, 128:256] = total[8:16]
    red_high.z_start()
    red_low.z_end()
    red_low.x_start()
    emit(8, 8)
    red_high.z_end()
    red_high.x_start()
    o_low[...] = red_low.x_end()
    o_high[...] = red_high.x_end()

    @pl.when(me < last)
    def _():
        for c in down:
            c.wait_send()

    @pl.when(me > 0)
    def _():
        for c in up:
            c.wait_send()


def step_call(x, w1, w2, sl, sh, kl, kh, p_low, p_high):
    v = pltpu.VMEM
    dma = pltpu.SemaphoreType.DMA

    def reduction_buffers(lanes):
        return [
            v((32, lanes), BF16),
            v((8, 16, lanes), BF16),
            v((16, lanes), BF16),
            v((4, 16, lanes), BF16),
        ]

    return pl.pallas_call(
        step_kernel,
        out_shape=(
            jax.ShapeDtypeStruct((2048, 256), BF16),
            jax.ShapeDtypeStruct((16, 384), F32),
            jax.ShapeDtypeStruct((16, 256), F32),
        ),
        in_specs=[HBM] * 9,
        out_specs=(VM, VM, VM),
        scratch_shapes=[
            v((10, 32, 1024), BF16),
            v((3, 1536, 768), BF16),
            v((3, 3, 3, 256, 256), BF16),
            v((4, 768, 1024), BF16),
            v((64, 128), F32),
            v((2, 3, 256, 256), F32),
            v((2, 256, 256), BF16),
            v((2, 2, 32, 256), BF16),
            v((3, 10, 32, 512), BF16),
            v((3, 3, 3, 256), F32),
            v((3, 3, 3, 128), F32),
            v((256, 256), BF16),
            v((128, 256), BF16),
            v((256, 256), BF16),
            v((256, 128), BF16),
            v((2, 10, 32, 256), BF16),
            v((2, 18, 64, 128), BF16),
            v((2, 10, 32, 256), F32),
            v((2, 2, 18, 32, 128), F32),
            v((512, 256), BF16),
            v((2048, 128), BF16),
            v((512, 256), BF16),
            v((2048, 256), BF16),
            v((512, 256), F32),
            v((2048, 128), F32),
            v((27, 8, 256), F32),
            v((27, 8, 128), F32),
            v((2, 2048, 128), F32),
            v((256, 384), F32),
            v((256, 128), F32),
            v((128, 128), F32),
            v((256, 384), BF16),
            v((7, 32, 384), BF16),
            v((256, 128), BF16),
            v((7, 32, 128), BF16),
            v((128, 128), BF16),
            v((7, 16, 128), BF16),
            *reduction_buffers(384),
            *reduction_buffers(256),
            dma((18,)),
            dma((2, 5)),
            dma((2, 5)),
            dma((21,)),
            dma((21,)),
            dma((28,)),
            dma((28,)),
        ],
        compiler_params=pltpu.CompilerParams(
            collective_id=0, has_side_effects=True, vmem_limit_bytes=STEP_VMEM
        ),
        name="step",
    )(*(pltpu.with_memory_space_constraint(v, pltpu.HBM) for v in (x, w1, w2, sl, sh, kl, kh, p_low, p_high)))


def unpack_kernel(mism_s, low, high, mism, o_al, o_kl, o_ah, o_kh, s_al, s_kl, s_ah, s_kh, sem):
    cs = [
        pltpu.make_async_copy(
            mism_s.reshape(2, 16, 64, 256).at[f, q * 4 : q * 4 + 4],
            mism.at[0, f, q * 4 : q * 4 + 4],
            sem.at[f * 4 + q],
        )
        for f in range(2)
        for q in range(4)
    ]
    for c in cs:
        c.start()
    s_al[...] = low[:, 0:256]
    s_ah[...] = jnp.concatenate([high[0:8, 0:128], high[8:16, 0:128]], axis=1)
    low_k = jnp.concatenate([low[:, 256:384], jnp.zeros((112, 128), F32)], axis=0).T
    high_k = jnp.concatenate([high[0:8, 128:256], jnp.zeros((120, 128), F32)], axis=0).T
    for dt in range(3):
        for dh in range(3):
            n = (dt * 3 + dh) * 3
            s_kl[dt, dh] = low_k[n : n + 3, 0:16]
            s_kh[dt, dh] = high_k[n : n + 3, 0:8]
    for n, (a, b) in enumerate(((s_al, o_al), (s_kl, o_kl), (s_ah, o_ah), (s_kh, o_kh))):
        cs.append(pltpu.make_async_copy(a, b, sem.at[8 + n]))
        cs[-1].start()
    for c in cs:
        c.wait()


def on_device(*args):
    shapes = ((16, 256), (3, 3, 3, 16), (8, 256), (3, 3, 3, 8))
    mism, a_low, k_low, a_high, k_high = pl.pallas_call(
        unpack_kernel,
        out_shape=(
            jax.ShapeDtypeStruct((1, 2, 16, 64, 256), BF16),
            *(jax.ShapeDtypeStruct(n, F32) for n in shapes),
        ),
        in_specs=[VM] * 3,
        out_specs=(HBM,) * 5,
        scratch_shapes=[
            *(pltpu.VMEM(n, F32) for n in shapes),
            pltpu.SemaphoreType.DMA((12,)),
        ],
        compiler_params=pltpu.CompilerParams(vmem_limit_bytes=4 << 20),
        name="unpack",
    )(*step_call(*args))
    return a_low, k_low, a_high, k_high, mism


def solution(mesh):
    rows = P("clip", None, "space", None, None)
    in_specs = (rows, P(), P(), rows, rows, P(), P(), P(), P())
    out_specs = (
        P("clip", None),
        P(None, None, None, "clip"),
        P("clip", None),
        P(None, None, None, "clip"),
        rows,
    )
    return jax.shard_map(
        on_device, mesh=mesh, in_specs=in_specs, out_specs=out_specs, check_vma=False
    )
```
